256 devices in a mesh: seq: 16 (over y, x), exp: 16 (over z, core).
Axes of the slice: x: 4, y: 4, z: 8, core: 2. Of those that a mesh axis runs over, the one named last changes fastest.
Arguments:
- x_in: bfloat16 [4096, 8192], P('seq', 'exp'), may hold values from -6 to 6
- z_gate: bfloat16 [4096, 8192], P('seq', 'exp'), may hold values from -6 to 6
- b_in: bfloat16 [4096, 128], P('seq'), may hold values from -0.52734375 to 0.52734375
- c_out: bfloat16 [4096, 128], P('seq'), may hold values from -0.1875 to 0.1875
- dt_step: float32 [4096, 128], P('seq', 'exp'), may hold values from 0.12 to 2052, as said below
- rate: float32 [128], P('exp'), may hold values from 0 to 0.06, as said below
- skip: float32 [128], P('exp'), may hold values from 0.5 to 1.5
- init_state: float32 [128, 64, 128], P('exp'), may hold values from -16.970562 to 16.970562
- residual: bfloat16 [4096, 8192], P(('seq', 'exp')), may hold values from -6 to 6
- norm_gain: float32 [8192], replicated, may hold values from 0.5 to 1.5
- expert_ids: int32 [4096, 2], P(('seq', 'exp')), may hold values from 0 to 15, all different within a row; in each aligned block of 16 rows (0 to 15, 16 to 31, ...) at most 3 rows name the same one
- gate_weights: float32 [4096, 2], P(('seq', 'exp')), may hold values from 0.2 to 1
- w_gate: bfloat16 [16, 8192, 2048], P('exp', None, 'seq'), may hold values from -0.0625 to 0.0625
- w_up: bfloat16 [16, 8192, 2048], P('exp', None, 'seq'), may hold values from -0.0625 to 0.0625
- w_down: bfloat16 [16, 2048, 8192], P('exp', 'seq'), may hold values from -0.125 to 0.125
Outputs:
- layer_out: bfloat16 [4096, 8192], P(('seq', 'exp'))
The draws below stay inside these ranges and needn't reach their ends.
Inputs may be any that keep to these rules, and one draw needn't show every extreme that they name: `dt_step`: positive step sizes. `rate`: positive rates. `expert_ids`: each row names two different experts; among the rows of one device (aligned blocks of 16 rows) no expert is named by more than 3 rows, and in every draw some expert is named by exactly 3 rows of some block.
All inputs are finite; a program needn't handle non-finite values.
Results may differ from the reference program's by a relative error of at most 0.0095.
Values may be sent and summed in bfloat16 or wider, within the bound.
A program may use at most 128 MiB of HBM per device.

```python
import math
import jax
import jax.numpy as jnp
import numpy as np
from jax import lax

D = 8192
HEADS = 128
HEAD_DIM = 64
STATE = 128
FF = 2048
GROUP = 128
TOK_SEQ = 256
TOK_DEV = 16
TOKENS = 4096
EXPERTS = 16
CAP = 3
N_SEQ = 16


def draw_dt_step(key, part):
    first, second, third = jax.random.split(key, 3)
    shards = TOKENS // TOK_SEQ
    base = jnp.exp(jax.random.uniform(first, (TOKENS, HEADS), jnp.float32, math.log(0.5), math.log(1.5)))
    level = jnp.exp(jax.random.uniform(second, (shards, 1, HEADS), jnp.float32, -0.7, 0.7))
    base = (base.reshape(shards, TOK_SEQ, HEADS) * level).reshape(TOKENS, HEADS)
    spots = jax.random.randint(third, (3,), 0, TOKENS)
    struck = jnp.any(jnp.arange(TOKENS)[:, None] == spots[None, :], axis=1)
    return base + jnp.where(struck, 0.5 * TOKENS, 0.0).astype(jnp.float32)[:, None]


def draw_rate(key, part):
    first, second, third = jax.random.split(key, 3)
    slowest = 0.5 / TOKENS
    pick = jax.random.uniform(first, (HEADS,), jnp.float32)
    slow_rate = slowest * jnp.exp(jax.random.uniform(second, (HEADS,), jnp.float32, 0.0, math.log(1.5)))
    fast_rate = jnp.exp(jax.random.uniform(third, (HEADS,), jnp.float32, math.log(1.0 / 60.0), math.log(1.0 / 20.0)))
    share = 0.5
    return jnp.where(pick < share, slow_rate, fast_rate)


def block_scale(key, extent, pieces, smallest, high):
    factor_of, own = 1.0, jax.random.fold_in(key, 6)
    for dim, shards_of in pieces:
        draws = jnp.exp(jax.random.uniform(jax.random.fold_in(own, dim), (shards_of,), jnp.float32, smallest / len(pieces), high / len(pieces)))
        factor_of = factor_of * jnp.repeat(draws, extent[dim] // shards_of).reshape([-1 if axis == dim else 1 for axis in range(len(extent))])
    return factor_of


def deal_out(stream_key, own, number, rows, amount, top, most, lean):
    sequence = jax.random.permutation(stream_key, amount)
    packed, usual = portions_of(amount, rows * top, most, lean, True), portions_of(amount, rows * top, most, lean, False)
    places = jnp.arange(amount)

    def named(tallies, rotation):
        used = int((tallies > 0).sum())
        fixed = max(1, used // 4)
        moved = fixed + (places - fixed + rotation * (used - fixed)) % max(1, amount - fixed)
        return jnp.zeros((amount,), jnp.int32).at[sequence[jnp.where(places < fixed, places, moved)]].set(jnp.asarray(tallies, jnp.int32))

    tallies = jnp.where(number % 4 == 0, named(packed, number // 4), named(usual, number - number // 4 - 1))
    mixed = jax.random.permutation(jax.random.fold_in(own, 3), amount)
    source_of, taker = mixed[0:amount // 2 * 2:2], mixed[1:amount // 2 * 2:2]
    slack = jnp.minimum(tallies[source_of] - 1, most - tallies[taker]) // 2
    slack = jnp.where((source_of == sequence[0]) | (taker == sequence[0]) | (tallies[taker] == 0), 0, jnp.maximum(slack, 0))
    moved = jax.random.randint(jax.random.fold_in(own, 4), (amount // 2,), 0, 1 << 20) % (slack + 1)
    tallies = tallies.at[source_of].add(-moved).at[taker].add(moved)
    members = jnp.searchsorted(jnp.cumsum(tallies), jnp.arange(rows * top), side="right").astype(jnp.int32)
    listing = members.reshape(top, rows).T
    listing = listing[jax.random.permutation(jax.random.fold_in(own, 1), rows)]
    rotation = jax.random.randint(jax.random.fold_in(own, 2), (rows, 1), 0, top)
    return jnp.take_along_axis(listing, (jnp.arange(top)[None, :] + rotation) % top, axis=1)


def portions_of(number_of, total, bound, slope, full):
    loads = [(1 << 20) // math.isqrt(standing ** slope) + 1 for standing in range(1, number_of + 1)]
    largest = bound if full else min(bound, max(-(-total // number_of), total * loads[0] // sum(loads)))
    least = 1 if total - largest >= number_of - 1 else 0
    counts, surplus = [largest] + [least] * (number_of - 1), total - largest - least * (number_of - 1)
    while surplus > 0:
        candidates = [i for i in range(1, number_of) if counts[i] < largest] or [i for i in range(1, number_of) if counts[i] < bound]
        pool, remaining = sum([loads[i] for i in candidates]), surplus
        for i in candidates:
            addition = min(bound - counts[i], max(1, remaining * loads[i] // pool), surplus)
            counts[i] = counts[i] + addition
            surplus = surplus - addition
    return np.array(counts)


def normal_values(rng, extent, deviation, bound, pieces=(), held_as=jnp.bfloat16):
    result = jax.random.normal(rng, extent, jnp.float32) * deviation
    if len(pieces) > 0:
        result = block_scale(rng, extent, pieces, -0.22, 0.18) * result
    return jnp.clip(result, min=-bound, max=bound).astype(held_as)


def setup_inputs(seed: int = 0) -> dict:
    key_list = jax.random.split(jax.random.key(seed), 16)
    x_in = normal_values(key_list[0], (TOKENS, D), 1.0, 6.0, ((0, 16), (1, 16)))
    z_gate = normal_values(key_list[1], (TOKENS, D), 1.0, 6.0, ((0, 16), (1, 16)))
    b_in = normal_values(key_list[2], (TOKENS, STATE), (1.0 / STATE ** 0.5), 0.52734375, ((0, 16),))
    c_out = normal_values(key_list[3], (TOKENS, STATE), (2.0 / TOKENS ** 0.5), 0.1875, ((0, 16),))
    dt_step = draw_dt_step(jax.random.fold_in(key_list[15], 71), 0)
    rate = draw_rate(jax.random.fold_in(key_list[15], 71), 0)
    skip = jnp.clip(0.5 + 1.0 * jax.random.uniform(key_list[6], (HEADS,), jnp.float32) ** block_scale(key_list[6], (HEADS,), ((0, 16),), -0.2, 0.2), 0.5, 1.5)
    init_state = normal_values(key_list[7], (HEADS, HEAD_DIM, STATE), (0.5 * (TOKENS / STATE) ** 0.5), 16.970562, ((0, 16),), jnp.float32)
    residual = normal_values(key_list[8], (TOKENS, D), 1.0, 6.0, ((0, 256),))
    norm_gain = jnp.clip(1.0 + 0.1 * jax.random.normal(key_list[9], (D,), jnp.float32), 0.5, 1.5)
    expert_ids_keys = jax.random.split(jax.random.fold_in(key_list[10], 1), TOKENS // TOK_DEV)
    expert_ids_turns = jax.random.permutation(jax.random.fold_in(key_list[10], 3), TOKENS // TOK_DEV)
    expert_ids = jax.vmap(lambda own, number: deal_out(jax.random.fold_in(key_list[10], 2), own, number, TOK_DEV, EXPERTS, 2, CAP, 2))(expert_ids_keys, expert_ids_turns).reshape((TOKENS, 2))
    gate_weights = jnp.clip(0.2 + 0.8 * jax.random.uniform(key_list[11], (TOKENS, 2), jnp.float32) ** block_scale(key_list[11], (TOKENS, 2), ((0, 256),), -0.2, 0.2), 0.2, 1.0)
    w_gate = normal_values(key_list[12], (EXPERTS, D, FF), D ** -0.5, 0.0625, ((0, 16), (2, 16)))
    w_up = normal_values(key_list[13], (EXPERTS, D, FF), D ** -0.5, 0.0625, ((0, 16), (2, 16)))
    w_down = normal_values(key_list[14], (EXPERTS, FF, D), FF ** -0.5, 0.125, ((0, 16), (1, 16)))
    return dict(x_in=x_in, z_gate=z_gate, b_in=b_in, c_out=c_out, dt_step=dt_step, rate=rate, skip=skip, init_state=init_state, residual=residual, norm_gain=norm_gain, expert_ids=expert_ids, gate_weights=gate_weights, w_gate=w_gate, w_up=w_up, w_down=w_down)


PRECISE = lax.Precision.HIGHEST

def mixer_layer(x_in, z_gate, b_in, c_out, dt_step, rate, skip, init_state):
    blocks = TOKENS // GROUP
    inputs = x_in.astype(jnp.float32).reshape(blocks, GROUP, HEADS, HEAD_DIM)
    keys_in = b_in.astype(jnp.float32).reshape(blocks, GROUP, STATE)
    queries = c_out.astype(jnp.float32).reshape(blocks, GROUP, STATE)
    log_steps = (-rate[None, :] * dt_step).reshape(blocks, GROUP, HEADS)
    causal = jnp.arange(GROUP)[:, None] >= jnp.arange(GROUP)[None, :]

    def advance(state, element):
        block_in, block_keys, block_queries, block_logs = element
        cumulative = jnp.cumsum(block_logs, axis=0)
        scores = jnp.dot(block_queries, block_keys.T, precision=PRECISE)
        spread = cumulative[:, None, :] - cumulative[None, :, :]
        weights = jnp.exp(jnp.where(causal[:, :, None], spread, -jnp.inf)) * scores[:, :, None]
        intra_out = jnp.einsum('tsh,shp->thp', weights, block_in, precision=PRECISE)
        inter_out = jnp.exp(cumulative)[:, :, None] * jnp.einsum('hpn,tn->thp', state, block_queries, precision=PRECISE)
        output = intra_out + inter_out + skip[None, :, None] * block_in
        tail_decay = jnp.exp(cumulative[-1:, :] - cumulative)
        new_state = jnp.exp(cumulative[-1])[:, None, None] * state + jnp.einsum('sh,shp,sn->hpn', tail_decay, block_in, block_keys, precision=PRECISE)
        return (new_state, output)
    _, outputs = lax.scan(advance, init_state, (inputs, keys_in, queries, log_steps))
    mixed_out = outputs.reshape(TOKENS, HEADS * HEAD_DIM)
    return (mixed_out * jax.nn.silu(z_gate.astype(jnp.float32))).astype(jnp.bfloat16)

def reference(x_in, z_gate, b_in, c_out, dt_step, rate, skip, init_state, residual, norm_gain, expert_ids, gate_weights, w_gate, w_up, w_down):
    mixer = mixer_layer(x_in, z_gate, b_in, c_out, dt_step, rate, skip, init_state)
    stream = (residual.astype(jnp.float32) + mixer.astype(jnp.float32)).astype(jnp.bfloat16)
    widened = stream.astype(jnp.float32)
    normed = (widened * lax.rsqrt(lax.optimization_barrier(jnp.mean(widened * widened, axis=-1, keepdims=True)) + 1e-06) * norm_gain[None, :]).astype(jnp.bfloat16)
    blocks = TOKENS // TOK_DEV
    chosen = expert_ids.reshape(blocks, 2 * TOK_DEV).astype(jnp.int32)
    onehot = (chosen[:, :, None] == jnp.arange(EXPERTS, dtype=jnp.int32)[None, None, :]).astype(jnp.int32)
    slot_index = lax.optimization_barrier(jnp.sum((jnp.cumsum(onehot, axis=1) - onehot) * onehot, axis=2)).astype(jnp.int32)
    block_ids = jnp.arange(blocks, dtype=jnp.int32)[:, None]
    target = (chosen * (blocks * CAP) + block_ids * CAP + slot_index).reshape(-1).astype(jnp.int32)
    pair_rows = jnp.repeat(normed, 2, axis=0)
    buffers = jnp.zeros((EXPERTS * blocks * CAP, D), jnp.bfloat16).at[target].set(pair_rows)
    buffers = buffers.reshape(EXPERTS, blocks * CAP, D)
    width_part = FF // N_SEQ

    def run_expert(operands):
        rows_in, gate_matrix, up_matrix, down_matrix = operands
        running = jnp.zeros((rows_in.shape[0], D), jnp.float32)
        for portion in range(N_SEQ):
            first_unit = portion * width_part
            last_unit = first_unit + width_part
            gate_proj = jnp.dot(rows_in, gate_matrix[:, first_unit:last_unit], preferred_element_type=jnp.float32)
            up_proj = jnp.dot(rows_in, up_matrix[:, first_unit:last_unit], preferred_element_type=jnp.float32)
            active = (jax.nn.silu(gate_proj) * up_proj).astype(jnp.bfloat16)
            partial_value = jnp.dot(active, down_matrix[first_unit:last_unit, :], preferred_element_type=jnp.float32).astype(jnp.bfloat16)
            partial_value = lax.optimization_barrier(partial_value)
            running = running + partial_value.astype(jnp.float32)
        return running.astype(jnp.bfloat16)
    outputs = lax.map(run_expert, (buffers, w_gate, w_up, w_down))
    picked = outputs.reshape(-1, D)[target].astype(jnp.float32).reshape(TOKENS, 2, D)
    mixture = lax.optimization_barrier(jnp.sum(picked * gate_weights[:, :, None], axis=1))
    return (widened + mixture).astype(jnp.bfloat16)
```

```python
import jax
import jax.numpy as jnp
from jax import lax
from jax.sharding import PartitionSpec as P

GROUP = 128


PRECISE = lax.Precision.HIGHEST


def exclusive_scan(log, state, axis):
    devices = lax.axis_size(axis)
    inc = (log, state)
    exc = (jnp.zeros_like(log), jnp.zeros_like(state))
    shift = 1
    while shift < devices:
        pairs = [(i, i + shift) for i in range(devices - shift)]
        got = (lax.ppermute(inc[0], axis, pairs), lax.ppermute(inc[1], axis, pairs))
        exc = chain_combine(got, exc)
        inc = chain_combine(got, inc)
        shift *= 2
    return exc


def chain_combine(earlier, later):
    return (earlier[0] + later[0], jnp.exp(later[0])[:, None, None] * earlier[1] + later[1])


def on_device(
    x_in,
    z_gate,
    b_in,
    c_out,
    dt_step,
    rate,
    skip,
    init_state,
    residual,
    norm_gain,
    expert_ids,
    gate_weights,
    w_gate,
    w_up,
    w_down,
):
    token_count, channels = x_in.shape
    heads_here = rate.shape[0]
    head_width = channels // heads_here
    state_width = b_in.shape[1]
    blocks = token_count // GROUP
    inputs = x_in.astype(jnp.float32).reshape(blocks, GROUP, heads_here, head_width)
    keys_in = b_in.astype(jnp.float32).reshape(blocks, GROUP, state_width)
    queries = c_out.astype(jnp.float32).reshape(blocks, GROUP, state_width)
    log_steps = (-rate[None, :] * dt_step).reshape(blocks, GROUP, heads_here)
    cumulative = jnp.cumsum(log_steps, axis=1)
    scores = jnp.einsum("ctn,csn->cts", queries, keys_in, precision=PRECISE)
    causal = jnp.arange(GROUP)[:, None] >= jnp.arange(GROUP)[None, :]
    spread = cumulative[:, :, None, :] - cumulative[:, None, :, :]
    weights = jnp.exp(jnp.where(causal[None, :, :, None], spread, -jnp.inf)) * scores[..., None]
    intra_out = jnp.einsum("ctsh,cshp->cthp", weights, inputs, precision=PRECISE)
    tail_decay = jnp.exp(cumulative[:, -1:, :] - cumulative)
    block_state = jnp.einsum("csh,cshp,csn->chpn", tail_decay, inputs, keys_in, precision=PRECISE)
    block_log = cumulative[:, -1, :]

    def advance(carried, element):
        total_log, total_state = carried
        step_log, step_state = element
        updated = (
            total_log + step_log,
            jnp.exp(step_log)[:, None, None] * total_state + step_state,
        )
        return (updated, (total_log, total_state))

    zero_state = jnp.zeros((heads_here, head_width, state_width), jnp.float32)
    zero_log = jnp.zeros((heads_here,), jnp.float32)
    (device_log, device_state), (enter_log, enter_state) = lax.scan(
        advance, (zero_log, zero_state), (block_log, block_state)
    )
    prior_log, prior_state = exclusive_scan(device_log, device_state, "seq")
    incoming = prior_state + jnp.exp(prior_log)[:, None, None] * init_state
    entering = enter_state + jnp.exp(enter_log)[:, :, None, None] * incoming[None]
    inter_out = jnp.exp(cumulative)[..., None] * jnp.einsum(
        "chpn,ctn->cthp", entering, queries, precision=PRECISE
    )
    mixed_out = (intra_out + inter_out + skip[None, None, :, None] * inputs).reshape(
        token_count, channels
    )
    mixer = (mixed_out * jax.nn.silu(z_gate.astype(jnp.float32))).astype(jnp.bfloat16)
    token_mix = lax.all_to_all(mixer, "exp", split_axis=0, concat_axis=1, tiled=True)
    stream = (residual.astype(jnp.float32) + token_mix.astype(jnp.float32)).astype(jnp.bfloat16)
    widened = stream.astype(jnp.float32)
    normed = (
        widened
        * lax.rsqrt(jnp.mean(widened * widened, axis=-1, keepdims=True) + 1e-06)
        * norm_gain[None, :]
    ).astype(jnp.bfloat16)
    rows_here = residual.shape[0]
    owners = lax.axis_size("exp")
    local_experts = w_gate.shape[0]
    experts = owners * local_experts
    capacity = max(2, 2 * rows_here // experts + 1)
    width = residual.shape[1]
    chosen = expert_ids.reshape(-1)
    onehot = (chosen[:, None] == jnp.arange(experts)[None, :]).astype(jnp.int32)
    slot_index = jnp.sum((jnp.cumsum(onehot, axis=0) - onehot) * onehot, axis=1)
    target = slot_index * experts + chosen
    placing = (target[None, :] == jnp.arange(experts * capacity)[:, None]).astype(jnp.bfloat16)
    pair_rows = jnp.repeat(normed, 2, axis=0)
    outgoing = jnp.dot(placing, pair_rows, preferred_element_type=jnp.float32).astype(jnp.bfloat16)
    outgoing = outgoing.reshape(capacity, experts, width)
    arrived = lax.all_to_all(outgoing, "exp", split_axis=1, concat_axis=1, tiled=True)
    arrived = arrived.reshape(capacity * experts, width)
    segment = lax.all_gather(arrived, "seq", axis=0, tiled=True)
    gate_proj = jnp.dot(segment, w_gate[0], preferred_element_type=jnp.float32)
    up_proj = jnp.dot(segment, w_up[0], preferred_element_type=jnp.float32)
    active = (jax.nn.silu(gate_proj) * up_proj).astype(jnp.bfloat16)
    partial_value = jnp.dot(active, w_down[0], preferred_element_type=jnp.float32)
    summed = lax.psum_scatter(partial_value.astype(jnp.bfloat16), "seq", scatter_dimension=0, tiled=True)
    summed = summed.reshape(capacity, experts, width)
    returned = lax.all_to_all(summed, "exp", split_axis=1, concat_axis=1, tiled=True)
    results = returned.reshape(experts * capacity, width)
    picked = results[target].astype(jnp.float32).reshape(rows_here, 2, width)
    mixture = jnp.sum(picked * gate_weights[:, :, None], axis=1)
    return (widened + mixture).astype(jnp.bfloat16)


def solution(mesh):
    return jax.shard_map(
        on_device,
        mesh=mesh,
        in_specs=(
            P("seq", "exp"),
            P("seq", "exp"),
            P("seq", None),
            P("seq", None),
            P("seq", "exp"),
            P("exp"),
            P("exp"),
            P("exp", None, None),
            P(("seq", "exp"), None),
            P(),
            P(("seq", "exp"), None),
            P(("seq", "exp"), None),
            P("exp", None, "seq"),
            P("exp", None, "seq"),
            P("exp", "seq", None),
        ),
        out_specs=P(("seq", "exp"), None),
        check_vma=False,
    )
```

```python
import jax
import jax.numpy as jnp
from jax import lax
from jax.sharding import PartitionSpec as P

GROUP = 128


PRECISE = lax.Precision.HIGHEST


def exclusive_scan(log, state, axis):
    devices = lax.axis_size(axis)
    inc = (log, state)
    exc = (jnp.zeros_like(log), jnp.zeros_like(state))
    shift = 1
    while shift < devices:
        pairs = [(i, i + shift) for i in range(devices - shift)]
        got = (lax.ppermute(inc[0], axis, pairs), lax.ppermute(inc[1], axis, pairs))
        exc = chain_combine(got, exc)
        inc = chain_combine(got, inc)
        shift *= 2
    return exc


def chain_combine(earlier, later):
    return (earlier[0] + later[0], jnp.exp(later[0])[:, None, None] * earlier[1] + later[1])


def on_device(
    x_in,
    z_gate,
    b_in,
    c_out,
    dt_step,
    rate,
    skip,
    init_state,
    residual,
    norm_gain,
    expert_ids,
    gate_weights,
    w_gate,
    w_up,
    w_down,
):
    token_count, channels = x_in.shape
    heads_here = rate.shape[0]
    head_width = channels // heads_here
    state_width = b_in.shape[1]
    blocks = token_count // GROUP
    inputs = x_in.astype(jnp.float32).reshape(blocks, GROUP, heads_here, head_width)
    keys_in = b_in.astype(jnp.float32).reshape(blocks, GROUP, state_width)
    queries = c_out.astype(jnp.float32).reshape(blocks, GROUP, state_width)
    log_steps = (-rate[None, :] * dt_step).reshape(blocks, GROUP, heads_here)
    cumulative = jnp.cumsum(log_steps, axis=1)
    scores = jnp.einsum("ctn,csn->cts", queries, keys_in, precision=PRECISE)
    causal = jnp.arange(GROUP)[:, None] >= jnp.arange(GROUP)[None, :]
    spread = cumulative[:, :, None, :] - cumulative[:, None, :, :]
    weights = jnp.exp(jnp.where(causal[None, :, :, None], spread, -jnp.inf)) * scores[..., None]
    intra_out = jnp.einsum("ctsh,cshp->cthp", weights, inputs, precision=PRECISE)
    tail_decay = jnp.exp(cumulative[:, -1:, :] - cumulative)
    block_state = jnp.einsum("csh,cshp,csn->chpn", tail_decay, inputs, keys_in, precision=PRECISE)
    block_log = cumulative[:, -1, :]

    def advance(carried, element):
        total_log, total_state = carried
        step_log, step_state = element
        updated = (
            total_log + step_log,
            jnp.exp(step_log)[:, None, None] * total_state + step_state,
        )
        return (updated, (total_log, total_state))

    zero_state = jnp.zeros((heads_here, head_width, state_width), jnp.float32)
    zero_log = jnp.zeros((heads_here,), jnp.float32)
    (device_log, device_state), (enter_log, enter_state) = lax.scan(
        advance, (zero_log, zero_state), (block_log, block_state)
    )
    prior_log, prior_state = exclusive_scan(device_log, device_state, "seq")
    incoming = prior_state + jnp.exp(prior_log)[:, None, None] * init_state
    entering = enter_state + jnp.exp(enter_log)[:, :, None, None] * incoming[None]
    inter_out = jnp.exp(cumulative)[..., None] * jnp.einsum(
        "chpn,ctn->cthp", entering, queries, precision=PRECISE
    )
    mixed_out = (intra_out + inter_out + skip[None, None, :, None] * inputs).reshape(
        token_count, channels
    )
    mixer = (mixed_out * jax.nn.silu(z_gate.astype(jnp.float32))).astype(jnp.bfloat16)
    token_mix = lax.all_to_all(mixer, "exp", split_axis=0, concat_axis=1, tiled=True)
    stream = (residual.astype(jnp.float32) + token_mix.astype(jnp.float32)).astype(jnp.bfloat16)
    widened = stream.astype(jnp.float32)
    normed = (
        widened
        * lax.rsqrt(jnp.mean(widened * widened, axis=-1, keepdims=True) + 1e-06)
        * norm_gain[None, :]
    ).astype(jnp.bfloat16)
    rows_here = residual.shape[0]
    owners = lax.axis_size("exp")
    local_experts = w_gate.shape[0]
    experts = owners * local_experts
    capacity = max(2, 2 * rows_here // experts + 1)
    width = residual.shape[1]
    chosen = expert_ids.reshape(-1)
    onehot = (chosen[:, None] == jnp.arange(experts)[None, :]).astype(jnp.int32)
    slot_index = jnp.sum((jnp.cumsum(onehot, axis=0) - onehot) * onehot, axis=1)
    target = slot_index * experts + chosen
    placing = (target[None, :] == jnp.arange(experts * capacity)[:, None]).astype(jnp.bfloat16)
    pair_rows = jnp.repeat(normed, 2, axis=0)
    outgoing = jnp.dot(placing, pair_rows, preferred_element_type=jnp.float32).astype(jnp.bfloat16)
    outgoing = outgoing.reshape(capacity, experts, width)
    arrived = lax.all_to_all(outgoing, "exp", split_axis=1, concat_axis=1, tiled=True)
    pieces = []
    for first, last in ((0, 1), (1, capacity)):
        chunk = arrived[first:last].reshape((last - first) * experts, width)
        segment = lax.all_gather(chunk, "seq", axis=0, tiled=True)
        gate_proj = jnp.dot(segment, w_gate[0], preferred_element_type=jnp.float32)
        up_proj = jnp.dot(segment, w_up[0], preferred_element_type=jnp.float32)
        active = (jax.nn.silu(gate_proj) * up_proj).astype(jnp.bfloat16)
        partial_value = jnp.dot(active, w_down[0], preferred_element_type=jnp.float32)
        pieces.append(
            lax.psum_scatter(partial_value.astype(jnp.bfloat16), "seq", scatter_dimension=0, tiled=True)
        )
    summed = jnp.concatenate(pieces, axis=0).reshape(capacity, experts, width)
    returned = lax.all_to_all(summed, "exp", split_axis=1, concat_axis=1, tiled=True)
    results = returned.reshape(experts * capacity, width)
    picked = results[target].astype(jnp.float32).reshape(rows_here, 2, width)
    mixture = jnp.sum(picked * gate_weights[:, :, None], axis=1)
    return (widened + mixture).astype(jnp.bfloat16)


def solution(mesh):
    return jax.shard_map(
        on_device,
        mesh=mesh,
        in_specs=(
            P("seq", "exp"),
            P("seq", "exp"),
            P("seq", None),
            P("seq", None),
            P("seq", "exp"),
            P("exp"),
            P("exp"),
            P("exp", None, None),
            P(("seq", "exp"), None),
            P(),
            P(("seq", "exp"), None),
            P(("seq", "exp"), None),
            P("exp", None, "seq"),
            P("exp", None, "seq"),
            P("exp", "seq", None),
        ),
        out_specs=P(("seq", "exp"), None),
        check_vma=False,
    )
```

```python
import jax
import jax.numpy as jnp
from jax import lax
from jax.sharding import PartitionSpec as P
from jax.experimental import pallas as pl
from jax.experimental.pallas import tpu as pltpu

GROUP = 128


PRECISE = lax.Precision.HIGHEST


def exchange_body(x_ref, o_ref, send_sem, recv_sem, local_sem):
    devices = x_ref.shape[0]
    me = lax.axis_index("exp")
    row = lax.axis_index("seq")
    mesh_id = pl.DeviceIdType.MESH
    barrier = pltpu.get_barrier_semaphore()
    for step in range(1, devices):
        peer = lax.rem(me + step, devices)
        pl.semaphore_signal(barrier, 1, device_id=(row, peer), device_id_type=mesh_id)
    pl.semaphore_wait(barrier, devices - 1)
    local = pltpu.make_async_copy(x_ref.at[me], o_ref.at[me], local_sem)
    local.start()
    copies = []
    for step in range(1, devices):
        peer = lax.rem(me + step, devices)
        copy = pltpu.make_async_remote_copy(
            src_ref=x_ref.at[peer],
            dst_ref=o_ref.at[me],
            send_sem=send_sem.at[step],
            recv_sem=recv_sem.at[step],
            device_id=(row, peer),
            device_id_type=mesh_id,
        )
        copy.start()
        copies.append(copy)
    local.wait()
    for copy in copies:
        copy.wait()


def exchange(x, collective):
    devices = x.shape[0]
    return pl.pallas_call(
        exchange_body,
        out_shape=jax.ShapeDtypeStruct(x.shape, x.dtype),
        in_specs=[pl.BlockSpec(memory_space=pltpu.VMEM)],
        out_specs=pl.BlockSpec(memory_space=pltpu.VMEM),
        scratch_shapes=[
            pltpu.SemaphoreType.DMA((devices,)),
            pltpu.SemaphoreType.DMA((devices,)),
            pltpu.SemaphoreType.DMA,
        ],
        compiler_params=pltpu.CompilerParams(collective_id=collective, has_side_effects=True),
    )(x)


def exclusive_scan(log, state, axis):
    devices = lax.axis_size(axis)
    inc = (log, state)
    exc = (jnp.zeros_like(log), jnp.zeros_like(state))
    shift = 1
    while shift < devices:
        pairs = [(i, i + shift) for i in range(devices - shift)]
        got = (lax.ppermute(inc[0], axis, pairs), lax.ppermute(inc[1], axis, pairs))
        exc = chain_combine(got, exc)
        inc = chain_combine(got, inc)
        shift *= 2
    return exc


def chain_combine(earlier, later):
    return (earlier[0] + later[0], jnp.exp(later[0])[:, None, None] * earlier[1] + later[1])


def on_device(
    x_in,
    z_gate,
    b_in,
    c_out,
    dt_step,
    rate,
    skip,
    init_state,
    residual,
    norm_gain,
    expert_ids,
    gate_weights,
    w_gate,
    w_up,
    w_down,
):
    token_count, channels = x_in.shape
    heads_here = rate.shape[0]
    head_width = channels // heads_here
    state_width = b_in.shape[1]
    blocks = token_count // GROUP
    inputs = x_in.astype(jnp.float32).reshape(blocks, GROUP, heads_here, head_width)
    keys_in = b_in.astype(jnp.float32).reshape(blocks, GROUP, state_width)
    queries = c_out.astype(jnp.float32).reshape(blocks, GROUP, state_width)
    log_steps = (-rate[None, :] * dt_step).reshape(blocks, GROUP, heads_here)
    cumulative = jnp.cumsum(log_steps, axis=1)
    scores = jnp.einsum("ctn,csn->cts", queries, keys_in, precision=PRECISE)
    causal = jnp.arange(GROUP)[:, None] >= jnp.arange(GROUP)[None, :]
    spread = cumulative[:, :, None, :] - cumulative[:, None, :, :]
    weights = jnp.exp(jnp.where(causal[None, :, :, None], spread, -jnp.inf)) * scores[..., None]
    intra_out = jnp.einsum("ctsh,cshp->cthp", weights, inputs, precision=PRECISE)
    tail_decay = jnp.exp(cumulative[:, -1:, :] - cumulative)
    block_state = jnp.einsum("csh,cshp,csn->chpn", tail_decay, inputs, keys_in, precision=PRECISE)
    block_log = cumulative[:, -1, :]

    def advance(carried, element):
        total_log, total_state = carried
        step_log, step_state = element
        updated = (
            total_log + step_log,
            jnp.exp(step_log)[:, None, None] * total_state + step_state,
        )
        return (updated, (total_log, total_state))

    zero_state = jnp.zeros((heads_here, head_width, state_width), jnp.float32)
    zero_log = jnp.zeros((heads_here,), jnp.float32)
    (device_log, device_state), (enter_log, enter_state) = lax.scan(
        advance, (zero_log, zero_state), (block_log, block_state)
    )
    prior_log, prior_state = exclusive_scan(device_log, device_state, "seq")
    incoming = prior_state + jnp.exp(prior_log)[:, None, None] * init_state
    entering = enter_state + jnp.exp(enter_log)[:, :, None, None] * incoming[None]
    inter_out = jnp.exp(cumulative)[..., None] * jnp.einsum(
        "chpn,ctn->cthp", entering, queries, precision=PRECISE
    )
    mixed_out = (intra_out + inter_out + skip[None, None, :, None] * inputs).reshape(
        token_count, channels
    )
    mixer = (mixed_out * jax.nn.silu(z_gate.astype(jnp.float32))).astype(jnp.bfloat16)
    owners = lax.axis_size("exp")
    rows_here = residual.shape[0]
    arrived_mix = exchange(mixer.reshape(owners, rows_here, channels), 0)
    token_mix = arrived_mix.transpose(1, 0, 2).reshape(rows_here, owners * channels)
    stream = (residual.astype(jnp.float32) + token_mix.astype(jnp.float32)).astype(jnp.bfloat16)
    widened = stream.astype(jnp.float32)
    normed = (
        widened
        * lax.rsqrt(jnp.mean(widened * widened, axis=-1, keepdims=True) + 1e-06)
        * norm_gain[None, :]
    ).astype(jnp.bfloat16)
    local_experts = w_gate.shape[0]
    experts = owners * local_experts
    capacity = max(2, 2 * rows_here // experts + 1)
    width = residual.shape[1]
    chosen = expert_ids.reshape(-1)
    onehot = (chosen[:, None] == jnp.arange(experts)[None, :]).astype(jnp.int32)
    slot_index = jnp.sum((jnp.cumsum(onehot, axis=0) - onehot) * onehot, axis=1)
    target = chosen * capacity + slot_index
    placing = (target[None, :] == jnp.arange(experts * capacity)[:, None]).astype(jnp.bfloat16)
    pair_rows = jnp.repeat(normed, 2, axis=0)
    outgoing = jnp.dot(placing, pair_rows, preferred_element_type=jnp.float32).astype(jnp.bfloat16)
    block = capacity * width // 16
    arrived = exchange(outgoing.reshape(experts, 16, block), 1)
    arrived = arrived.reshape(capacity * experts, width)
    segment = lax.all_gather(arrived, "seq", axis=0, tiled=True)
    gate_proj = jnp.dot(segment, w_gate[0], preferred_element_type=jnp.float32)
    up_proj = jnp.dot(segment, w_up[0], preferred_element_type=jnp.float32)
    active = (jax.nn.silu(gate_proj) * up_proj).astype(jnp.bfloat16)
    partial_value = jnp.dot(active, w_down[0], preferred_element_type=jnp.float32)
    summed = lax.psum_scatter(partial_value.astype(jnp.bfloat16), "seq", scatter_dimension=0, tiled=True)
    returned = exchange(summed.reshape(experts, 16, block), 2)
    results = returned.reshape(experts * capacity, width)
    picked = results[target].astype(jnp.float32).reshape(rows_here, 2, width)
    mixture = jnp.sum(picked * gate_weights[:, :, None], axis=1)
    return (widened + mixture).astype(jnp.bfloat16)


def solution(mesh):
    return jax.shard_map(
        on_device,
        mesh=mesh,
        in_specs=(
            P("seq", "exp"),
            P("seq", "exp"),
            P("seq", None),
            P("seq", None),
            P("seq", "exp"),
            P("exp"),
            P("exp"),
            P("exp", None, None),
            P(("seq", "exp"), None),
            P(),
            P(("seq", "exp"), None),
            P(("seq", "exp"), None),
            P("exp", None, "seq"),
            P("exp", None, "seq"),
            P("exp", "seq", None),
        ),
        out_specs=P(("seq", "exp"), None),
        check_vma=False,
    )
```

```python
import functools

import jax
import jax.numpy as jnp
from jax import lax
from jax.sharding import PartitionSpec as P
from jax.experimental import pallas as pl
from jax.experimental.pallas import tpu as pltpu

GROUP = 128


PRECISE = lax.Precision.HIGHEST


def exchange_body(x_ref, o_ref, send_sem, recv_sem, local_sem):
    devices = x_ref.shape[0]
    me = lax.axis_index("exp")
    row = lax.axis_index("seq")
    mesh_id = pl.DeviceIdType.MESH
    barrier = pltpu.get_barrier_semaphore()
    for step in range(1, devices):
        peer = lax.rem(me + step, devices)
        pl.semaphore_signal(barrier, 1, device_id=(row, peer), device_id_type=mesh_id)
    pl.semaphore_wait(barrier, devices - 1)
    local = pltpu.make_async_copy(x_ref.at[me], o_ref.at[me], local_sem)
    local.start()
    copies = []
    for step in range(1, devices):
        peer = lax.rem(me + step, devices)
        copy = pltpu.make_async_remote_copy(
            src_ref=x_ref.at[peer],
            dst_ref=o_ref.at[me],
            send_sem=send_sem.at[step],
            recv_sem=recv_sem.at[step],
            device_id=(row, peer),
            device_id_type=mesh_id,
        )
        copy.start()
        copies.append(copy)
    local.wait()
    for copy in copies:
        copy.wait()


def exchange(x, collective):
    devices = x.shape[0]
    return pl.pallas_call(
        exchange_body,
        out_shape=jax.ShapeDtypeStruct(x.shape, x.dtype),
        in_specs=[pl.BlockSpec(memory_space=pltpu.VMEM)],
        out_specs=pl.BlockSpec(memory_space=pltpu.VMEM),
        scratch_shapes=[
            pltpu.SemaphoreType.DMA((devices,)),
            pltpu.SemaphoreType.DMA((devices,)),
            pltpu.SemaphoreType.DMA,
        ],
        compiler_params=pltpu.CompilerParams(collective_id=collective, has_side_effects=True),
    )(x)


def scan_rounds(devices):
    rounds, base = [], 1
    while base < devices:
        rounds.append([j * base for j in range(1, 4) if j * base < devices])
        base *= 4
    return rounds


def fold(earlier, later, state_rows):
    row = lax.broadcasted_iota(jnp.int32, later.shape, 1)
    decay = jnp.exp(later[:, state_rows:state_rows + 1, :])
    return jnp.where(row < state_rows, decay, 1.0) * earlier + later


def scan_body(devices, state_rows, x_ref, o_ref, inc_ref, recv_ref, send_sem, recv_sem):
    me = lax.axis_index("seq")
    col = lax.axis_index("exp")
    mesh_id = pl.DeviceIdType.MESH
    barrier = pltpu.get_barrier_semaphore()
    for step in range(1, devices):
        peer = lax.rem(me + step, devices)
        pl.semaphore_signal(barrier, 1, device_id=(peer, col), device_id_type=mesh_id)
    pl.semaphore_wait(barrier, devices - 1)
    inc_ref[0] = x_ref[...]
    o_ref[...] = jnp.zeros_like(o_ref)
    for level, shifts in enumerate(scan_rounds(devices)):
        def link(slot, shift, peer):
            return pltpu.make_async_remote_copy(
                src_ref=inc_ref.at[level],
                dst_ref=recv_ref.at[level, slot],
                send_sem=send_sem.at[level, slot],
                recv_sem=recv_sem.at[level, slot],
                device_id=(peer, col),
                device_id_type=mesh_id,
            )
        for slot, shift in enumerate(shifts):
            @pl.when(me + shift < devices)
            def _():
                link(slot, shift, me + shift).start()
        inc_ref[level + 1] = inc_ref[level]
        for slot, shift in enumerate(shifts):
            @pl.when(me >= shift)
            def _():
                link(slot, shift, me - shift).wait_recv()
                got = recv_ref[level, slot]
                inc_ref[level + 1] = fold(got, inc_ref[level + 1], state_rows)
                o_ref[...] = fold(got, o_ref[...], state_rows)
        for slot, shift in enumerate(shifts):
            @pl.when(me + shift < devices)
            def _():
                link(slot, shift, me + shift).wait_send()


def exclusive_scan(log, state, axis):
    devices = lax.axis_size(axis)
    heads, state_rows, lanes = state.shape
    packed = jnp.concatenate(
        [state, jnp.broadcast_to(log[:, None, None], (heads, 8, lanes))], axis=1
    )
    levels = len(scan_rounds(devices))
    result = pl.pallas_call(
        functools.partial(scan_body, devices, state_rows),
        out_shape=jax.ShapeDtypeStruct(packed.shape, packed.dtype),
        in_specs=[pl.BlockSpec(memory_space=pltpu.VMEM)],
        out_specs=pl.BlockSpec(memory_space=pltpu.VMEM),
        scratch_shapes=[
            pltpu.VMEM((levels + 1,) + packed.shape, packed.dtype),
            pltpu.VMEM((levels, 3) + packed.shape, packed.dtype),
            pltpu.SemaphoreType.DMA((levels, 3)),
            pltpu.SemaphoreType.DMA((levels, 3)),
        ],
        compiler_params=pltpu.CompilerParams(collective_id=3, has_side_effects=True),
    )(packed)
    return result[:, state_rows, 0], result[:, :state_rows, :]


def chain_combine(earlier, later):
    return (earlier[0] + later[0], jnp.exp(later[0])[:, None, None] * earlier[1] + later[1])


def on_device(
    x_in,
    z_gate,
    b_in,
    c_out,
    dt_step,
    rate,
    skip,
    init_state,
    residual,
    norm_gain,
    expert_ids,
    gate_weights,
    w_gate,
    w_up,
    w_down,
):
    token_count, channels = x_in.shape
    heads_here = rate.shape[0]
    head_width = channels // heads_here
    state_width = b_in.shape[1]
    blocks = token_count // GROUP
    inputs = x_in.astype(jnp.float32).reshape(blocks, GROUP, heads_here, head_width)
    keys_in = b_in.astype(jnp.float32).reshape(blocks, GROUP, state_width)
    queries = c_out.astype(jnp.float32).reshape(blocks, GROUP, state_width)
    log_steps = (-rate[None, :] * dt_step).reshape(blocks, GROUP, heads_here)
    cumulative = jnp.cumsum(log_steps, axis=1)
    scores = jnp.einsum("ctn,csn->cts", queries, keys_in, precision=PRECISE)
    causal = jnp.arange(GROUP)[:, None] >= jnp.arange(GROUP)[None, :]
    spread = cumulative[:, :, None, :] - cumulative[:, None, :, :]
    weights = jnp.exp(jnp.where(causal[None, :, :, None], spread, -jnp.inf)) * scores[..., None]
    intra_out = jnp.einsum("ctsh,cshp->cthp", weights, inputs, precision=PRECISE)
    tail_decay = jnp.exp(cumulative[:, -1:, :] - cumulative)
    block_state = jnp.einsum("csh,cshp,csn->chpn", tail_decay, inputs, keys_in, precision=PRECISE)
    block_log = cumulative[:, -1, :]

    def advance(carried, element):
        total_log, total_state = carried
        step_log, step_state = element
        updated = (
            total_log + step_log,
            jnp.exp(step_log)[:, None, None] * total_state + step_state,
        )
        return (updated, (total_log, total_state))

    zero_state = jnp.zeros((heads_here, head_width, state_width), jnp.float32)
    zero_log = jnp.zeros((heads_here,), jnp.float32)
    (device_log, device_state), (enter_log, enter_state) = lax.scan(
        advance, (zero_log, zero_state), (block_log, block_state)
    )
    prior_log, prior_state = exclusive_scan(device_log, device_state, "seq")
    incoming = prior_state + jnp.exp(prior_log)[:, None, None] * init_state
    entering = enter_state + jnp.exp(enter_log)[:, :, None, None] * incoming[None]
    inter_out = jnp.exp(cumulative)[..., None] * jnp.einsum(
        "chpn,ctn->cthp", entering, queries, precision=PRECISE
    )
    mixed_out = (intra_out + inter_out + skip[None, None, :, None] * inputs).reshape(
        token_count, channels
    )
    mixer = (mixed_out * jax.nn.silu(z_gate.astype(jnp.float32))).astype(jnp.bfloat16)
    owners = lax.axis_size("exp")
    rows_here = residual.shape[0]
    arrived_mix = exchange(mixer.reshape(owners, rows_here, channels), 0)
    token_mix = arrived_mix.transpose(1, 0, 2).reshape(rows_here, owners * channels)
    stream = (residual.astype(jnp.float32) + token_mix.astype(jnp.float32)).astype(jnp.bfloat16)
    widened = stream.astype(jnp.float32)
    normed = (
        widened
        * lax.rsqrt(jnp.mean(widened * widened, axis=-1, keepdims=True) + 1e-06)
        * norm_gain[None, :]
    ).astype(jnp.bfloat16)
    local_experts = w_gate.shape[0]
    experts = owners * local_experts
    capacity = max(2, 2 * rows_here // experts + 1)
    width = residual.shape[1]
    chosen = expert_ids.reshape(-1)
    onehot = (chosen[:, None] == jnp.arange(experts)[None, :]).astype(jnp.int32)
    slot_index = jnp.sum((jnp.cumsum(onehot, axis=0) - onehot) * onehot, axis=1)
    target = chosen * capacity + slot_index
    placing = (target[None, :] == jnp.arange(experts * capacity)[:, None]).astype(jnp.bfloat16)
    pair_rows = jnp.repeat(normed, 2, axis=0)
    outgoing = jnp.dot(placing, pair_rows, preferred_element_type=jnp.float32).astype(jnp.bfloat16)
    block = capacity * width // 16
    arrived = exchange(outgoing.reshape(experts, 16, block), 1)
    arrived = arrived.reshape(capacity * experts, width)
    segment = lax.all_gather(arrived, "seq", axis=0, tiled=True)
    gate_proj = jnp.dot(segment, w_gate[0], preferred_element_type=jnp.float32)
    up_proj = jnp.dot(segment, w_up[0], preferred_element_type=jnp.float32)
    active = (jax.nn.silu(gate_proj) * up_proj).astype(jnp.bfloat16)
    partial_value = jnp.dot(active, w_down[0], preferred_element_type=jnp.float32)
    summed = lax.psum_scatter(partial_value.astype(jnp.bfloat16), "seq", scatter_dimension=0, tiled=True)
    returned = exchange(summed.reshape(experts, 16, block), 2)
    results = returned.reshape(experts * capacity, width)
    picked = results[target].astype(jnp.float32).reshape(rows_here, 2, width)
    mixture = jnp.sum(picked * gate_weights[:, :, None], axis=1)
    return (widened + mixture).astype(jnp.bfloat16)


def solution(mesh):
    return jax.shard_map(
        on_device,
        mesh=mesh,
        in_specs=(
            P("seq", "exp"),
            P("seq", "exp"),
            P("seq", None),
            P("seq", None),
            P("seq", "exp"),
            P("exp"),
            P("exp"),
            P("exp", None, None),
            P(("seq", "exp"), None),
            P(),
            P(("seq", "exp"), None),
            P(("seq", "exp"), None),
            P("exp", None, "seq"),
            P("exp", None, "seq"),
            P("exp", "seq", None),
        ),
        out_specs=P(("seq", "exp"), None),
        check_vma=False,
    )
```

```python
import functools

import jax
import jax.numpy as jnp
from jax import lax
from jax.sharding import PartitionSpec as P
from jax.experimental import pallas as pl
from jax.experimental.pallas import tpu as pltpu

GROUP = 128


PRECISE = lax.Precision.HIGHEST


def exchange_body(x_ref, o_ref, send_sem, recv_sem, local_sem):
    devices = x_ref.shape[0]
    me = lax.axis_index("exp")
    row = lax.axis_index("seq")
    mesh_id = pl.DeviceIdType.MESH
    barrier = pltpu.get_barrier_semaphore()
    for step in range(1, devices):
        peer = lax.rem(me + step, devices)
        pl.semaphore_signal(barrier, 1, device_id=(row, peer), device_id_type=mesh_id)
    pl.semaphore_wait(barrier, devices - 1)
    local = pltpu.make_async_copy(x_ref.at[me], o_ref.at[me], local_sem)
    local.start()
    copies = []
    for step in range(1, devices):
        peer = lax.rem(me + step, devices)
        copy = pltpu.make_async_remote_copy(
            src_ref=x_ref.at[peer],
            dst_ref=o_ref.at[me],
            send_sem=send_sem.at[step],
            recv_sem=recv_sem.at[step],
            device_id=(row, peer),
            device_id_type=mesh_id,
        )
        copy.start()
        copies.append(copy)
    local.wait()
    for copy in copies:
        copy.wait()


def exchange(x, collective):
    devices = x.shape[0]
    return pl.pallas_call(
        exchange_body,
        out_shape=jax.ShapeDtypeStruct(x.shape, x.dtype),
        in_specs=[pl.BlockSpec(memory_space=pltpu.VMEM)],
        out_specs=pl.BlockSpec(memory_space=pltpu.VMEM),
        scratch_shapes=[
            pltpu.SemaphoreType.DMA((devices,)),
            pltpu.SemaphoreType.DMA((devices,)),
            pltpu.SemaphoreType.DMA,
        ],
        compiler_params=pltpu.CompilerParams(collective_id=collective, has_side_effects=True),
    )(x)


def down_body(a_ref, w_ref, o_ref):
    o_ref[...] = jnp.dot(a_ref[...], w_ref[...], preferred_element_type=jnp.float32).astype(o_ref.dtype)


def down_project(active, weight):
    rows, inner = active.shape
    width = weight.shape[1]
    columns = 1024
    return pl.pallas_call(
        down_body,
        grid=(width // columns,),
        in_specs=[
            pl.BlockSpec((rows, inner), lambda j: (0, 0)),
            pl.BlockSpec((inner, columns), lambda j: (0, j)),
        ],
        out_specs=pl.BlockSpec((rows, columns), lambda j: (0, j)),
        out_shape=jax.ShapeDtypeStruct((rows, width), jnp.bfloat16),
        cost_estimate=pl.CostEstimate(
            flops=2 * rows * inner * width,
            transcendentals=0,
            bytes_accessed=2 * (rows * inner + inner * width + rows * width),
        ),
    )(active, weight)


def scan_rounds(devices):
    rounds, base = [], 1
    while base < devices:
        rounds.append([j * base for j in range(1, 4) if j * base < devices])
        base *= 4
    return rounds


def fold(earlier, later, state_rows):
    row = lax.broadcasted_iota(jnp.int32, later.shape, 1)
    decay = jnp.exp(later[:, state_rows:state_rows + 1, :])
    return jnp.where(row < state_rows, decay, 1.0) * earlier + later


def scan_body(devices, state_rows, x_ref, o_ref, inc_ref, recv_ref, send_sem, recv_sem):
    me = lax.axis_index("seq")
    col = lax.axis_index("exp")
    mesh_id = pl.DeviceIdType.MESH
    barrier = pltpu.get_barrier_semaphore()
    for step in range(1, devices):
        peer = lax.rem(me + step, devices)
        pl.semaphore_signal(barrier, 1, device_id=(peer, col), device_id_type=mesh_id)
    pl.semaphore_wait(barrier, devices - 1)
    inc_ref[0] = x_ref[...]
    o_ref[...] = jnp.zeros_like(o_ref)
    for level, shifts in enumerate(scan_rounds(devices)):
        def link(slot, shift, peer):
            return pltpu.make_async_remote_copy(
                src_ref=inc_ref.at[level],
                dst_ref=recv_ref.at[level, slot],
                send_sem=send_sem.at[level, slot],
                recv_sem=recv_sem.at[level, slot],
                device_id=(peer, col),
                device_id_type=mesh_id,
            )
        for slot, shift in enumerate(shifts):
            @pl.when(me + shift < devices)
            def _():
                link(slot, shift, me + shift).start()
        inc_ref[level + 1] = inc_ref[level]
        for slot, shift in enumerate(shifts):
            @pl.when(me >= shift)
            def _():
                link(slot, shift, me - shift).wait_recv()
                got = recv_ref[level, slot]
                inc_ref[level + 1] = fold(got, inc_ref[level + 1], state_rows)
                o_ref[...] = fold(got, o_ref[...], state_rows)
        for slot, shift in enumerate(shifts):
            @pl.when(me + shift < devices)
            def _():
                link(slot, shift, me + shift).wait_send()


def exclusive_scan(log, state, axis):
    devices = lax.axis_size(axis)
    heads, state_rows, lanes = state.shape
    packed = jnp.concatenate(
        [state, jnp.broadcast_to(log[:, None, None], (heads, 8, lanes))], axis=1
    )
    levels = len(scan_rounds(devices))
    result = pl.pallas_call(
        functools.partial(scan_body, devices, state_rows),
        out_shape=jax.ShapeDtypeStruct(packed.shape, packed.dtype),
        in_specs=[pl.BlockSpec(memory_space=pltpu.VMEM)],
        out_specs=pl.BlockSpec(memory_space=pltpu.VMEM),
        scratch_shapes=[
            pltpu.VMEM((levels + 1,) + packed.shape, packed.dtype),
            pltpu.VMEM((levels, 3) + packed.shape, packed.dtype),
            pltpu.SemaphoreType.DMA((levels, 3)),
            pltpu.SemaphoreType.DMA((levels, 3)),
        ],
        compiler_params=pltpu.CompilerParams(collective_id=3, has_side_effects=True),
    )(packed)
    return result[:, state_rows, 0], result[:, :state_rows, :]


def chain_combine(earlier, later):
    return (earlier[0] + later[0], jnp.exp(later[0])[:, None, None] * earlier[1] + later[1])


def on_device(
    x_in,
    z_gate,
    b_in,
    c_out,
    dt_step,
    rate,
    skip,
    init_state,
    residual,
    norm_gain,
    expert_ids,
    gate_weights,
    w_gate,
    w_up,
    w_down,
):
    token_count, channels = x_in.shape
    heads_here = rate.shape[0]
    head_width = channels // heads_here
    state_width = b_in.shape[1]
    blocks = token_count // GROUP
    inputs = x_in.astype(jnp.float32).reshape(blocks, GROUP, heads_here, head_width)
    keys_in = b_in.astype(jnp.float32).reshape(blocks, GROUP, state_width)
    queries = c_out.astype(jnp.float32).reshape(blocks, GROUP, state_width)
    log_steps = (-rate[None, :] * dt_step).reshape(blocks, GROUP, heads_here)
    cumulative = jnp.cumsum(log_steps, axis=1)
    scores = jnp.einsum("ctn,csn->cts", queries, keys_in, precision=PRECISE)
    causal = jnp.arange(GROUP)[:, None] >= jnp.arange(GROUP)[None, :]
    spread = cumulative[:, :, None, :] - cumulative[:, None, :, :]
    weights = jnp.exp(jnp.where(causal[None, :, :, None], spread, -jnp.inf)) * scores[..., None]
    intra_out = jnp.einsum("ctsh,cshp->cthp", weights, inputs, precision=PRECISE)
    tail_decay = jnp.exp(cumulative[:, -1:, :] - cumulative)
    block_state = jnp.einsum("csh,cshp,csn->chpn", tail_decay, inputs, keys_in, precision=PRECISE)
    block_log = cumulative[:, -1, :]

    def advance(carried, element):
        total_log, total_state = carried
        step_log, step_state = element
        updated = (
            total_log + step_log,
            jnp.exp(step_log)[:, None, None] * total_state + step_state,
        )
        return (updated, (total_log, total_state))

    zero_state = jnp.zeros((heads_here, head_width, state_width), jnp.float32)
    zero_log = jnp.zeros((heads_here,), jnp.float32)
    (device_log, device_state), (enter_log, enter_state) = lax.scan(
        advance, (zero_log, zero_state), (block_log, block_state)
    )
    prior_log, prior_state = exclusive_scan(device_log, device_state, "seq")
    incoming = prior_state + jnp.exp(prior_log)[:, None, None] * init_state
    entering = enter_state + jnp.exp(enter_log)[:, :, None, None] * incoming[None]
    inter_out = jnp.exp(cumulative)[..., None] * jnp.einsum(
        "chpn,ctn->cthp", entering, queries, precision=PRECISE
    )
    mixed_out = (intra_out + inter_out + skip[None, None, :, None] * inputs).reshape(
        token_count, channels
    )
    mixer = (mixed_out * jax.nn.silu(z_gate.astype(jnp.float32))).astype(jnp.bfloat16)
    owners = lax.axis_size("exp")
    rows_here = residual.shape[0]
    arrived_mix = exchange(mixer.reshape(owners, rows_here, channels), 0)
    token_mix = arrived_mix.transpose(1, 0, 2).reshape(rows_here, owners * channels)
    stream = (residual.astype(jnp.float32) + token_mix.astype(jnp.float32)).astype(jnp.bfloat16)
    widened = stream.astype(jnp.float32)
    normed = (
        widened
        * lax.rsqrt(jnp.mean(widened * widened, axis=-1, keepdims=True) + 1e-06)
        * norm_gain[None, :]
    ).astype(jnp.bfloat16)
    local_experts = w_gate.shape[0]
    experts = owners * local_experts
    capacity = max(2, 2 * rows_here // experts + 1)
    width = residual.shape[1]
    chosen = expert_ids.reshape(-1)
    onehot = (chosen[:, None] == jnp.arange(experts)[None, :]).astype(jnp.int32)
    slot_index = jnp.sum((jnp.cumsum(onehot, axis=0) - onehot) * onehot, axis=1)
    target = chosen * capacity + slot_index
    placing = (target[None, :] == jnp.arange(experts * capacity)[:, None]).astype(jnp.bfloat16)
    pair_rows = jnp.repeat(normed, 2, axis=0)
    outgoing = jnp.dot(placing, pair_rows, preferred_element_type=jnp.float32).astype(jnp.bfloat16)
    block = capacity * width // 16
    arrived = exchange(outgoing.reshape(experts, 16, block), 1)
    arrived = arrived.reshape(capacity * experts, width)
    segment = lax.all_gather(arrived, "seq", axis=0, tiled=True)
    gate_proj = jnp.dot(segment, w_gate[0], preferred_element_type=jnp.float32)
    up_proj = jnp.dot(segment, w_up[0], preferred_element_type=jnp.float32)
    active = (jax.nn.silu(gate_proj) * up_proj).astype(jnp.bfloat16)
    partial_value = down_project(active, w_down[0])
    summed = lax.psum_scatter(partial_value, "seq", scatter_dimension=0, tiled=True)
    returned = exchange(summed.reshape(experts, 16, block), 2)
    results = returned.reshape(experts * capacity, width)
    picked = results[target].astype(jnp.float32).reshape(rows_here, 2, width)
    mixture = jnp.sum(picked * gate_weights[:, :, None], axis=1)
    return (widened + mixture).astype(jnp.bfloat16)


def solution(mesh):
    return jax.shard_map(
        on_device,
        mesh=mesh,
        in_specs=(
            P("seq", "exp"),
            P("seq", "exp"),
            P("seq", None),
            P("seq", None),
            P("seq", "exp"),
            P("exp"),
            P("exp"),
            P("exp", None, None),
            P(("seq", "exp"), None),
            P(),
            P(("seq", "exp"), None),
            P(("seq", "exp"), None),
            P("exp", None, "seq"),
            P("exp", None, "seq"),
            P("exp", "seq", None),
        ),
        out_specs=P(("seq", "exp"), None),
        check_vma=False,
    )
```

```python
import functools

import jax
import jax.numpy as jnp
from jax import lax
from jax.sharding import PartitionSpec as P
from jax.experimental import pallas as pl
from jax.experimental.pallas import tpu as pltpu

GROUP = 128


PRECISE = lax.Precision.HIGHEST


def exchange_body(x_ref, o_ref, send_sem, recv_sem, local_sem):
    devices = x_ref.shape[0]
    me = lax.axis_index("exp")
    row = lax.axis_index("seq")
    mesh_id = pl.DeviceIdType.MESH
    barrier = pltpu.get_barrier_semaphore()
    for step in range(1, devices):
        peer = lax.rem(me + step, devices)
        pl.semaphore_signal(barrier, 1, device_id=(row, peer), device_id_type=mesh_id)
    pl.semaphore_wait(barrier, devices - 1)
    local = pltpu.make_async_copy(x_ref.at[me], o_ref.at[me], local_sem)
    local.start()
    copies = []
    for step in range(1, devices):
        peer = lax.rem(me + step, devices)
        copy = pltpu.make_async_remote_copy(
            src_ref=x_ref.at[peer],
            dst_ref=o_ref.at[me],
            send_sem=send_sem.at[step],
            recv_sem=recv_sem.at[step],
            device_id=(row, peer),
            device_id_type=mesh_id,
        )
        copy.start()
        copies.append(copy)
    local.wait()
    for copy in copies:
        copy.wait()


def exchange(x, collective):
    devices = x.shape[0]
    return pl.pallas_call(
        exchange_body,
        out_shape=jax.ShapeDtypeStruct(x.shape, x.dtype),
        in_specs=[pl.BlockSpec(memory_space=pltpu.VMEM)],
        out_specs=pl.BlockSpec(memory_space=pltpu.VMEM),
        scratch_shapes=[
            pltpu.SemaphoreType.DMA((devices,)),
            pltpu.SemaphoreType.DMA((devices,)),
            pltpu.SemaphoreType.DMA,
        ],
        compiler_params=pltpu.CompilerParams(collective_id=collective, has_side_effects=True),
    )(x)


def expert_body(depth_steps, seg_ref, gate_ref, up_ref, down_ref, o_ref, gate_acc, up_acc, active):
    step = pl.program_id(0)

    @pl.when(step == 0)
    def _():
        gate_acc[...] = jnp.zeros_like(gate_acc)
        up_acc[...] = jnp.zeros_like(up_acc)

    @pl.when(step < depth_steps)
    def _():
        rows = seg_ref[...]
        gate_acc[...] += jnp.dot(rows, gate_ref[...], preferred_element_type=jnp.float32)
        up_acc[...] += jnp.dot(rows, up_ref[...], preferred_element_type=jnp.float32)

    @pl.when(step == depth_steps - 1)
    def _():
        gate = gate_acc[...]
        active[...] = (gate / (1.0 + jnp.exp(-gate)) * up_acc[...]).astype(active.dtype)

    @pl.when(step >= depth_steps)
    def _():
        o_ref[...] = jnp.dot(
            active[...], down_ref[...], preferred_element_type=jnp.float32
        ).astype(o_ref.dtype)


def expert_mlp(segment, gate_w, up_w, down_w):
    rows, width = segment.shape
    hidden = gate_w.shape[1]
    block = 1024
    depth_steps = width // block
    column_steps = width // block
    return pl.pallas_call(
        functools.partial(expert_body, depth_steps),
        grid=(depth_steps + column_steps,),
        in_specs=[
            pl.BlockSpec((rows, block), lambda i: (0, jnp.minimum(i, depth_steps - 1))),
            pl.BlockSpec((block, hidden), lambda i: (jnp.minimum(i, depth_steps - 1), 0)),
            pl.BlockSpec((block, hidden), lambda i: (jnp.minimum(i, depth_steps - 1), 0)),
            pl.BlockSpec((hidden, block), lambda i: (0, jnp.maximum(i - depth_steps, 0))),
        ],
        out_specs=pl.BlockSpec((rows, block), lambda i: (0, jnp.maximum(i - depth_steps, 0))),
        out_shape=jax.ShapeDtypeStruct((rows, width), jnp.bfloat16),
        scratch_shapes=[
            pltpu.VMEM((rows, hidden), jnp.float32),
            pltpu.VMEM((rows, hidden), jnp.float32),
            pltpu.VMEM((rows, hidden), jnp.bfloat16),
        ],
        cost_estimate=pl.CostEstimate(
            flops=6 * rows * width * hidden,
            transcendentals=rows * hidden,
            bytes_accessed=2 * (2 * rows * width + 3 * width * hidden),
        ),
    )(segment, gate_w, up_w, down_w)


def scan_rounds(devices):
    rounds, base = [], 1
    while base < devices:
        rounds.append([j * base for j in range(1, 4) if j * base < devices])
        base *= 4
    return rounds


def fold(earlier, later, state_rows):
    row = lax.broadcasted_iota(jnp.int32, later.shape, 1)
    decay = jnp.exp(later[:, state_rows:state_rows + 1, :])
    return jnp.where(row < state_rows, decay, 1.0) * earlier + later


def scan_body(devices, state_rows, x_ref, o_ref, inc_ref, recv_ref, send_sem, recv_sem):
    me = lax.axis_index("seq")
    col = lax.axis_index("exp")
    mesh_id = pl.DeviceIdType.MESH
    barrier = pltpu.get_barrier_semaphore()
    for step in range(1, devices):
        peer = lax.rem(me + step, devices)
        pl.semaphore_signal(barrier, 1, device_id=(peer, col), device_id_type=mesh_id)
    pl.semaphore_wait(barrier, devices - 1)
    inc_ref[0] = x_ref[...]
    o_ref[...] = jnp.zeros_like(o_ref)
    for level, shifts in enumerate(scan_rounds(devices)):
        def link(slot, shift, peer):
            return pltpu.make_async_remote_copy(
                src_ref=inc_ref.at[level],
                dst_ref=recv_ref.at[level, slot],
                send_sem=send_sem.at[level, slot],
                recv_sem=recv_sem.at[level, slot],
                device_id=(peer, col),
                device_id_type=mesh_id,
            )
        for slot, shift in enumerate(shifts):
            @pl.when(me + shift < devices)
            def _():
                link(slot, shift, me + shift).start()
        inc_ref[level + 1] = inc_ref[level]
        for slot, shift in enumerate(shifts):
            @pl.when(me >= shift)
            def _():
                link(slot, shift, me - shift).wait_recv()
                got = recv_ref[level, slot]
                inc_ref[level + 1] = fold(got, inc_ref[level + 1], state_rows)
                o_ref[...] = fold(got, o_ref[...], state_rows)
        for slot, shift in enumerate(shifts):
            @pl.when(me + shift < devices)
            def _():
                link(slot, shift, me + shift).wait_send()


def exclusive_scan(log, state, axis):
    devices = lax.axis_size(axis)
    heads, state_rows, lanes = state.shape
    packed = jnp.concatenate(
        [state, jnp.broadcast_to(log[:, None, None], (heads, 8, lanes))], axis=1
    )
    levels = len(scan_rounds(devices))
    result = pl.pallas_call(
        functools.partial(scan_body, devices, state_rows),
        out_shape=jax.ShapeDtypeStruct(packed.shape, packed.dtype),
        in_specs=[pl.BlockSpec(memory_space=pltpu.VMEM)],
        out_specs=pl.BlockSpec(memory_space=pltpu.VMEM),
        scratch_shapes=[
            pltpu.VMEM((levels + 1,) + packed.shape, packed.dtype),
            pltpu.VMEM((levels, 3) + packed.shape, packed.dtype),
            pltpu.SemaphoreType.DMA((levels, 3)),
            pltpu.SemaphoreType.DMA((levels, 3)),
        ],
        compiler_params=pltpu.CompilerParams(collective_id=3, has_side_effects=True),
    )(packed)
    return result[:, state_rows, 0], result[:, :state_rows, :]


def chain_combine(earlier, later):
    return (earlier[0] + later[0], jnp.exp(later[0])[:, None, None] * earlier[1] + later[1])


def on_device(
    x_in,
    z_gate,
    b_in,
    c_out,
    dt_step,
    rate,
    skip,
    init_state,
    residual,
    norm_gain,
    expert_ids,
    gate_weights,
    w_gate,
    w_up,
    w_down,
):
    token_count, channels = x_in.shape
    heads_here = rate.shape[0]
    head_width = channels // heads_here
    state_width = b_in.shape[1]
    blocks = token_count // GROUP
    inputs = x_in.astype(jnp.float32).reshape(blocks, GROUP, heads_here, head_width)
    keys_in = b_in.astype(jnp.float32).reshape(blocks, GROUP, state_width)
    queries = c_out.astype(jnp.float32).reshape(blocks, GROUP, state_width)
    log_steps = (-rate[None, :] * dt_step).reshape(blocks, GROUP, heads_here)
    cumulative = jnp.cumsum(log_steps, axis=1)
    scores = jnp.einsum("ctn,csn->cts", queries, keys_in, precision=PRECISE)
    causal = jnp.arange(GROUP)[:, None] >= jnp.arange(GROUP)[None, :]
    spread = cumulative[:, :, None, :] - cumulative[:, None, :, :]
    weights = jnp.exp(jnp.where(causal[None, :, :, None], spread, -jnp.inf)) * scores[..., None]
    intra_out = jnp.einsum("ctsh,cshp->cthp", weights, inputs, precision=PRECISE)
    tail_decay = jnp.exp(cumulative[:, -1:, :] - cumulative)
    block_state = jnp.einsum("csh,cshp,csn->chpn", tail_decay, inputs, keys_in, precision=PRECISE)
    block_log = cumulative[:, -1, :]

    def advance(carried, element):
        total_log, total_state = carried
        step_log, step_state = element
        updated = (
            total_log + step_log,
            jnp.exp(step_log)[:, None, None] * total_state + step_state,
        )
        return (updated, (total_log, total_state))

    zero_state = jnp.zeros((heads_here, head_width, state_width), jnp.float32)
    zero_log = jnp.zeros((heads_here,), jnp.float32)
    (device_log, device_state), (enter_log, enter_state) = lax.scan(
        advance, (zero_log, zero_state), (block_log, block_state)
    )
    prior_log, prior_state = exclusive_scan(device_log, device_state, "seq")
    incoming = prior_state + jnp.exp(prior_log)[:, None, None] * init_state
    entering = enter_state + jnp.exp(enter_log)[:, :, None, None] * incoming[None]
    inter_out = jnp.exp(cumulative)[..., None] * jnp.einsum(
        "chpn,ctn->cthp", entering, queries, precision=PRECISE
    )
    mixed_out = (intra_out + inter_out + skip[None, None, :, None] * inputs).reshape(
        token_count, channels
    )
    mixer = (mixed_out * jax.nn.silu(z_gate.astype(jnp.float32))).astype(jnp.bfloat16)
    owners = lax.axis_size("exp")
    rows_here = residual.shape[0]
    arrived_mix = exchange(mixer.reshape(owners, rows_here, channels), 0)
    token_mix = arrived_mix.transpose(1, 0, 2).reshape(rows_here, owners * channels)
    stream = (residual.astype(jnp.float32) + token_mix.astype(jnp.float32)).astype(jnp.bfloat16)
    widened = stream.astype(jnp.float32)
    normed = (
        widened
        * lax.rsqrt(jnp.mean(widened * widened, axis=-1, keepdims=True) + 1e-06)
        * norm_gain[None, :]
    ).astype(jnp.bfloat16)
    local_experts = w_gate.shape[0]
    experts = owners * local_experts
    capacity = max(2, 2 * rows_here // experts + 1)
    width = residual.shape[1]
    chosen = expert_ids.reshape(-1)
    onehot = (chosen[:, None] == jnp.arange(experts)[None, :]).astype(jnp.int32)
    slot_index = jnp.sum((jnp.cumsum(onehot, axis=0) - onehot) * onehot, axis=1)
    target = chosen * capacity + slot_index
    placing = (target[None, :] == jnp.arange(experts * capacity)[:, None]).astype(jnp.bfloat16)
    pair_rows = jnp.repeat(normed, 2, axis=0)
    outgoing = jnp.dot(placing, pair_rows, preferred_element_type=jnp.float32).astype(jnp.bfloat16)
    block = capacity * width // 16
    arrived = exchange(outgoing.reshape(experts, 16, block), 1)
    arrived = arrived.reshape(capacity * experts, width)
    segment = lax.all_gather(arrived, "seq", axis=0, tiled=True)
    partial_value = expert_mlp(segment, w_gate[0], w_up[0], w_down[0])
    summed = lax.psum_scatter(partial_value, "seq", scatter_dimension=0, tiled=True)
    returned = exchange(summed.reshape(experts, 16, block), 2)
    results = returned.reshape(experts * capacity, width)
    picked = results[target].astype(jnp.float32).reshape(rows_here, 2, width)
    mixture = jnp.sum(picked * gate_weights[:, :, None], axis=1)
    return (widened + mixture).astype(jnp.bfloat16)


def solution(mesh):
    return jax.shard_map(
        on_device,
        mesh=mesh,
        in_specs=(
            P("seq", "exp"),
            P("seq", "exp"),
            P("seq", None),
            P("seq", None),
            P("seq", "exp"),
            P("exp"),
            P("exp"),
            P("exp", None, None),
            P(("seq", "exp"), None),
            P(),
            P(("seq", "exp"), None),
            P(("seq", "exp"), None),
            P("exp", None, "seq"),
            P("exp", None, "seq"),
            P("exp", "seq", None),
        ),
        out_specs=P(("seq", "exp"), None),
        check_vma=False,
    )
```

```python
import functools

import jax
import jax.numpy as jnp
from jax import lax
from jax.sharding import PartitionSpec as P
from jax.experimental import pallas as pl
from jax.experimental.pallas import tpu as pltpu

GROUP = 128


PRECISE = lax.Precision.HIGHEST


def exchange_body(x_ref, o_ref, send_sem, recv_sem, local_sem):
    devices = x_ref.shape[0]
    me = lax.axis_index("exp")
    row = lax.axis_index("seq")
    mesh_id = pl.DeviceIdType.MESH
    barrier = pltpu.get_barrier_semaphore()
    for step in range(1, devices):
        peer = lax.rem(me + step, devices)
        pl.semaphore_signal(barrier, 1, device_id=(row, peer), device_id_type=mesh_id)
    pl.semaphore_wait(barrier, devices - 1)
    local = pltpu.make_async_copy(x_ref.at[me], o_ref.at[me], local_sem)
    local.start()
    copies = []
    for step in range(1, devices):
        peer = lax.rem(me + step, devices)
        copy = pltpu.make_async_remote_copy(
            src_ref=x_ref.at[peer],
            dst_ref=o_ref.at[me],
            send_sem=send_sem.at[step],
            recv_sem=recv_sem.at[step],
            device_id=(row, peer),
            device_id_type=mesh_id,
        )
        copy.start()
        copies.append(copy)
    local.wait()
    for copy in copies:
        copy.wait()


def exchange(x, collective):
    devices = x.shape[0]
    return pl.pallas_call(
        exchange_body,
        out_shape=jax.ShapeDtypeStruct(x.shape, x.dtype),
        in_specs=[pl.BlockSpec(memory_space=pltpu.VMEM)],
        out_specs=pl.BlockSpec(memory_space=pltpu.VMEM),
        scratch_shapes=[
            pltpu.SemaphoreType.DMA((devices,)),
            pltpu.SemaphoreType.DMA((devices,)),
            pltpu.SemaphoreType.DMA,
        ],
        compiler_params=pltpu.CompilerParams(collective_id=collective, has_side_effects=True),
    )(x)


def expert_body(depth_steps, seg_ref, gate_ref, up_ref, down_ref, o_ref, gate_acc, up_acc, active):
    step = pl.program_id(0)

    @pl.when(step == 0)
    def _():
        gate_acc[...] = jnp.zeros_like(gate_acc)
        up_acc[...] = jnp.zeros_like(up_acc)

    @pl.when(step < depth_steps)
    def _():
        rows = seg_ref[...]
        gate_acc[...] += jnp.dot(rows, gate_ref[...], preferred_element_type=jnp.float32)
        up_acc[...] += jnp.dot(rows, up_ref[...], preferred_element_type=jnp.float32)

    @pl.when(step == depth_steps - 1)
    def _():
        gate = gate_acc[...]
        active[...] = (gate / (1.0 + jnp.exp(-gate)) * up_acc[...]).astype(active.dtype)

    @pl.when(step >= depth_steps)
    def _():
        o_ref[...] = jnp.dot(
            active[...], down_ref[...], preferred_element_type=jnp.float32
        ).astype(o_ref.dtype)


def expert_mlp(segment, gate_w, up_w, down_w):
    rows, width = segment.shape
    hidden = gate_w.shape[1]
    block = 1024
    depth_steps = width // block
    column_steps = width // block
    return pl.pallas_call(
        functools.partial(expert_body, depth_steps),
        grid=(depth_steps + column_steps,),
        in_specs=[
            pl.BlockSpec((rows, block), lambda i: (0, jnp.minimum(i, depth_steps - 1))),
            pl.BlockSpec((block, hidden), lambda i: (jnp.minimum(i, depth_steps - 1), 0)),
            pl.BlockSpec((block, hidden), lambda i: (jnp.minimum(i, depth_steps - 1), 0)),
            pl.BlockSpec((hidden, block), lambda i: (0, jnp.maximum(i - depth_steps, 0))),
        ],
        out_specs=pl.BlockSpec((rows, block), lambda i: (0, jnp.maximum(i - depth_steps, 0))),
        out_shape=jax.ShapeDtypeStruct((rows, width), jnp.bfloat16),
        scratch_shapes=[
            pltpu.VMEM((rows, hidden), jnp.float32),
            pltpu.VMEM((rows, hidden), jnp.float32),
            pltpu.VMEM((rows, hidden), jnp.bfloat16),
        ],
        cost_estimate=pl.CostEstimate(
            flops=6 * rows * width * hidden,
            transcendentals=rows * hidden,
            bytes_accessed=2 * (2 * rows * width + 3 * width * hidden),
        ),
    )(segment, gate_w, up_w, down_w)


def scan_rounds(devices):
    rounds, base = [], 1
    while base < devices:
        rounds.append([j * base for j in range(1, 4) if j * base < devices])
        base *= 4
    return rounds


def fold(earlier_state, earlier_log, later_state, later_log):
    decay = jnp.exp(later_log[:, 0:1, :])
    return decay * earlier_state + later_state, earlier_log + later_log


def scan_body(devices, x_state, x_log, o_state, o_log, inc_state, inc_log, wire, recv, send_sem, recv_sem):
    me = lax.axis_index("seq")
    col = lax.axis_index("exp")
    rows = x_state.shape[1]
    mesh_id = pl.DeviceIdType.MESH
    barrier = pltpu.get_barrier_semaphore()
    for step in range(1, devices):
        peer = lax.rem(me + step, devices)
        pl.semaphore_signal(barrier, 1, device_id=(peer, col), device_id_type=mesh_id)
    pl.semaphore_wait(barrier, devices - 1)
    inc_state[0] = x_state[...]
    inc_log[0] = x_log[...]
    o_state[...] = jnp.zeros_like(o_state)
    o_log[...] = jnp.zeros_like(o_log)
    for level, shifts in enumerate(scan_rounds(devices)):
        log_now = inc_log[level]
        high = log_now.astype(jnp.bfloat16).astype(jnp.float32)
        wire[level, :, :rows, :] = inc_state[level].astype(jnp.bfloat16)
        wire[level, :, rows:, :] = jnp.concatenate([high, log_now - high], axis=1).astype(jnp.bfloat16)

        def link(slot, peer):
            return pltpu.make_async_remote_copy(
                src_ref=wire.at[level],
                dst_ref=recv.at[level, slot],
                send_sem=send_sem.at[level, slot],
                recv_sem=recv_sem.at[level, slot],
                device_id=(peer, col),
                device_id_type=mesh_id,
            )
        for slot, shift in enumerate(shifts):
            @pl.when(me + shift < devices)
            def _():
                link(slot, me + shift).start()
        inc_state[level + 1] = inc_state[level]
        inc_log[level + 1] = inc_log[level]
        for slot, shift in enumerate(shifts):
            @pl.when(me >= shift)
            def _():
                link(slot, me - shift).wait_recv()
                got_state = recv[level, slot, :, :rows, :].astype(jnp.float32)
                parts = recv[level, slot, :, rows:, :].astype(jnp.float32)
                got_log = parts[:, :8, :] + parts[:, 8:, :]
                new_state, new_log = fold(got_state, got_log, inc_state[level + 1], inc_log[level + 1])
                inc_state[level + 1] = new_state
                inc_log[level + 1] = new_log
                new_state, new_log = fold(got_state, got_log, o_state[...], o_log[...])
                o_state[...] = new_state
                o_log[...] = new_log
        for slot, shift in enumerate(shifts):
            @pl.when(me + shift < devices)
            def _():
                link(slot, me + shift).wait_send()


def exclusive_scan(log, state, axis):
    devices = lax.axis_size(axis)
    heads, state_rows, lanes = state.shape
    log_rows = jnp.broadcast_to(log[:, None, None], (heads, 8, lanes))
    levels = len(scan_rounds(devices))
    wire_shape = (heads, state_rows + 16, lanes)
    prior_state, prior_log = pl.pallas_call(
        functools.partial(scan_body, devices),
        out_shape=(
            jax.ShapeDtypeStruct(state.shape, jnp.float32),
            jax.ShapeDtypeStruct(log_rows.shape, jnp.float32),
        ),
        in_specs=[pl.BlockSpec(memory_space=pltpu.VMEM)] * 2,
        out_specs=(pl.BlockSpec(memory_space=pltpu.VMEM),) * 2,
        scratch_shapes=[
            pltpu.VMEM((levels + 1,) + state.shape, jnp.float32),
            pltpu.VMEM((levels + 1,) + log_rows.shape, jnp.float32),
            pltpu.VMEM((levels,) + wire_shape, jnp.bfloat16),
            pltpu.VMEM((levels, 3) + wire_shape, jnp.bfloat16),
            pltpu.SemaphoreType.DMA((levels, 3)),
            pltpu.SemaphoreType.DMA((levels, 3)),
        ],
        compiler_params=pltpu.CompilerParams(collective_id=3, has_side_effects=True),
    )(state, log_rows)
    return prior_log[:, 0, 0], prior_state


def chain_combine(earlier, later):
    return (earlier[0] + later[0], jnp.exp(later[0])[:, None, None] * earlier[1] + later[1])


def on_device(
    x_in,
    z_gate,
    b_in,
    c_out,
    dt_step,
    rate,
    skip,
    init_state,
    residual,
    norm_gain,
    expert_ids,
    gate_weights,
    w_gate,
    w_up,
    w_down,
):
    token_count, channels = x_in.shape
    heads_here = rate.shape[0]
    head_width = channels // heads_here
    state_width = b_in.shape[1]
    blocks = token_count // GROUP
    inputs = x_in.astype(jnp.float32).reshape(blocks, GROUP, heads_here, head_width)
    keys_in = b_in.astype(jnp.float32).reshape(blocks, GROUP, state_width)
    queries = c_out.astype(jnp.float32).reshape(blocks, GROUP, state_width)
    log_steps = (-rate[None, :] * dt_step).reshape(blocks, GROUP, heads_here)
    cumulative = jnp.cumsum(log_steps, axis=1)
    scores = jnp.einsum("ctn,csn->cts", queries, keys_in, precision=PRECISE)
    causal = jnp.arange(GROUP)[:, None] >= jnp.arange(GROUP)[None, :]
    spread = cumulative[:, :, None, :] - cumulative[:, None, :, :]
    weights = jnp.exp(jnp.where(causal[None, :, :, None], spread, -jnp.inf)) * scores[..., None]
    intra_out = jnp.einsum("ctsh,cshp->cthp", weights, inputs, precision=PRECISE)
    tail_decay = jnp.exp(cumulative[:, -1:, :] - cumulative)
    block_state = jnp.einsum("csh,cshp,csn->chpn", tail_decay, inputs, keys_in, precision=PRECISE)
    block_log = cumulative[:, -1, :]

    def advance(carried, element):
        total_log, total_state = carried
        step_log, step_state = element
        updated = (
            total_log + step_log,
            jnp.exp(step_log)[:, None, None] * total_state + step_state,
        )
        return (updated, (total_log, total_state))

    zero_state = jnp.zeros((heads_here, head_width, state_width), jnp.float32)
    zero_log = jnp.zeros((heads_here,), jnp.float32)
    (device_log, device_state), (enter_log, enter_state) = lax.scan(
        advance, (zero_log, zero_state), (block_log, block_state)
    )
    prior_log, prior_state = exclusive_scan(device_log, device_state, "seq")
    incoming = prior_state + jnp.exp(prior_log)[:, None, None] * init_state
    entering = enter_state + jnp.exp(enter_log)[:, :, None, None] * incoming[None]
    inter_out = jnp.exp(cumulative)[..., None] * jnp.einsum(
        "chpn,ctn->cthp", entering, queries, precision=PRECISE
    )
    mixed_out = (intra_out + inter_out + skip[None, None, :, None] * inputs).reshape(
        token_count, channels
    )
    mixer = (mixed_out * jax.nn.silu(z_gate.astype(jnp.float32))).astype(jnp.bfloat16)
    owners = lax.axis_size("exp")
    rows_here = residual.shape[0]
    arrived_mix = exchange(mixer.reshape(owners, rows_here, channels), 0)
    token_mix = arrived_mix.transpose(1, 0, 2).reshape(rows_here, owners * channels)
    stream = (residual.astype(jnp.float32) + token_mix.astype(jnp.float32)).astype(jnp.bfloat16)
    widened = stream.astype(jnp.float32)
    normed = (
        widened
        * lax.rsqrt(jnp.mean(widened * widened, axis=-1, keepdims=True) + 1e-06)
        * norm_gain[None, :]
    ).astype(jnp.bfloat16)
    local_experts = w_gate.shape[0]
    experts = owners * local_experts
    capacity = max(2, 2 * rows_here // experts + 1)
    width = residual.shape[1]
    chosen = expert_ids.reshape(-1)
    onehot = (chosen[:, None] == jnp.arange(experts)[None, :]).astype(jnp.int32)
    slot_index = jnp.sum((jnp.cumsum(onehot, axis=0) - onehot) * onehot, axis=1)
    target = chosen * capacity + slot_index
    placing = (target[None, :] == jnp.arange(experts * capacity)[:, None]).astype(jnp.bfloat16)
    pair_rows = jnp.repeat(normed, 2, axis=0)
    outgoing = jnp.dot(placing, pair_rows, preferred_element_type=jnp.float32).astype(jnp.bfloat16)
    block = capacity * width // 16
    arrived = exchange(outgoing.reshape(experts, 16, block), 1)
    arrived = arrived.reshape(capacity * experts, width)
    segment = lax.all_gather(arrived, "seq", axis=0, tiled=True)
    partial_value = expert_mlp(segment, w_gate[0], w_up[0], w_down[0])
    summed = lax.psum_scatter(partial_value, "seq", scatter_dimension=0, tiled=True)
    returned = exchange(summed.reshape(experts, 16, block), 2)
    results = returned.reshape(experts * capacity, width)
    picked = results[target].astype(jnp.float32).reshape(rows_here, 2, width)
    mixture = jnp.sum(picked * gate_weights[:, :, None], axis=1)
    return (widened + mixture).astype(jnp.bfloat16)


def solution(mesh):
    return jax.shard_map(
        on_device,
        mesh=mesh,
        in_specs=(
            P("seq", "exp"),
            P("seq", "exp"),
            P("seq", None),
            P("seq", None),
            P("seq", "exp"),
            P("exp"),
            P("exp"),
            P("exp", None, None),
            P(("seq", "exp"), None),
            P(),
            P(("seq", "exp"), None),
            P(("seq", "exp"), None),
            P("exp", None, "seq"),
            P("exp", None, "seq"),
            P("exp", "seq", None),
        ),
        out_specs=P(("seq", "exp"), None),
        check_vma=False,
    )
```

```python
import functools

import jax
import jax.numpy as jnp
from jax import lax
from jax.sharding import PartitionSpec as P
from jax.experimental import pallas as pl
from jax.experimental.pallas import tpu as pltpu

GROUP = 128


PRECISE = lax.Precision.HIGHEST


def exchange_body(x_ref, o_ref, send_sem, recv_sem, local_sem):
    devices = x_ref.shape[0]
    me = lax.axis_index("exp")
    row = lax.axis_index("seq")
    mesh_id = pl.DeviceIdType.MESH
    barrier = pltpu.get_barrier_semaphore()
    for step in range(1, devices):
        peer = lax.rem(me + step, devices)
        pl.semaphore_signal(barrier, 1, device_id=(row, peer), device_id_type=mesh_id)
    pl.semaphore_wait(barrier, devices - 1)
    local = pltpu.make_async_copy(x_ref.at[me], o_ref.at[me], local_sem)
    local.start()
    copies = []
    for step in range(1, devices):
        peer = lax.rem(me + step, devices)
        copy = pltpu.make_async_remote_copy(
            src_ref=x_ref.at[peer],
            dst_ref=o_ref.at[me],
            send_sem=send_sem.at[step],
            recv_sem=recv_sem.at[step],
            device_id=(row, peer),
            device_id_type=mesh_id,
        )
        copy.start()
        copies.append(copy)
    local.wait()
    for copy in copies:
        copy.wait()


def exchange(x, collective):
    devices = x.shape[0]
    return pl.pallas_call(
        exchange_body,
        out_shape=jax.ShapeDtypeStruct(x.shape, x.dtype),
        in_specs=[pl.BlockSpec(memory_space=pltpu.VMEM)],
        out_specs=pl.BlockSpec(memory_space=pltpu.VMEM),
        scratch_shapes=[
            pltpu.SemaphoreType.DMA((devices,)),
            pltpu.SemaphoreType.DMA((devices,)),
            pltpu.SemaphoreType.DMA,
        ],
        compiler_params=pltpu.CompilerParams(collective_id=collective, has_side_effects=True),
    )(x)


def expert_body(depth_steps, seg_ref, gate_ref, up_ref, down_ref, o_ref, gate_acc, up_acc, active):
    step = pl.program_id(0)

    @pl.when(step == 0)
    def _():
        gate_acc[...] = jnp.zeros_like(gate_acc)
        up_acc[...] = jnp.zeros_like(up_acc)

    @pl.when(step < depth_steps)
    def _():
        joined = jnp.concatenate([gate_ref[...], up_ref[...]], axis=1)
        both = jnp.dot(seg_ref[...], joined, preferred_element_type=jnp.float32)
        hidden = gate_acc.shape[1]
        gate_acc[...] += both[:, :hidden]
        up_acc[...] += both[:, hidden:]

    @pl.when(step == depth_steps - 1)
    def _():
        gate = gate_acc[...]
        active[...] = (gate / (1.0 + jnp.exp(-gate)) * up_acc[...]).astype(active.dtype)

    @pl.when(step >= depth_steps)
    def _():
        o_ref[...] = jnp.dot(
            active[...], down_ref[...], preferred_element_type=jnp.float32
        ).astype(o_ref.dtype)


def expert_mlp(segment, gate_w, up_w, down_w):
    rows, width = segment.shape
    hidden = gate_w.shape[1]
    block = 2048
    depth_steps = width // block
    column_steps = width // block
    return pl.pallas_call(
        functools.partial(expert_body, depth_steps),
        grid=(depth_steps + column_steps,),
        in_specs=[
            pl.BlockSpec((rows, block), lambda i: (0, jnp.minimum(i, depth_steps - 1))),
            pl.BlockSpec((block, hidden), lambda i: (jnp.minimum(i, depth_steps - 1), 0)),
            pl.BlockSpec((block, hidden), lambda i: (jnp.minimum(i, depth_steps - 1), 0)),
            pl.BlockSpec((hidden, block), lambda i: (0, jnp.maximum(i - depth_steps, 0))),
        ],
        out_specs=pl.BlockSpec((rows, block), lambda i: (0, jnp.maximum(i - depth_steps, 0))),
        out_shape=jax.ShapeDtypeStruct((rows, width), jnp.bfloat16),
        scratch_shapes=[
            pltpu.VMEM((rows, hidden), jnp.float32),
            pltpu.VMEM((rows, hidden), jnp.float32),
            pltpu.VMEM((rows, hidden), jnp.bfloat16),
        ],
        cost_estimate=pl.CostEstimate(
            flops=6 * rows * width * hidden,
            transcendentals=rows * hidden,
            bytes_accessed=2 * (2 * rows * width + 3 * width * hidden),
        ),
    )(segment, gate_w, up_w, down_w)


def scan_rounds(devices):
    rounds, base = [], 1
    while base < devices:
        rounds.append([j * base for j in range(1, 4) if j * base < devices])
        base *= 4
    return rounds


def fold(earlier_state, earlier_log, later_state, later_log):
    decay = jnp.exp(later_log[:, 0:1, :])
    return decay * earlier_state + later_state, earlier_log + later_log


def scan_body(devices, x_state, x_log, o_state, o_log, inc_state, inc_log, wire, recv, send_sem, recv_sem):
    me = lax.axis_index("seq")
    col = lax.axis_index("exp")
    rows = x_state.shape[1]
    mesh_id = pl.DeviceIdType.MESH
    barrier = pltpu.get_barrier_semaphore()
    for step in range(1, devices):
        peer = lax.rem(me + step, devices)
        pl.semaphore_signal(barrier, 1, device_id=(peer, col), device_id_type=mesh_id)
    pl.semaphore_wait(barrier, devices - 1)
    inc_state[0] = x_state[...]
    inc_log[0] = x_log[...]
    o_state[...] = jnp.zeros_like(o_state)
    o_log[...] = jnp.zeros_like(o_log)
    for level, shifts in enumerate(scan_rounds(devices)):
        log_now = inc_log[level]
        high = log_now.astype(jnp.bfloat16).astype(jnp.float32)
        wire[level, :, :rows, :] = inc_state[level].astype(jnp.bfloat16)
        wire[level, :, rows:, :] = jnp.concatenate([high, log_now - high], axis=1).astype(jnp.bfloat16)

        def link(slot, peer):
            return pltpu.make_async_remote_copy(
                src_ref=wire.at[level],
                dst_ref=recv.at[level, slot],
                send_sem=send_sem.at[level, slot],
                recv_sem=recv_sem.at[level, slot],
                device_id=(peer, col),
                device_id_type=mesh_id,
            )
        for slot, shift in enumerate(shifts):
            @pl.when(me + shift < devices)
            def _():
                link(slot, me + shift).start()
        inc_state[level + 1] = inc_state[level]
        inc_log[level + 1] = inc_log[level]
        for slot, shift in enumerate(shifts):
            @pl.when(me >= shift)
            def _():
                link(slot, me - shift).wait_recv()
                got_state = recv[level, slot, :, :rows, :].astype(jnp.float32)
                parts = recv[level, slot, :, rows:, :].astype(jnp.float32)
                got_log = parts[:, :8, :] + parts[:, 8:, :]
                new_state, new_log = fold(got_state, got_log, inc_state[level + 1], inc_log[level + 1])
                inc_state[level + 1] = new_state
                inc_log[level + 1] = new_log
                new_state, new_log = fold(got_state, got_log, o_state[...], o_log[...])
                o_state[...] = new_state
                o_log[...] = new_log
        for slot, shift in enumerate(shifts):
            @pl.when(me + shift < devices)
            def _():
                link(slot, me + shift).wait_send()


def exclusive_scan(log, state, axis):
    devices = lax.axis_size(axis)
    heads, state_rows, lanes = state.shape
    log_rows = jnp.broadcast_to(log[:, None, None], (heads, 8, lanes))
    levels = len(scan_rounds(devices))
    wire_shape = (heads, state_rows + 16, lanes)
    prior_state, prior_log = pl.pallas_call(
        functools.partial(scan_body, devices),
        out_shape=(
            jax.ShapeDtypeStruct(state.shape, jnp.float32),
            jax.ShapeDtypeStruct(log_rows.shape, jnp.float32),
        ),
        in_specs=[pl.BlockSpec(memory_space=pltpu.VMEM)] * 2,
        out_specs=(pl.BlockSpec(memory_space=pltpu.VMEM),) * 2,
        scratch_shapes=[
            pltpu.VMEM((levels + 1,) + state.shape, jnp.float32),
            pltpu.VMEM((levels + 1,) + log_rows.shape, jnp.float32),
            pltpu.VMEM((levels,) + wire_shape, jnp.bfloat16),
            pltpu.VMEM((levels, 3) + wire_shape, jnp.bfloat16),
            pltpu.SemaphoreType.DMA((levels, 3)),
            pltpu.SemaphoreType.DMA((levels, 3)),
        ],
        compiler_params=pltpu.CompilerParams(collective_id=3, has_side_effects=True),
    )(state, log_rows)
    return prior_log[:, 0, 0], prior_state


def chain_combine(earlier, later):
    return (earlier[0] + later[0], jnp.exp(later[0])[:, None, None] * earlier[1] + later[1])


def on_device(
    x_in,
    z_gate,
    b_in,
    c_out,
    dt_step,
    rate,
    skip,
    init_state,
    residual,
    norm_gain,
    expert_ids,
    gate_weights,
    w_gate,
    w_up,
    w_down,
):
    token_count, channels = x_in.shape
    heads_here = rate.shape[0]
    head_width = channels // heads_here
    state_width = b_in.shape[1]
    blocks = token_count // GROUP
    inputs = x_in.astype(jnp.float32).reshape(blocks, GROUP, heads_here, head_width)
    keys_in = b_in.astype(jnp.float32).reshape(blocks, GROUP, state_width)
    queries = c_out.astype(jnp.float32).reshape(blocks, GROUP, state_width)
    log_steps = (-rate[None, :] * dt_step).reshape(blocks, GROUP, heads_here)
    cumulative = jnp.cumsum(log_steps, axis=1)
    scores = jnp.einsum("ctn,csn->cts", queries, keys_in, precision=PRECISE)
    causal = jnp.arange(GROUP)[:, None] >= jnp.arange(GROUP)[None, :]
    spread = cumulative[:, :, None, :] - cumulative[:, None, :, :]
    weights = jnp.exp(jnp.where(causal[None, :, :, None], spread, -jnp.inf)) * scores[..., None]
    intra_out = jnp.einsum("ctsh,cshp->cthp", weights, inputs, precision=PRECISE)
    tail_decay = jnp.exp(cumulative[:, -1:, :] - cumulative)
    block_state = jnp.einsum("csh,cshp,csn->chpn", tail_decay, inputs, keys_in, precision=PRECISE)
    block_log = cumulative[:, -1, :]

    def advance(carried, element):
        total_log, total_state = carried
        step_log, step_state = element
        updated = (
            total_log + step_log,
            jnp.exp(step_log)[:, None, None] * total_state + step_state,
        )
        return (updated, (total_log, total_state))

    zero_state = jnp.zeros((heads_here, head_width, state_width), jnp.float32)
    zero_log = jnp.zeros((heads_here,), jnp.float32)
    (device_log, device_state), (enter_log, enter_state) = lax.scan(
        advance, (zero_log, zero_state), (block_log, block_state)
    )
    prior_log, prior_state = exclusive_scan(device_log, device_state, "seq")
    incoming = prior_state + jnp.exp(prior_log)[:, None, None] * init_state
    entering = enter_state + jnp.exp(enter_log)[:, :, None, None] * incoming[None]
    inter_out = jnp.exp(cumulative)[..., None] * jnp.einsum(
        "chpn,ctn->cthp", entering, queries, precision=PRECISE
    )
    mixed_out = (intra_out + inter_out + skip[None, None, :, None] * inputs).reshape(
        token_count, channels
    )
    mixer = (mixed_out * jax.nn.silu(z_gate.astype(jnp.float32))).astype(jnp.bfloat16)
    owners = lax.axis_size("exp")
    rows_here = residual.shape[0]
    arrived_mix = exchange(mixer.reshape(owners, rows_here, channels), 0)
    token_mix = arrived_mix.transpose(1, 0, 2).reshape(rows_here, owners * channels)
    stream = (residual.astype(jnp.float32) + token_mix.astype(jnp.float32)).astype(jnp.bfloat16)
    widened = stream.astype(jnp.float32)
    normed = (
        widened
        * lax.rsqrt(jnp.mean(widened * widened, axis=-1, keepdims=True) + 1e-06)
        * norm_gain[None, :]
    ).astype(jnp.bfloat16)
    local_experts = w_gate.shape[0]
    experts = owners * local_experts
    capacity = max(2, 2 * rows_here // experts + 1)
    width = residual.shape[1]
    chosen = expert_ids.reshape(-1)
    onehot = (chosen[:, None] == jnp.arange(experts)[None, :]).astype(jnp.int32)
    slot_index = jnp.sum((jnp.cumsum(onehot, axis=0) - onehot) * onehot, axis=1)
    target = chosen * capacity + slot_index
    placing = (target[None, :] == jnp.arange(experts * capacity)[:, None]).astype(jnp.bfloat16)
    pair_rows = jnp.repeat(normed, 2, axis=0)
    outgoing = jnp.dot(placing, pair_rows, preferred_element_type=jnp.float32).astype(jnp.bfloat16)
    block = capacity * width // 16
    arrived = exchange(outgoing.reshape(experts, 16, block), 1)
    arrived = arrived.reshape(capacity * experts, width)
    segment = lax.all_gather(arrived, "seq", axis=0, tiled=True)
    partial_value = expert_mlp(segment, w_gate[0], w_up[0], w_down[0])
    summed = lax.psum_scatter(partial_value, "seq", scatter_dimension=0, tiled=True)
    returned = exchange(summed.reshape(experts, 16, block), 2)
    results = returned.reshape(experts * capacity, width)
    picked = results[target].astype(jnp.float32).reshape(rows_here, 2, width)
    mixture = jnp.sum(picked * gate_weights[:, :, None], axis=1)
    return (widened + mixture).astype(jnp.bfloat16)


def solution(mesh):
    return jax.shard_map(
        on_device,
        mesh=mesh,
        in_specs=(
            P("seq", "exp"),
            P("seq", "exp"),
            P("seq", None),
            P("seq", None),
            P("seq", "exp"),
            P("exp"),
            P("exp"),
            P("exp", None, None),
            P(("seq", "exp"), None),
            P(),
            P(("seq", "exp"), None),
            P(("seq", "exp"), None),
            P("exp", None, "seq"),
            P("exp", None, "seq"),
            P("exp", "seq", None),
        ),
        out_specs=P(("seq", "exp"), None),
        check_vma=False,
    )
```

```python
import functools

import jax
import jax.numpy as jnp
from jax import lax
from jax.sharding import PartitionSpec as P
from jax.experimental import pallas as pl
from jax.experimental.pallas import tpu as pltpu

GROUP = 128


PRECISE = lax.Precision.HIGHEST


def exchange_body(x_ref, o_ref, send_sem, recv_sem, local_sem):
    devices = x_ref.shape[0]
    me = lax.axis_index("exp")
    row = lax.axis_index("seq")
    mesh_id = pl.DeviceIdType.MESH
    barrier = pltpu.get_barrier_semaphore()
    for step in range(1, devices):
        peer = lax.rem(me + step, devices)
        pl.semaphore_signal(barrier, 1, device_id=(row, peer), device_id_type=mesh_id)
    pl.semaphore_wait(barrier, devices - 1)
    local = pltpu.make_async_copy(x_ref.at[me], o_ref.at[me], local_sem)
    local.start()
    copies = []
    for step in range(1, devices):
        peer = lax.rem(me + step, devices)
        copy = pltpu.make_async_remote_copy(
            src_ref=x_ref.at[peer],
            dst_ref=o_ref.at[me],
            send_sem=send_sem.at[step],
            recv_sem=recv_sem.at[step],
            device_id=(row, peer),
            device_id_type=mesh_id,
        )
        copy.start()
        copies.append(copy)
    local.wait()
    for copy in copies:
        copy.wait()


def exchange(x, collective):
    devices = x.shape[0]
    return pl.pallas_call(
        exchange_body,
        out_shape=jax.ShapeDtypeStruct(x.shape, x.dtype),
        in_specs=[pl.BlockSpec(memory_space=pltpu.VMEM)],
        out_specs=pl.BlockSpec(memory_space=pltpu.VMEM),
        scratch_shapes=[
            pltpu.SemaphoreType.DMA((devices,)),
            pltpu.SemaphoreType.DMA((devices,)),
            pltpu.SemaphoreType.DMA,
        ],
        compiler_params=pltpu.CompilerParams(collective_id=collective, has_side_effects=True),
    )(x)


def expert_body(depth_steps, seg_ref, gate_ref, up_ref, down_ref, o_ref, gate_acc, up_acc, active):
    step = pl.program_id(0)

    @pl.when(step == 0)
    def _():
        gate_acc[...] = jnp.zeros_like(gate_acc)
        up_acc[...] = jnp.zeros_like(up_acc)

    @pl.when(step < depth_steps)
    def _():
        joined = jnp.concatenate([gate_ref[...], up_ref[...]], axis=1)
        both = jnp.dot(seg_ref[...], joined, preferred_element_type=jnp.float32)
        hidden = gate_acc.shape[1]
        gate_acc[...] += both[:, :hidden]
        up_acc[...] += both[:, hidden:]

    @pl.when(step == depth_steps - 1)
    def _():
        gate = gate_acc[...]
        active[...] = (gate / (1.0 + jnp.exp(-gate)) * up_acc[...]).astype(active.dtype)

    @pl.when(step >= depth_steps)
    def _():
        o_ref[...] = jnp.dot(
            active[...], down_ref[...], preferred_element_type=jnp.float32
        ).astype(o_ref.dtype)


def expert_mlp(segment, gate_w, up_w, down_w):
    rows, width = segment.shape
    hidden = gate_w.shape[1]
    block = 4096
    columns = 2048
    depth_steps = width // block
    column_steps = width // columns
    return pl.pallas_call(
        functools.partial(expert_body, depth_steps),
        grid=(depth_steps + column_steps,),
        in_specs=[
            pl.BlockSpec((rows, block), lambda i: (0, jnp.minimum(i, depth_steps - 1))),
            pl.BlockSpec((block, hidden), lambda i: (jnp.minimum(i, depth_steps - 1), 0)),
            pl.BlockSpec((block, hidden), lambda i: (jnp.minimum(i, depth_steps - 1), 0)),
            pl.BlockSpec((hidden, columns), lambda i: (0, jnp.maximum(i - depth_steps, 0))),
        ],
        out_specs=pl.BlockSpec((rows, columns), lambda i: (0, jnp.maximum(i - depth_steps, 0))),
        out_shape=jax.ShapeDtypeStruct((rows, width), jnp.bfloat16),
        scratch_shapes=[
            pltpu.VMEM((rows, hidden), jnp.float32),
            pltpu.VMEM((rows, hidden), jnp.float32),
            pltpu.VMEM((rows, hidden), jnp.bfloat16),
        ],
        cost_estimate=pl.CostEstimate(
            flops=6 * rows * width * hidden,
            transcendentals=rows * hidden,
            bytes_accessed=2 * (2 * rows * width + 3 * width * hidden),
        ),
    )(segment, gate_w, up_w, down_w)


def scan_rounds(devices):
    rounds, base = [], 1
    while base < devices:
        rounds.append([j * base for j in range(1, 4) if j * base < devices])
        base *= 4
    return rounds


def fold(earlier_state, earlier_log, later_state, later_log):
    decay = jnp.exp(later_log[:, 0:1, :])
    return decay * earlier_state + later_state, earlier_log + later_log


def scan_body(devices, x_state, x_log, o_state, o_log, inc_state, inc_log, wire, recv, send_sem, recv_sem):
    me = lax.axis_index("seq")
    col = lax.axis_index("exp")
    rows = x_state.shape[1]
    mesh_id = pl.DeviceIdType.MESH
    barrier = pltpu.get_barrier_semaphore()
    for step in range(1, devices):
        peer = lax.rem(me + step, devices)
        pl.semaphore_signal(barrier, 1, device_id=(peer, col), device_id_type=mesh_id)
    pl.semaphore_wait(barrier, devices - 1)
    inc_state[0] = x_state[...]
    inc_log[0] = x_log[...]
    o_state[...] = jnp.zeros_like(o_state)
    o_log[...] = jnp.zeros_like(o_log)
    for level, shifts in enumerate(scan_rounds(devices)):
        log_now = inc_log[level]
        high = log_now.astype(jnp.bfloat16).astype(jnp.float32)
        wire[level, :, :rows, :] = inc_state[level].astype(jnp.bfloat16)
        wire[level, :, rows:, :] = jnp.concatenate([high, log_now - high], axis=1).astype(jnp.bfloat16)

        def link(slot, peer):
            return pltpu.make_async_remote_copy(
                src_ref=wire.at[level],
                dst_ref=recv.at[level, slot],
                send_sem=send_sem.at[level, slot],
                recv_sem=recv_sem.at[level, slot],
                device_id=(peer, col),
                device_id_type=mesh_id,
            )
        for slot, shift in enumerate(shifts):
            @pl.when(me + shift < devices)
            def _():
                link(slot, me + shift).start()
        inc_state[level + 1] = inc_state[level]
        inc_log[level + 1] = inc_log[level]
        for slot, shift in enumerate(shifts):
            @pl.when(me >= shift)
            def _():
                link(slot, me - shift).wait_recv()
                got_state = recv[level, slot, :, :rows, :].astype(jnp.float32)
                parts = recv[level, slot, :, rows:, :].astype(jnp.float32)
                got_log = parts[:, :8, :] + parts[:, 8:, :]
                new_state, new_log = fold(got_state, got_log, inc_state[level + 1], inc_log[level + 1])
                inc_state[level + 1] = new_state
                inc_log[level + 1] = new_log
                new_state, new_log = fold(got_state, got_log, o_state[...], o_log[...])
                o_state[...] = new_state
                o_log[...] = new_log
        for slot, shift in enumerate(shifts):
            @pl.when(me + shift < devices)
            def _():
                link(slot, me + shift).wait_send()


def exclusive_scan(log, state, axis):
    devices = lax.axis_size(axis)
    heads, state_rows, lanes = state.shape
    log_rows = jnp.broadcast_to(log[:, None, None], (heads, 8, lanes))
    levels = len(scan_rounds(devices))
    wire_shape = (heads, state_rows + 16, lanes)
    prior_state, prior_log = pl.pallas_call(
        functools.partial(scan_body, devices),
        out_shape=(
            jax.ShapeDtypeStruct(state.shape, jnp.float32),
            jax.ShapeDtypeStruct(log_rows.shape, jnp.float32),
        ),
        in_specs=[pl.BlockSpec(memory_space=pltpu.VMEM)] * 2,
        out_specs=(pl.BlockSpec(memory_space=pltpu.VMEM),) * 2,
        scratch_shapes=[
            pltpu.VMEM((levels + 1,) + state.shape, jnp.float32),
            pltpu.VMEM((levels + 1,) + log_rows.shape, jnp.float32),
            pltpu.VMEM((levels,) + wire_shape, jnp.bfloat16),
            pltpu.VMEM((levels, 3) + wire_shape, jnp.bfloat16),
            pltpu.SemaphoreType.DMA((levels, 3)),
            pltpu.SemaphoreType.DMA((levels, 3)),
        ],
        compiler_params=pltpu.CompilerParams(collective_id=3, has_side_effects=True),
    )(state, log_rows)
    return prior_log[:, 0, 0], prior_state


def chain_combine(earlier, later):
    return (earlier[0] + later[0], jnp.exp(later[0])[:, None, None] * earlier[1] + later[1])


def on_device(
    x_in,
    z_gate,
    b_in,
    c_out,
    dt_step,
    rate,
    skip,
    init_state,
    residual,
    norm_gain,
    expert_ids,
    gate_weights,
    w_gate,
    w_up,
    w_down,
):
    token_count, channels = x_in.shape
    heads_here = rate.shape[0]
    head_width = channels // heads_here
    state_width = b_in.shape[1]
    blocks = token_count // GROUP
    inputs = x_in.astype(jnp.float32).reshape(blocks, GROUP, heads_here, head_width)
    keys_in = b_in.astype(jnp.float32).reshape(blocks, GROUP, state_width)
    queries = c_out.astype(jnp.float32).reshape(blocks, GROUP, state_width)
    log_steps = (-rate[None, :] * dt_step).reshape(blocks, GROUP, heads_here)
    cumulative = jnp.cumsum(log_steps, axis=1)
    scores = jnp.einsum("ctn,csn->cts", queries, keys_in, precision=PRECISE)
    causal = jnp.arange(GROUP)[:, None] >= jnp.arange(GROUP)[None, :]
    spread = cumulative[:, :, None, :] - cumulative[:, None, :, :]
    weights = jnp.exp(jnp.where(causal[None, :, :, None], spread, -jnp.inf)) * scores[..., None]
    intra_out = jnp.einsum("ctsh,cshp->cthp", weights, inputs, precision=PRECISE)
    tail_decay = jnp.exp(cumulative[:, -1:, :] - cumulative)
    block_state = jnp.einsum("csh,cshp,csn->chpn", tail_decay, inputs, keys_in, precision=PRECISE)
    block_log = cumulative[:, -1, :]

    def advance(carried, element):
        total_log, total_state = carried
        step_log, step_state = element
        updated = (
            total_log + step_log,
            jnp.exp(step_log)[:, None, None] * total_state + step_state,
        )
        return (updated, (total_log, total_state))

    zero_state = jnp.zeros((heads_here, head_width, state_width), jnp.float32)
    zero_log = jnp.zeros((heads_here,), jnp.float32)
    (device_log, device_state), (enter_log, enter_state) = lax.scan(
        advance, (zero_log, zero_state), (block_log, block_state)
    )
    prior_log, prior_state = exclusive_scan(device_log, device_state, "seq")
    incoming = prior_state + jnp.exp(prior_log)[:, None, None] * init_state
    entering = enter_state + jnp.exp(enter_log)[:, :, None, None] * incoming[None]
    inter_out = jnp.exp(cumulative)[..., None] * jnp.einsum(
        "chpn,ctn->cthp", entering, queries, precision=PRECISE
    )
    mixed_out = (intra_out + inter_out + skip[None, None, :, None] * inputs).reshape(
        token_count, channels
    )
    mixer = (mixed_out * jax.nn.silu(z_gate.astype(jnp.float32))).astype(jnp.bfloat16)
    owners = lax.axis_size("exp")
    rows_here = residual.shape[0]
    arrived_mix = exchange(mixer.reshape(owners, rows_here, channels), 0)
    token_mix = arrived_mix.transpose(1, 0, 2).reshape(rows_here, owners * channels)
    stream = (residual.astype(jnp.float32) + token_mix.astype(jnp.float32)).astype(jnp.bfloat16)
    widened = stream.astype(jnp.float32)
    normed = (
        widened
        * lax.rsqrt(jnp.mean(widened * widened, axis=-1, keepdims=True) + 1e-06)
        * norm_gain[None, :]
    ).astype(jnp.bfloat16)
    local_experts = w_gate.shape[0]
    experts = owners * local_experts
    capacity = max(2, 2 * rows_here // experts + 1)
    width = residual.shape[1]
    chosen = expert_ids.reshape(-1)
    onehot = (chosen[:, None] == jnp.arange(experts)[None, :]).astype(jnp.int32)
    slot_index = jnp.sum((jnp.cumsum(onehot, axis=0) - onehot) * onehot, axis=1)
    target = chosen * capacity + slot_index
    placing = (target[None, :] == jnp.arange(experts * capacity)[:, None]).astype(jnp.bfloat16)
    pair_rows = jnp.repeat(normed, 2, axis=0)
    outgoing = jnp.dot(placing, pair_rows, preferred_element_type=jnp.float32).astype(jnp.bfloat16)
    block = capacity * width // 16
    arrived = exchange(outgoing.reshape(experts, 16, block), 1)
    arrived = arrived.reshape(capacity * experts, width)
    segment = lax.all_gather(arrived, "seq", axis=0, tiled=True)
    partial_value = expert_mlp(segment, w_gate[0], w_up[0], w_down[0])
    summed = lax.psum_scatter(partial_value, "seq", scatter_dimension=0, tiled=True)
    returned = exchange(summed.reshape(experts, 16, block), 2)
    results = returned.reshape(experts * capacity, width)
    picked = results[target].astype(jnp.float32).reshape(rows_here, 2, width)
    mixture = jnp.sum(picked * gate_weights[:, :, None], axis=1)
    return (widened + mixture).astype(jnp.bfloat16)


def solution(mesh):
    return jax.shard_map(
        on_device,
        mesh=mesh,
        in_specs=(
            P("seq", "exp"),
            P("seq", "exp"),
            P("seq", None),
            P("seq", None),
            P("seq", "exp"),
            P("exp"),
            P("exp"),
            P("exp", None, None),
            P(("seq", "exp"), None),
            P(),
            P(("seq", "exp"), None),
            P(("seq", "exp"), None),
            P("exp", None, "seq"),
            P("exp", None, "seq"),
            P("exp", "seq", None),
        ),
        out_specs=P(("seq", "exp"), None),
        check_vma=False,
    )
```

```python
import functools

import jax
import jax.numpy as jnp
from jax import lax
from jax.sharding import PartitionSpec as P
from jax.experimental import pallas as pl
from jax.experimental.pallas import tpu as pltpu

GROUP = 128


PRECISE = lax.Precision.HIGHEST


def exchange_body(x_ref, o_ref, send_sem, recv_sem, local_sem):
    devices = x_ref.shape[0]
    me = lax.axis_index("exp")
    row = lax.axis_index("seq")
    mesh_id = pl.DeviceIdType.MESH
    barrier = pltpu.get_barrier_semaphore()
    for step in range(1, devices):
        peer = lax.rem(me + step, devices)
        pl.semaphore_signal(barrier, 1, device_id=(row, peer), device_id_type=mesh_id)
    local = pltpu.make_async_copy(x_ref.at[me], o_ref.at[me], local_sem)
    local.start()
    pl.semaphore_wait(barrier, devices - 1)
    copies = []
    order = sorted(range(1, devices), key=lambda step: -min(step, devices - step))
    for step in order:
        peer = lax.rem(me + step, devices)
        copy = pltpu.make_async_remote_copy(
            src_ref=x_ref.at[peer],
            dst_ref=o_ref.at[me],
            send_sem=send_sem.at[step],
            recv_sem=recv_sem.at[step],
            device_id=(row, peer),
            device_id_type=mesh_id,
        )
        copy.start()
        copies.append(copy)
    local.wait()
    for copy in copies:
        copy.wait()


def exchange(x, collective):
    devices = x.shape[0]
    return pl.pallas_call(
        exchange_body,
        out_shape=jax.ShapeDtypeStruct(x.shape, x.dtype),
        in_specs=[pl.BlockSpec(memory_space=pltpu.VMEM)],
        out_specs=pl.BlockSpec(memory_space=pltpu.VMEM),
        scratch_shapes=[
            pltpu.SemaphoreType.DMA((devices,)),
            pltpu.SemaphoreType.DMA((devices,)),
            pltpu.SemaphoreType.DMA,
        ],
        compiler_params=pltpu.CompilerParams(collective_id=collective, has_side_effects=True),
    )(x)


def expert_body(depth_steps, seg_ref, gate_ref, up_ref, down_ref, o_ref, gate_acc, up_acc, active):
    step = pl.program_id(0)

    @pl.when(step == 0)
    def _():
        gate_acc[...] = jnp.zeros_like(gate_acc)
        up_acc[...] = jnp.zeros_like(up_acc)

    @pl.when(step < depth_steps)
    def _():
        joined = jnp.concatenate([gate_ref[...], up_ref[...]], axis=1)
        both = jnp.dot(seg_ref[...], joined, preferred_element_type=jnp.float32)
        hidden = gate_acc.shape[1]
        gate_acc[...] += both[:, :hidden]
        up_acc[...] += both[:, hidden:]

    @pl.when(step == depth_steps - 1)
    def _():
        gate = gate_acc[...]
        active[...] = (gate / (1.0 + jnp.exp(-gate)) * up_acc[...]).astype(active.dtype)

    @pl.when(step >= depth_steps)
    def _():
        o_ref[...] = jnp.dot(
            active[...], down_ref[...], preferred_element_type=jnp.float32
        ).astype(o_ref.dtype)


def expert_mlp(segment, gate_w, up_w, down_w):
    rows, width = segment.shape
    hidden = gate_w.shape[1]
    block = 4096
    columns = 2048
    depth_steps = width // block
    column_steps = width // columns
    return pl.pallas_call(
        functools.partial(expert_body, depth_steps),
        grid=(depth_steps + column_steps,),
        in_specs=[
            pl.BlockSpec((rows, block), lambda i: (0, jnp.minimum(i, depth_steps - 1))),
            pl.BlockSpec((block, hidden), lambda i: (jnp.minimum(i, depth_steps - 1), 0)),
            pl.BlockSpec((block, hidden), lambda i: (jnp.minimum(i, depth_steps - 1), 0)),
            pl.BlockSpec((hidden, columns), lambda i: (0, jnp.maximum(i - depth_steps, 0))),
        ],
        out_specs=pl.BlockSpec((rows, columns), lambda i: (0, jnp.maximum(i - depth_steps, 0))),
        out_shape=jax.ShapeDtypeStruct((rows, width), jnp.bfloat16),
        scratch_shapes=[
            pltpu.VMEM((rows, hidden), jnp.float32),
            pltpu.VMEM((rows, hidden), jnp.float32),
            pltpu.VMEM((rows, hidden), jnp.bfloat16),
        ],
        cost_estimate=pl.CostEstimate(
            flops=6 * rows * width * hidden,
            transcendentals=rows * hidden,
            bytes_accessed=2 * (2 * rows * width + 3 * width * hidden),
        ),
    )(segment, gate_w, up_w, down_w)


def scan_rounds(devices):
    rounds, base = [], 1
    while base < devices:
        rounds.append([j * base for j in range(1, 4) if j * base < devices])
        base *= 4
    return rounds


def fold(earlier_state, earlier_log, later_state, later_log):
    decay = jnp.exp(later_log[:, 0:1, :])
    return decay * earlier_state + later_state, earlier_log + later_log


def scan_body(devices, x_state, x_log, o_state, o_log, inc_state, inc_log, wire, recv, send_sem, recv_sem):
    me = lax.axis_index("seq")
    col = lax.axis_index("exp")
    rows = x_state.shape[1]
    mesh_id = pl.DeviceIdType.MESH
    barrier = pltpu.get_barrier_semaphore()
    for step in range(1, devices):
        peer = lax.rem(me + step, devices)
        pl.semaphore_signal(barrier, 1, device_id=(peer, col), device_id_type=mesh_id)
    pl.semaphore_wait(barrier, devices - 1)
    inc_state[0] = x_state[...]
    inc_log[0] = x_log[...]
    o_state[...] = jnp.zeros_like(o_state)
    o_log[...] = jnp.zeros_like(o_log)
    for level, shifts in enumerate(scan_rounds(devices)):
        log_now = inc_log[level]
        high = log_now.astype(jnp.bfloat16).astype(jnp.float32)
        wire[level, :, :rows, :] = inc_state[level].astype(jnp.bfloat16)
        wire[level, :, rows:, :] = jnp.concatenate([high, log_now - high], axis=1).astype(jnp.bfloat16)

        def link(slot, peer):
            return pltpu.make_async_remote_copy(
                src_ref=wire.at[level],
                dst_ref=recv.at[level, slot],
                send_sem=send_sem.at[level, slot],
                recv_sem=recv_sem.at[level, slot],
                device_id=(peer, col),
                device_id_type=mesh_id,
            )
        for slot, shift in enumerate(shifts):
            @pl.when(me + shift < devices)
            def _():
                link(slot, me + shift).start()
        inc_state[level + 1] = inc_state[level]
        inc_log[level + 1] = inc_log[level]
        for slot, shift in enumerate(shifts):
            @pl.when(me >= shift)
            def _():
                link(slot, me - shift).wait_recv()
                got_state = recv[level, slot, :, :rows, :].astype(jnp.float32)
                parts = recv[level, slot, :, rows:, :].astype(jnp.float32)
                got_log = parts[:, :8, :] + parts[:, 8:, :]
                new_state, new_log = fold(got_state, got_log, inc_state[level + 1], inc_log[level + 1])
                inc_state[level + 1] = new_state
                inc_log[level + 1] = new_log
                new_state, new_log = fold(got_state, got_log, o_state[...], o_log[...])
                o_state[...] = new_state
                o_log[...] = new_log
        for slot, shift in enumerate(shifts):
            @pl.when(me + shift < devices)
            def _():
                link(slot, me + shift).wait_send()


def exclusive_scan(log, state, axis):
    devices = lax.axis_size(axis)
    heads, state_rows, lanes = state.shape
    log_rows = jnp.broadcast_to(log[:, None, None], (heads, 8, lanes))
    levels = len(scan_rounds(devices))
    wire_shape = (heads, state_rows + 16, lanes)
    prior_state, prior_log = pl.pallas_call(
        functools.partial(scan_body, devices),
        out_shape=(
            jax.ShapeDtypeStruct(state.shape, jnp.float32),
            jax.ShapeDtypeStruct(log_rows.shape, jnp.float32),
        ),
        in_specs=[pl.BlockSpec(memory_space=pltpu.VMEM)] * 2,
        out_specs=(pl.BlockSpec(memory_space=pltpu.VMEM),) * 2,
        scratch_shapes=[
            pltpu.VMEM((levels + 1,) + state.shape, jnp.float32),
            pltpu.VMEM((levels + 1,) + log_rows.shape, jnp.float32),
            pltpu.VMEM((levels,) + wire_shape, jnp.bfloat16),
            pltpu.VMEM((levels, 3) + wire_shape, jnp.bfloat16),
            pltpu.SemaphoreType.DMA((levels, 3)),
            pltpu.SemaphoreType.DMA((levels, 3)),
        ],
        compiler_params=pltpu.CompilerParams(collective_id=3, has_side_effects=True),
    )(state, log_rows)
    return prior_log[:, 0, 0], prior_state


def chain_combine(earlier, later):
    return (earlier[0] + later[0], jnp.exp(later[0])[:, None, None] * earlier[1] + later[1])


def on_device(
    x_in,
    z_gate,
    b_in,
    c_out,
    dt_step,
    rate,
    skip,
    init_state,
    residual,
    norm_gain,
    expert_ids,
    gate_weights,
    w_gate,
    w_up,
    w_down,
):
    token_count, channels = x_in.shape
    heads_here = rate.shape[0]
    head_width = channels // heads_here
    state_width = b_in.shape[1]
    blocks = token_count // GROUP
    inputs = x_in.astype(jnp.float32).reshape(blocks, GROUP, heads_here, head_width)
    keys_in = b_in.astype(jnp.float32).reshape(blocks, GROUP, state_width)
    queries = c_out.astype(jnp.float32).reshape(blocks, GROUP, state_width)
    log_steps = (-rate[None, :] * dt_step).reshape(blocks, GROUP, heads_here)
    cumulative = jnp.cumsum(log_steps, axis=1)
    scores = jnp.einsum("ctn,csn->cts", queries, keys_in, precision=PRECISE)
    causal = jnp.arange(GROUP)[:, None] >= jnp.arange(GROUP)[None, :]
    spread = cumulative[:, :, None, :] - cumulative[:, None, :, :]
    weights = jnp.exp(jnp.where(causal[None, :, :, None], spread, -jnp.inf)) * scores[..., None]
    intra_out = jnp.einsum("ctsh,cshp->cthp", weights, inputs, precision=PRECISE)
    tail_decay = jnp.exp(cumulative[:, -1:, :] - cumulative)
    block_state = jnp.einsum("csh,cshp,csn->chpn", tail_decay, inputs, keys_in, precision=PRECISE)
    block_log = cumulative[:, -1, :]

    def advance(carried, element):
        total_log, total_state = carried
        step_log, step_state = element
        updated = (
            total_log + step_log,
            jnp.exp(step_log)[:, None, None] * total_state + step_state,
        )
        return (updated, (total_log, total_state))

    zero_state = jnp.zeros((heads_here, head_width, state_width), jnp.float32)
    zero_log = jnp.zeros((heads_here,), jnp.float32)
    (device_log, device_state), (enter_log, enter_state) = lax.scan(
        advance, (zero_log, zero_state), (block_log, block_state)
    )
    prior_log, prior_state = exclusive_scan(device_log, device_state, "seq")
    incoming = prior_state + jnp.exp(prior_log)[:, None, None] * init_state
    entering = enter_state + jnp.exp(enter_log)[:, :, None, None] * incoming[None]
    inter_out = jnp.exp(cumulative)[..., None] * jnp.einsum(
        "chpn,ctn->cthp", entering, queries, precision=PRECISE
    )
    mixed_out = (intra_out + inter_out + skip[None, None, :, None] * inputs).reshape(
        token_count, channels
    )
    mixer = (mixed_out * jax.nn.silu(z_gate.astype(jnp.float32))).astype(jnp.bfloat16)
    owners = lax.axis_size("exp")
    rows_here = residual.shape[0]
    arrived_mix = exchange(mixer.reshape(owners, rows_here, channels), 0)
    token_mix = arrived_mix.transpose(1, 0, 2).reshape(rows_here, owners * channels)
    stream = (residual.astype(jnp.float32) + token_mix.astype(jnp.float32)).astype(jnp.bfloat16)
    widened = stream.astype(jnp.float32)
    normed = (
        widened
        * lax.rsqrt(jnp.mean(widened * widened, axis=-1, keepdims=True) + 1e-06)
        * norm_gain[None, :]
    ).astype(jnp.bfloat16)
    local_experts = w_gate.shape[0]
    experts = owners * local_experts
    capacity = max(2, 2 * rows_here // experts + 1)
    width = residual.shape[1]
    chosen = expert_ids.reshape(-1)
    onehot = (chosen[:, None] == jnp.arange(experts)[None, :]).astype(jnp.int32)
    slot_index = jnp.sum((jnp.cumsum(onehot, axis=0) - onehot) * onehot, axis=1)
    target = chosen * capacity + slot_index
    placing = (target[None, :] == jnp.arange(experts * capacity)[:, None]).astype(jnp.bfloat16)
    pair_rows = jnp.repeat(normed, 2, axis=0)
    outgoing = jnp.dot(placing, pair_rows, preferred_element_type=jnp.float32).astype(jnp.bfloat16)
    block = capacity * width // 16
    arrived = exchange(outgoing.reshape(experts, 16, block), 1)
    arrived = arrived.reshape(capacity * experts, width)
    segment = lax.all_gather(arrived, "seq", axis=0, tiled=True)
    partial_value = expert_mlp(segment, w_gate[0], w_up[0], w_down[0])
    summed = lax.psum_scatter(partial_value, "seq", scatter_dimension=0, tiled=True)
    returned = exchange(summed.reshape(experts, 16, block), 2)
    results = returned.reshape(experts * capacity, width)
    picked = results[target].astype(jnp.float32).reshape(rows_here, 2, width)
    mixture = jnp.sum(picked * gate_weights[:, :, None], axis=1)
    return (widened + mixture).astype(jnp.bfloat16)


def solution(mesh):
    return jax.shard_map(
        on_device,
        mesh=mesh,
        in_specs=(
            P("seq", "exp"),
            P("seq", "exp"),
            P("seq", None),
            P("seq", None),
            P("seq", "exp"),
            P("exp"),
            P("exp"),
            P("exp", None, None),
            P(("seq", "exp"), None),
            P(),
            P(("seq", "exp"), None),
            P(("seq", "exp"), None),
            P("exp", None, "seq"),
            P("exp", None, "seq"),
            P("exp", "seq", None),
        ),
        out_specs=P(("seq", "exp"), None),
        check_vma=False,
    )
```

```python
import functools

import jax
import jax.numpy as jnp
from jax import lax
from jax.sharding import PartitionSpec as P
from jax.experimental import pallas as pl
from jax.experimental.pallas import tpu as pltpu

GROUP = 128


PRECISE = lax.Precision.HIGHEST


def exchange_body(x_ref, o_ref, send_sem, recv_sem, local_sem):
    devices = x_ref.shape[0]
    me = lax.axis_index("exp")
    row = lax.axis_index("seq")
    mesh_id = pl.DeviceIdType.MESH
    barrier = pltpu.get_barrier_semaphore()
    for step in range(1, devices):
        peer = lax.rem(me + step, devices)
        pl.semaphore_signal(barrier, 1, device_id=(row, peer), device_id_type=mesh_id)
    local = pltpu.make_async_copy(x_ref.at[me], o_ref.at[me], local_sem)
    local.start()
    pl.semaphore_wait(barrier, devices - 1)
    copies = []
    order = sorted(range(1, devices), key=lambda step: -min(step, devices - step))
    for step in order:
        peer = lax.rem(me + step, devices)
        copy = pltpu.make_async_remote_copy(
            src_ref=x_ref.at[peer],
            dst_ref=o_ref.at[me],
            send_sem=send_sem.at[step],
            recv_sem=recv_sem.at[step],
            device_id=(row, peer),
            device_id_type=mesh_id,
        )
        copy.start()
        copies.append(copy)
    local.wait()
    for copy in copies:
        copy.wait()


def exchange(x, collective):
    devices = x.shape[0]
    return pl.pallas_call(
        exchange_body,
        out_shape=jax.ShapeDtypeStruct(x.shape, x.dtype),
        in_specs=[pl.BlockSpec(memory_space=pltpu.VMEM)],
        out_specs=pl.BlockSpec(memory_space=pltpu.VMEM),
        scratch_shapes=[
            pltpu.SemaphoreType.DMA((devices,)),
            pltpu.SemaphoreType.DMA((devices,)),
            pltpu.SemaphoreType.DMA,
        ],
        compiler_params=pltpu.CompilerParams(collective_id=collective, has_side_effects=True),
    )(x)


def expert_body(depth_steps, seg_ref, gate_ref, up_ref, down_ref, o_ref, gate_acc, up_acc, active):
    step = pl.program_id(0)

    @pl.when(step == 0)
    def _():
        gate_acc[...] = jnp.zeros_like(gate_acc)
        up_acc[...] = jnp.zeros_like(up_acc)

    @pl.when(step < depth_steps)
    def _():
        joined = jnp.concatenate([gate_ref[...], up_ref[...]], axis=1)
        both = jnp.dot(seg_ref[...], joined, preferred_element_type=jnp.float32)
        hidden = gate_acc.shape[1]
        gate_acc[...] += both[:, :hidden]
        up_acc[...] += both[:, hidden:]

    @pl.when(step == depth_steps - 1)
    def _():
        gate = gate_acc[...]
        active[...] = (gate / (1.0 + jnp.exp(-gate)) * up_acc[...]).astype(active.dtype)

    @pl.when(step >= depth_steps)
    def _():
        o_ref[...] = jnp.dot(
            active[...], down_ref[...], preferred_element_type=jnp.float32
        ).astype(o_ref.dtype)


def expert_mlp(segment, gate_w, up_w, down_w):
    rows, width = segment.shape
    hidden = gate_w.shape[1]
    block = 4096
    columns = 2048
    depth_steps = width // block
    column_steps = width // columns
    return pl.pallas_call(
        functools.partial(expert_body, depth_steps),
        grid=(depth_steps + column_steps,),
        in_specs=[
            pl.BlockSpec((rows, block), lambda i: (0, jnp.minimum(i, depth_steps - 1))),
            pl.BlockSpec((block, hidden), lambda i: (jnp.minimum(i, depth_steps - 1), 0)),
            pl.BlockSpec((block, hidden), lambda i: (jnp.minimum(i, depth_steps - 1), 0)),
            pl.BlockSpec((hidden, columns), lambda i: (0, jnp.maximum(i - depth_steps, 0))),
        ],
        out_specs=pl.BlockSpec((rows, columns), lambda i: (0, jnp.maximum(i - depth_steps, 0))),
        out_shape=jax.ShapeDtypeStruct((rows, width), jnp.bfloat16),
        scratch_shapes=[
            pltpu.VMEM((rows, hidden), jnp.float32),
            pltpu.VMEM((rows, hidden), jnp.float32),
            pltpu.VMEM((rows, hidden), jnp.bfloat16),
        ],
        cost_estimate=pl.CostEstimate(
            flops=6 * rows * width * hidden,
            transcendentals=rows * hidden,
            bytes_accessed=2 * (2 * rows * width + 3 * width * hidden),
        ),
    )(segment, gate_w, up_w, down_w)


def scan_rounds(devices):
    return [list(range(1, devices))]


def fold(earlier_state, earlier_log, later_state, later_log):
    decay = jnp.exp(later_log[:, 0:1, :])
    return decay * earlier_state + later_state, earlier_log + later_log


def scan_body(devices, x_state, x_log, o_state, o_log, inc_state, inc_log, wire, recv, send_sem, recv_sem):
    me = lax.axis_index("seq")
    col = lax.axis_index("exp")
    rows = x_state.shape[1]
    mesh_id = pl.DeviceIdType.MESH
    barrier = pltpu.get_barrier_semaphore()
    for step in range(1, devices):
        peer = lax.rem(me + step, devices)
        pl.semaphore_signal(barrier, 1, device_id=(peer, col), device_id_type=mesh_id)
    pl.semaphore_wait(barrier, devices - 1)
    inc_state[0] = x_state[...]
    inc_log[0] = x_log[...]
    o_state[...] = jnp.zeros_like(o_state)
    o_log[...] = jnp.zeros_like(o_log)
    for level, shifts in enumerate(scan_rounds(devices)):
        log_now = inc_log[level]
        high = log_now.astype(jnp.bfloat16).astype(jnp.float32)
        wire[level, :, :rows, :] = inc_state[level].astype(jnp.bfloat16)
        wire[level, :, rows:, :] = jnp.concatenate([high, log_now - high], axis=1).astype(jnp.bfloat16)

        def link(slot, peer):
            return pltpu.make_async_remote_copy(
                src_ref=wire.at[level],
                dst_ref=recv.at[level, slot],
                send_sem=send_sem.at[level, slot],
                recv_sem=recv_sem.at[level, slot],
                device_id=(peer, col),
                device_id_type=mesh_id,
            )
        for slot, shift in enumerate(shifts):
            @pl.when(me + shift < devices)
            def _():
                link(slot, me + shift).start()
        inc_state[level + 1] = inc_state[level]
        inc_log[level + 1] = inc_log[level]
        for slot, shift in enumerate(shifts):
            @pl.when(me >= shift)
            def _():
                link(slot, me - shift).wait_recv()
                got_state = recv[level, slot, :, :rows, :].astype(jnp.float32)
                parts = recv[level, slot, :, rows:, :].astype(jnp.float32)
                got_log = parts[:, :8, :] + parts[:, 8:, :]
                new_state, new_log = fold(got_state, got_log, inc_state[level + 1], inc_log[level + 1])
                inc_state[level + 1] = new_state
                inc_log[level + 1] = new_log
                new_state, new_log = fold(got_state, got_log, o_state[...], o_log[...])
                o_state[...] = new_state
                o_log[...] = new_log
        for slot, shift in enumerate(shifts):
            @pl.when(me + shift < devices)
            def _():
                link(slot, me + shift).wait_send()


def exclusive_scan(log, state, axis):
    devices = lax.axis_size(axis)
    heads, state_rows, lanes = state.shape
    log_rows = jnp.broadcast_to(log[:, None, None], (heads, 8, lanes))
    levels = len(scan_rounds(devices))
    wire_shape = (heads, state_rows + 16, lanes)
    prior_state, prior_log = pl.pallas_call(
        functools.partial(scan_body, devices),
        out_shape=(
            jax.ShapeDtypeStruct(state.shape, jnp.float32),
            jax.ShapeDtypeStruct(log_rows.shape, jnp.float32),
        ),
        in_specs=[pl.BlockSpec(memory_space=pltpu.VMEM)] * 2,
        out_specs=(pl.BlockSpec(memory_space=pltpu.VMEM),) * 2,
        scratch_shapes=[
            pltpu.VMEM((levels + 1,) + state.shape, jnp.float32),
            pltpu.VMEM((levels + 1,) + log_rows.shape, jnp.float32),
            pltpu.VMEM((levels,) + wire_shape, jnp.bfloat16),
            pltpu.VMEM((levels, devices - 1) + wire_shape, jnp.bfloat16),
            pltpu.SemaphoreType.DMA((levels, devices - 1)),
            pltpu.SemaphoreType.DMA((levels, devices - 1)),
        ],
        compiler_params=pltpu.CompilerParams(collective_id=3, has_side_effects=True),
    )(state, log_rows)
    return prior_log[:, 0, 0], prior_state


def chain_combine(earlier, later):
    return (earlier[0] + later[0], jnp.exp(later[0])[:, None, None] * earlier[1] + later[1])


def on_device(
    x_in,
    z_gate,
    b_in,
    c_out,
    dt_step,
    rate,
    skip,
    init_state,
    residual,
    norm_gain,
    expert_ids,
    gate_weights,
    w_gate,
    w_up,
    w_down,
):
    token_count, channels = x_in.shape
    heads_here = rate.shape[0]
    head_width = channels // heads_here
    state_width = b_in.shape[1]
    blocks = token_count // GROUP
    inputs = x_in.astype(jnp.float32).reshape(blocks, GROUP, heads_here, head_width)
    keys_in = b_in.astype(jnp.float32).reshape(blocks, GROUP, state_width)
    queries = c_out.astype(jnp.float32).reshape(blocks, GROUP, state_width)
    log_steps = (-rate[None, :] * dt_step).reshape(blocks, GROUP, heads_here)
    cumulative = jnp.cumsum(log_steps, axis=1)
    scores = jnp.einsum("ctn,csn->cts", queries, keys_in, precision=PRECISE)
    causal = jnp.arange(GROUP)[:, None] >= jnp.arange(GROUP)[None, :]
    spread = cumulative[:, :, None, :] - cumulative[:, None, :, :]
    weights = jnp.exp(jnp.where(causal[None, :, :, None], spread, -jnp.inf)) * scores[..., None]
    intra_out = jnp.einsum("ctsh,cshp->cthp", weights, inputs, precision=PRECISE)
    tail_decay = jnp.exp(cumulative[:, -1:, :] - cumulative)
    block_state = jnp.einsum("csh,cshp,csn->chpn", tail_decay, inputs, keys_in, precision=PRECISE)
    block_log = cumulative[:, -1, :]

    def advance(carried, element):
        total_log, total_state = carried
        step_log, step_state = element
        updated = (
            total_log + step_log,
            jnp.exp(step_log)[:, None, None] * total_state + step_state,
        )
        return (updated, (total_log, total_state))

    zero_state = jnp.zeros((heads_here, head_width, state_width), jnp.float32)
    zero_log = jnp.zeros((heads_here,), jnp.float32)
    (device_log, device_state), (enter_log, enter_state) = lax.scan(
        advance, (zero_log, zero_state), (block_log, block_state)
    )
    prior_log, prior_state = exclusive_scan(device_log, device_state, "seq")
    incoming = prior_state + jnp.exp(prior_log)[:, None, None] * init_state
    entering = enter_state + jnp.exp(enter_log)[:, :, None, None] * incoming[None]
    inter_out = jnp.exp(cumulative)[..., None] * jnp.einsum(
        "chpn,ctn->cthp", entering, queries, precision=PRECISE
    )
    mixed_out = (intra_out + inter_out + skip[None, None, :, None] * inputs).reshape(
        token_count, channels
    )
    mixer = (mixed_out * jax.nn.silu(z_gate.astype(jnp.float32))).astype(jnp.bfloat16)
    owners = lax.axis_size("exp")
    rows_here = residual.shape[0]
    arrived_mix = exchange(mixer.reshape(owners, rows_here, channels), 0)
    token_mix = arrived_mix.transpose(1, 0, 2).reshape(rows_here, owners * channels)
    stream = (residual.astype(jnp.float32) + token_mix.astype(jnp.float32)).astype(jnp.bfloat16)
    widened = stream.astype(jnp.float32)
    normed = (
        widened
        * lax.rsqrt(jnp.mean(widened * widened, axis=-1, keepdims=True) + 1e-06)
        * norm_gain[None, :]
    ).astype(jnp.bfloat16)
    local_experts = w_gate.shape[0]
    experts = owners * local_experts
    capacity = max(2, 2 * rows_here // experts + 1)
    width = residual.shape[1]
    chosen = expert_ids.reshape(-1)
    onehot = (chosen[:, None] == jnp.arange(experts)[None, :]).astype(jnp.int32)
    slot_index = jnp.sum((jnp.cumsum(onehot, axis=0) - onehot) * onehot, axis=1)
    target = chosen * capacity + slot_index
    placing = (target[None, :] == jnp.arange(experts * capacity)[:, None]).astype(jnp.bfloat16)
    pair_rows = jnp.repeat(normed, 2, axis=0)
    outgoing = jnp.dot(placing, pair_rows, preferred_element_type=jnp.float32).astype(jnp.bfloat16)
    block = capacity * width // 16
    arrived = exchange(outgoing.reshape(experts, 16, block), 1)
    arrived = arrived.reshape(capacity * experts, width)
    segment = lax.all_gather(arrived, "seq", axis=0, tiled=True)
    partial_value = expert_mlp(segment, w_gate[0], w_up[0], w_down[0])
    summed = lax.psum_scatter(partial_value, "seq", scatter_dimension=0, tiled=True)
    returned = exchange(summed.reshape(experts, 16, block), 2)
    results = returned.reshape(experts * capacity, width)
    picked = results[target].astype(jnp.float32).reshape(rows_here, 2, width)
    mixture = jnp.sum(picked * gate_weights[:, :, None], axis=1)
    return (widened + mixture).astype(jnp.bfloat16)


def solution(mesh):
    return jax.shard_map(
        on_device,
        mesh=mesh,
        in_specs=(
            P("seq", "exp"),
            P("seq", "exp"),
            P("seq", None),
            P("seq", None),
            P("seq", "exp"),
            P("exp"),
            P("exp"),
            P("exp", None, None),
            P(("seq", "exp"), None),
            P(),
            P(("seq", "exp"), None),
            P(("seq", "exp"), None),
            P("exp", None, "seq"),
            P("exp", None, "seq"),
            P("exp", "seq", None),
        ),
        out_specs=P(("seq", "exp"), None),
        check_vma=False,
    )
```

```python
import functools

import jax
import jax.numpy as jnp
from jax import lax
from jax.sharding import PartitionSpec as P
from jax.experimental import pallas as pl
from jax.experimental.pallas import tpu as pltpu

GROUP = 128


PRECISE = lax.Precision.HIGHEST


def exchange_body(x_ref, o_ref, send_sem, recv_sem, local_sem):
    devices = x_ref.shape[0]
    me = lax.axis_index("exp")
    row = lax.axis_index("seq")
    mesh_id = pl.DeviceIdType.MESH
    barrier = pltpu.get_barrier_semaphore()
    for step in range(1, devices):
        peer = lax.rem(me + step, devices)
        pl.semaphore_signal(barrier, 1, device_id=(row, peer), device_id_type=mesh_id)
    local = pltpu.make_async_copy(x_ref.at[me], o_ref.at[me], local_sem)
    local.start()
    pl.semaphore_wait(barrier, devices - 1)
    copies = []
    order = sorted(range(1, devices), key=lambda step: -min(step, devices - step))
    for step in order:
        peer = lax.rem(me + step, devices)
        copy = pltpu.make_async_remote_copy(
            src_ref=x_ref.at[peer],
            dst_ref=o_ref.at[me],
            send_sem=send_sem.at[step],
            recv_sem=recv_sem.at[step],
            device_id=(row, peer),
            device_id_type=mesh_id,
        )
        copy.start()
        copies.append(copy)
    local.wait()
    for copy in copies:
        copy.wait()


def exchange(x, collective):
    devices = x.shape[0]
    return pl.pallas_call(
        exchange_body,
        out_shape=jax.ShapeDtypeStruct(x.shape, x.dtype),
        in_specs=[pl.BlockSpec(memory_space=pltpu.VMEM)],
        out_specs=pl.BlockSpec(memory_space=pltpu.VMEM),
        scratch_shapes=[
            pltpu.SemaphoreType.DMA((devices,)),
            pltpu.SemaphoreType.DMA((devices,)),
            pltpu.SemaphoreType.DMA,
        ],
        compiler_params=pltpu.CompilerParams(collective_id=collective, has_side_effects=True),
    )(x)


def expert_body(depth_steps, seg_ref, gate_ref, up_ref, down_ref, o_ref, gate_acc, up_acc, active):
    step = pl.program_id(0)

    @pl.when(step == 0)
    def _():
        gate_acc[...] = jnp.zeros_like(gate_acc)
        up_acc[...] = jnp.zeros_like(up_acc)

    @pl.when(step < depth_steps)
    def _():
        joined = jnp.concatenate([gate_ref[...], up_ref[...]], axis=1)
        both = jnp.dot(seg_ref[...], joined, preferred_element_type=jnp.float32)
        hidden = gate_acc.shape[1]
        gate_acc[...] += both[:, :hidden]
        up_acc[...] += both[:, hidden:]

    @pl.when(step == depth_steps - 1)
    def _():
        gate = gate_acc[...]
        active[...] = (gate / (1.0 + jnp.exp(-gate)) * up_acc[...]).astype(active.dtype)

    @pl.when(step >= depth_steps)
    def _():
        o_ref[...] = jnp.dot(
            active[...], down_ref[...], preferred_element_type=jnp.float32
        ).astype(o_ref.dtype)


def expert_mlp(segment, gate_w, up_w, down_w):
    rows, width = segment.shape
    hidden = gate_w.shape[1]
    block = 4096
    columns = 2048
    depth_steps = width // block
    column_steps = width // columns
    return pl.pallas_call(
        functools.partial(expert_body, depth_steps),
        grid=(depth_steps + column_steps,),
        in_specs=[
            pl.BlockSpec((rows, block), lambda i: (0, jnp.minimum(i, depth_steps - 1))),
            pl.BlockSpec((block, hidden), lambda i: (jnp.minimum(i, depth_steps - 1), 0)),
            pl.BlockSpec((block, hidden), lambda i: (jnp.minimum(i, depth_steps - 1), 0)),
            pl.BlockSpec((hidden, columns), lambda i: (0, jnp.maximum(i - depth_steps, 0))),
        ],
        out_specs=pl.BlockSpec((rows, columns), lambda i: (0, jnp.maximum(i - depth_steps, 0))),
        out_shape=jax.ShapeDtypeStruct((rows, width), jnp.bfloat16),
        scratch_shapes=[
            pltpu.VMEM((rows, hidden), jnp.float32),
            pltpu.VMEM((rows, hidden), jnp.float32),
            pltpu.VMEM((rows, hidden), jnp.bfloat16),
        ],
        cost_estimate=pl.CostEstimate(
            flops=6 * rows * width * hidden,
            transcendentals=rows * hidden,
            bytes_accessed=2 * (2 * rows * width + 3 * width * hidden),
        ),
    )(segment, gate_w, up_w, down_w)


def scan_rounds(devices):
    rounds, base = [], 1
    while base < devices:
        rounds.append([j * base for j in range(1, 4) if j * base < devices])
        base *= 4
    return rounds


def fold(earlier_state, earlier_log, later_state, later_log):
    decay = jnp.exp(later_log[:, 0:1, :])
    return decay * earlier_state + later_state, earlier_log + later_log


def scan_body(devices, x_state, x_log, o_state, o_log, inc_state, inc_log, wire, recv, send_sem, recv_sem):
    me = lax.axis_index("seq")
    col = lax.axis_index("exp")
    rows = x_state.shape[1]
    mesh_id = pl.DeviceIdType.MESH
    barrier = pltpu.get_barrier_semaphore()
    for step in range(1, devices):
        peer = lax.rem(me + step, devices)
        pl.semaphore_signal(barrier, 1, device_id=(peer, col), device_id_type=mesh_id)
    pl.semaphore_wait(barrier, devices - 1)
    o_state[...] = jnp.zeros_like(o_state)
    o_log[...] = jnp.zeros_like(o_log)
    levels = scan_rounds(devices)
    for level, shifts in enumerate(levels):
        last = level == len(levels) - 1
        state_now = x_state if level == 0 else inc_state.at[level]
        log_now = x_log[...] if level == 0 else inc_log[level]
        high = log_now.astype(jnp.bfloat16).astype(jnp.float32)
        wire[level, :, :rows, :] = state_now[...].astype(jnp.bfloat16)
        wire[level, :, rows:, :] = jnp.concatenate([high, log_now - high], axis=1).astype(jnp.bfloat16)

        def link(slot, peer):
            return pltpu.make_async_remote_copy(
                src_ref=wire.at[level],
                dst_ref=recv.at[level, slot],
                send_sem=send_sem.at[level, slot],
                recv_sem=recv_sem.at[level, slot],
                device_id=(peer, col),
                device_id_type=mesh_id,
            )
        for slot, shift in enumerate(shifts):
            @pl.when(me + shift < devices)
            def _():
                link(slot, me + shift).start()
        if not last:
            inc_state[level + 1] = state_now[...]
            inc_log[level + 1] = log_now
        for slot, shift in enumerate(shifts):
            @pl.when(me >= shift)
            def _():
                link(slot, me - shift).wait_recv()
                got_state = recv[level, slot, :, :rows, :].astype(jnp.float32)
                parts = recv[level, slot, :, rows:, :].astype(jnp.float32)
                got_log = parts[:, :8, :] + parts[:, 8:, :]
                if not last:
                    new_state, new_log = fold(got_state, got_log, inc_state[level + 1], inc_log[level + 1])
                    inc_state[level + 1] = new_state
                    inc_log[level + 1] = new_log
                new_state, new_log = fold(got_state, got_log, o_state[...], o_log[...])
                o_state[...] = new_state
                o_log[...] = new_log
        for slot, shift in enumerate(shifts):
            @pl.when(me + shift < devices)
            def _():
                link(slot, me + shift).wait_send()


def exclusive_scan(log, state, axis):
    devices = lax.axis_size(axis)
    heads, state_rows, lanes = state.shape
    log_rows = jnp.broadcast_to(log[:, None, None], (heads, 8, lanes))
    levels = len(scan_rounds(devices))
    wire_shape = (heads, state_rows + 16, lanes)
    prior_state, prior_log = pl.pallas_call(
        functools.partial(scan_body, devices),
        out_shape=(
            jax.ShapeDtypeStruct(state.shape, jnp.float32),
            jax.ShapeDtypeStruct(log_rows.shape, jnp.float32),
        ),
        in_specs=[pl.BlockSpec(memory_space=pltpu.VMEM)] * 2,
        out_specs=(pl.BlockSpec(memory_space=pltpu.VMEM),) * 2,
        scratch_shapes=[
            pltpu.VMEM((levels + 1,) + state.shape, jnp.float32),
            pltpu.VMEM((levels + 1,) + log_rows.shape, jnp.float32),
            pltpu.VMEM((levels,) + wire_shape, jnp.bfloat16),
            pltpu.VMEM((levels, 3) + wire_shape, jnp.bfloat16),
            pltpu.SemaphoreType.DMA((levels, 3)),
            pltpu.SemaphoreType.DMA((levels, 3)),
        ],
        compiler_params=pltpu.CompilerParams(collective_id=3, has_side_effects=True),
    )(state, log_rows)
    return prior_log[:, 0, 0], prior_state


def chain_combine(earlier, later):
    return (earlier[0] + later[0], jnp.exp(later[0])[:, None, None] * earlier[1] + later[1])


def on_device(
    x_in,
    z_gate,
    b_in,
    c_out,
    dt_step,
    rate,
    skip,
    init_state,
    residual,
    norm_gain,
    expert_ids,
    gate_weights,
    w_gate,
    w_up,
    w_down,
):
    token_count, channels = x_in.shape
    heads_here = rate.shape[0]
    head_width = channels // heads_here
    state_width = b_in.shape[1]
    blocks = token_count // GROUP
    inputs = x_in.astype(jnp.float32).reshape(blocks, GROUP, heads_here, head_width)
    keys_in = b_in.astype(jnp.float32).reshape(blocks, GROUP, state_width)
    queries = c_out.astype(jnp.float32).reshape(blocks, GROUP, state_width)
    log_steps = (-rate[None, :] * dt_step).reshape(blocks, GROUP, heads_here)
    cumulative = jnp.cumsum(log_steps, axis=1)
    scores = jnp.einsum("ctn,csn->cts", queries, keys_in, precision=PRECISE)
    causal = jnp.arange(GROUP)[:, None] >= jnp.arange(GROUP)[None, :]
    spread = cumulative[:, :, None, :] - cumulative[:, None, :, :]
    weights = jnp.exp(jnp.where(causal[None, :, :, None], spread, -jnp.inf)) * scores[..., None]
    intra_out = jnp.einsum("ctsh,cshp->cthp", weights, inputs, precision=PRECISE)
    tail_decay = jnp.exp(cumulative[:, -1:, :] - cumulative)
    block_state = jnp.einsum("csh,cshp,csn->chpn", tail_decay, inputs, keys_in, precision=PRECISE)
    block_log = cumulative[:, -1, :]

    def advance(carried, element):
        total_log, total_state = carried
        step_log, step_state = element
        updated = (
            total_log + step_log,
            jnp.exp(step_log)[:, None, None] * total_state + step_state,
        )
        return (updated, (total_log, total_state))

    zero_state = jnp.zeros((heads_here, head_width, state_width), jnp.float32)
    zero_log = jnp.zeros((heads_here,), jnp.float32)
    (device_log, device_state), (enter_log, enter_state) = lax.scan(
        advance, (zero_log, zero_state), (block_log, block_state)
    )
    prior_log, prior_state = exclusive_scan(device_log, device_state, "seq")
    incoming = prior_state + jnp.exp(prior_log)[:, None, None] * init_state
    entering = enter_state + jnp.exp(enter_log)[:, :, None, None] * incoming[None]
    inter_out = jnp.exp(cumulative)[..., None] * jnp.einsum(
        "chpn,ctn->cthp", entering, queries, precision=PRECISE
    )
    mixed_out = (intra_out + inter_out + skip[None, None, :, None] * inputs).reshape(
        token_count, channels
    )
    mixer = (mixed_out * jax.nn.silu(z_gate.astype(jnp.float32))).astype(jnp.bfloat16)
    owners = lax.axis_size("exp")
    rows_here = residual.shape[0]
    arrived_mix = exchange(mixer.reshape(owners, rows_here, channels), 0)
    token_mix = arrived_mix.transpose(1, 0, 2).reshape(rows_here, owners * channels)
    stream = (residual.astype(jnp.float32) + token_mix.astype(jnp.float32)).astype(jnp.bfloat16)
    widened = stream.astype(jnp.float32)
    normed = (
        widened
        * lax.rsqrt(jnp.mean(widened * widened, axis=-1, keepdims=True) + 1e-06)
        * norm_gain[None, :]
    ).astype(jnp.bfloat16)
    local_experts = w_gate.shape[0]
    experts = owners * local_experts
    capacity = max(2, 2 * rows_here // experts + 1)
    width = residual.shape[1]
    chosen = expert_ids.reshape(-1)
    onehot = (chosen[:, None] == jnp.arange(experts)[None, :]).astype(jnp.int32)
    slot_index = jnp.sum((jnp.cumsum(onehot, axis=0) - onehot) * onehot, axis=1)
    target = chosen * capacity + slot_index
    placing = (target[None, :] == jnp.arange(experts * capacity)[:, None]).astype(jnp.bfloat16)
    pair_rows = jnp.repeat(normed, 2, axis=0)
    outgoing = jnp.dot(placing, pair_rows, preferred_element_type=jnp.float32).astype(jnp.bfloat16)
    block = capacity * width // 16
    arrived = exchange(outgoing.reshape(experts, 16, block), 1)
    arrived = arrived.reshape(capacity * experts, width)
    segment = lax.all_gather(arrived, "seq", axis=0, tiled=True)
    partial_value = expert_mlp(segment, w_gate[0], w_up[0], w_down[0])
    summed = lax.psum_scatter(partial_value, "seq", scatter_dimension=0, tiled=True)
    returned = exchange(summed.reshape(experts, 16, block), 2)
    results = returned.reshape(experts * capacity, width)
    picked = results[target].astype(jnp.float32).reshape(rows_here, 2, width)
    mixture = jnp.sum(picked * gate_weights[:, :, None], axis=1)
    return (widened + mixture).astype(jnp.bfloat16)


def solution(mesh):
    return jax.shard_map(
        on_device,
        mesh=mesh,
        in_specs=(
            P("seq", "exp"),
            P("seq", "exp"),
            P("seq", None),
            P("seq", None),
            P("seq", "exp"),
            P("exp"),
            P("exp"),
            P("exp", None, None),
            P(("seq", "exp"), None),
            P(),
            P(("seq", "exp"), None),
            P(("seq", "exp"), None),
            P("exp", None, "seq"),
            P("exp", None, "seq"),
            P("exp", "seq", None),
        ),
        out_specs=P(("seq", "exp"), None),
        check_vma=False,
    )
```

```python
import functools

import jax
import jax.numpy as jnp
from jax import lax
from jax.sharding import PartitionSpec as P
from jax.experimental import pallas as pl
from jax.experimental.pallas import tpu as pltpu

GROUP = 128


PRECISE = lax.Precision.HIGHEST


def exchange_body(x_ref, o_ref, send_sem, recv_sem, local_sem):
    devices = x_ref.shape[0]
    me = lax.axis_index("exp")
    row = lax.axis_index("seq")
    mesh_id = pl.DeviceIdType.MESH
    barrier = pltpu.get_barrier_semaphore()
    for step in range(1, devices):
        peer = lax.rem(me + step, devices)
        pl.semaphore_signal(barrier, 1, device_id=(row, peer), device_id_type=mesh_id)
    local = pltpu.make_async_copy(x_ref.at[me], o_ref.at[me], local_sem)
    local.start()
    pl.semaphore_wait(barrier, devices - 1)
    copies = []
    order = sorted(range(1, devices), key=lambda step: -min(step, devices - step))
    for step in order:
        peer = lax.rem(me + step, devices)
        copy = pltpu.make_async_remote_copy(
            src_ref=x_ref.at[peer],
            dst_ref=o_ref.at[me],
            send_sem=send_sem.at[step],
            recv_sem=recv_sem.at[step],
            device_id=(row, peer),
            device_id_type=mesh_id,
        )
        copy.start()
        copies.append(copy)
    local.wait()
    for copy in copies:
        copy.wait()


def exchange(x, collective):
    devices = x.shape[0]
    return pl.pallas_call(
        exchange_body,
        out_shape=jax.ShapeDtypeStruct(x.shape, x.dtype),
        in_specs=[pl.BlockSpec(memory_space=pltpu.VMEM)],
        out_specs=pl.BlockSpec(memory_space=pltpu.VMEM),
        scratch_shapes=[
            pltpu.SemaphoreType.DMA((devices,)),
            pltpu.SemaphoreType.DMA((devices,)),
            pltpu.SemaphoreType.DMA,
        ],
        compiler_params=pltpu.CompilerParams(collective_id=collective, has_side_effects=True),
    )(x)


def expert_body(depth_steps, seg_ref, gate_ref, up_ref, down_ref, o_ref, gate_acc, up_acc, active):
    step = pl.program_id(0)

    @pl.when(step == 0)
    def _():
        gate_acc[...] = jnp.zeros_like(gate_acc)
        up_acc[...] = jnp.zeros_like(up_acc)

    @pl.when(step < depth_steps)
    def _():
        joined = jnp.concatenate([gate_ref[...], up_ref[...]], axis=1)
        both = jnp.dot(seg_ref[...], joined, preferred_element_type=jnp.float32)
        hidden = gate_acc.shape[1]
        gate_acc[...] += both[:, :hidden]
        up_acc[...] += both[:, hidden:]

    @pl.when(step == depth_steps - 1)
    def _():
        gate = gate_acc[...]
        active[...] = (gate / (1.0 + jnp.exp(-gate)) * up_acc[...]).astype(active.dtype)

    @pl.when(step >= depth_steps)
    def _():
        o_ref[...] = jnp.dot(
            active[...], down_ref[...], preferred_element_type=jnp.float32
        ).astype(o_ref.dtype)


def expert_mlp(segment, gate_w, up_w, down_w):
    rows, width = segment.shape
    hidden = gate_w.shape[1]
    block = 4096
    columns = 2048
    depth_steps = width // block
    column_steps = width // columns
    return pl.pallas_call(
        functools.partial(expert_body, depth_steps),
        grid=(depth_steps + column_steps,),
        in_specs=[
            pl.BlockSpec((rows, block), lambda i: (0, jnp.minimum(i, depth_steps - 1))),
            pl.BlockSpec((block, hidden), lambda i: (jnp.minimum(i, depth_steps - 1), 0)),
            pl.BlockSpec((block, hidden), lambda i: (jnp.minimum(i, depth_steps - 1), 0)),
            pl.BlockSpec((hidden, columns), lambda i: (0, jnp.maximum(i - depth_steps, 0))),
        ],
        out_specs=pl.BlockSpec((rows, columns), lambda i: (0, jnp.maximum(i - depth_steps, 0))),
        out_shape=jax.ShapeDtypeStruct((rows, width), jnp.bfloat16),
        scratch_shapes=[
            pltpu.VMEM((rows, hidden), jnp.float32),
            pltpu.VMEM((rows, hidden), jnp.float32),
            pltpu.VMEM((rows, hidden), jnp.bfloat16),
        ],
        cost_estimate=pl.CostEstimate(
            flops=6 * rows * width * hidden,
            transcendentals=rows * hidden,
            bytes_accessed=2 * (2 * rows * width + 3 * width * hidden),
        ),
    )(segment, gate_w, up_w, down_w)


def scan_rounds(devices):
    rounds, base = [], 1
    while base < devices:
        rounds.append([base])
        base *= 2
    return rounds


def fold(earlier_state, earlier_log, later_state, later_log):
    decay = jnp.exp(later_log[:, 0:1, :])
    return decay * earlier_state + later_state, earlier_log + later_log


def scan_body(devices, x_state, x_log, o_state, o_log, inc_state, inc_log, wire, recv, send_sem, recv_sem):
    me = lax.axis_index("seq")
    col = lax.axis_index("exp")
    rows = x_state.shape[1]
    mesh_id = pl.DeviceIdType.MESH
    barrier = pltpu.get_barrier_semaphore()
    for step in range(1, devices):
        peer = lax.rem(me + step, devices)
        pl.semaphore_signal(barrier, 1, device_id=(peer, col), device_id_type=mesh_id)
    pl.semaphore_wait(barrier, devices - 1)
    o_state[...] = jnp.zeros_like(o_state)
    o_log[...] = jnp.zeros_like(o_log)
    levels = scan_rounds(devices)
    for level, shifts in enumerate(levels):
        last = level == len(levels) - 1
        state_now = x_state if level == 0 else inc_state.at[level]
        log_now = x_log[...] if level == 0 else inc_log[level]
        high = log_now.astype(jnp.bfloat16).astype(jnp.float32)
        wire[level, :, :rows, :] = state_now[...].astype(jnp.bfloat16)
        wire[level, :, rows:, :] = jnp.concatenate([high, log_now - high], axis=1).astype(jnp.bfloat16)

        def link(slot, peer):
            return pltpu.make_async_remote_copy(
                src_ref=wire.at[level],
                dst_ref=recv.at[level, slot],
                send_sem=send_sem.at[level, slot],
                recv_sem=recv_sem.at[level, slot],
                device_id=(peer, col),
                device_id_type=mesh_id,
            )
        for slot, shift in enumerate(shifts):
            @pl.when(me + shift < devices)
            def _():
                link(slot, me + shift).start()
        if not last:
            inc_state[level + 1] = state_now[...]
            inc_log[level + 1] = log_now
        for slot, shift in enumerate(shifts):
            @pl.when(me >= shift)
            def _():
                link(slot, me - shift).wait_recv()
                got_state = recv[level, slot, :, :rows, :].astype(jnp.float32)
                parts = recv[level, slot, :, rows:, :].astype(jnp.float32)
                got_log = parts[:, :8, :] + parts[:, 8:, :]
                if not last:
                    new_state, new_log = fold(got_state, got_log, inc_state[level + 1], inc_log[level + 1])
                    inc_state[level + 1] = new_state
                    inc_log[level + 1] = new_log
                new_state, new_log = fold(got_state, got_log, o_state[...], o_log[...])
                o_state[...] = new_state
                o_log[...] = new_log
        for slot, shift in enumerate(shifts):
            @pl.when(me + shift < devices)
            def _():
                link(slot, me + shift).wait_send()


def exclusive_scan(log, state, axis):
    devices = lax.axis_size(axis)
    heads, state_rows, lanes = state.shape
    log_rows = jnp.broadcast_to(log[:, None, None], (heads, 8, lanes))
    levels = len(scan_rounds(devices))
    wire_shape = (heads, state_rows + 16, lanes)
    prior_state, prior_log = pl.pallas_call(
        functools.partial(scan_body, devices),
        out_shape=(
            jax.ShapeDtypeStruct(state.shape, jnp.float32),
            jax.ShapeDtypeStruct(log_rows.shape, jnp.float32),
        ),
        in_specs=[pl.BlockSpec(memory_space=pltpu.VMEM)] * 2,
        out_specs=(pl.BlockSpec(memory_space=pltpu.VMEM),) * 2,
        scratch_shapes=[
            pltpu.VMEM((levels + 1,) + state.shape, jnp.float32),
            pltpu.VMEM((levels + 1,) + log_rows.shape, jnp.float32),
            pltpu.VMEM((levels,) + wire_shape, jnp.bfloat16),
            pltpu.VMEM((levels, 1) + wire_shape, jnp.bfloat16),
            pltpu.SemaphoreType.DMA((levels, 1)),
            pltpu.SemaphoreType.DMA((levels, 1)),
        ],
        compiler_params=pltpu.CompilerParams(collective_id=3, has_side_effects=True),
    )(state, log_rows)
    return prior_log[:, 0, 0], prior_state


def chain_combine(earlier, later):
    return (earlier[0] + later[0], jnp.exp(later[0])[:, None, None] * earlier[1] + later[1])


def on_device(
    x_in,
    z_gate,
    b_in,
    c_out,
    dt_step,
    rate,
    skip,
    init_state,
    residual,
    norm_gain,
    expert_ids,
    gate_weights,
    w_gate,
    w_up,
    w_down,
):
    token_count, channels = x_in.shape
    heads_here = rate.shape[0]
    head_width = channels // heads_here
    state_width = b_in.shape[1]
    blocks = token_count // GROUP
    inputs = x_in.astype(jnp.float32).reshape(blocks, GROUP, heads_here, head_width)
    keys_in = b_in.astype(jnp.float32).reshape(blocks, GROUP, state_width)
    queries = c_out.astype(jnp.float32).reshape(blocks, GROUP, state_width)
    log_steps = (-rate[None, :] * dt_step).reshape(blocks, GROUP, heads_here)
    cumulative = jnp.cumsum(log_steps, axis=1)
    scores = jnp.einsum("ctn,csn->cts", queries, keys_in, precision=PRECISE)
    causal = jnp.arange(GROUP)[:, None] >= jnp.arange(GROUP)[None, :]
    spread = cumulative[:, :, None, :] - cumulative[:, None, :, :]
    weights = jnp.exp(jnp.where(causal[None, :, :, None], spread, -jnp.inf)) * scores[..., None]
    intra_out = jnp.einsum("ctsh,cshp->cthp", weights, inputs, precision=PRECISE)
    tail_decay = jnp.exp(cumulative[:, -1:, :] - cumulative)
    block_state = jnp.einsum("csh,cshp,csn->chpn", tail_decay, inputs, keys_in, precision=PRECISE)
    block_log = cumulative[:, -1, :]

    def advance(carried, element):
        total_log, total_state = carried
        step_log, step_state = element
        updated = (
            total_log + step_log,
            jnp.exp(step_log)[:, None, None] * total_state + step_state,
        )
        return (updated, (total_log, total_state))

    zero_state = jnp.zeros((heads_here, head_width, state_width), jnp.float32)
    zero_log = jnp.zeros((heads_here,), jnp.float32)
    (device_log, device_state), (enter_log, enter_state) = lax.scan(
        advance, (zero_log, zero_state), (block_log, block_state)
    )
    prior_log, prior_state = exclusive_scan(device_log, device_state, "seq")
    incoming = prior_state + jnp.exp(prior_log)[:, None, None] * init_state
    entering = enter_state + jnp.exp(enter_log)[:, :, None, None] * incoming[None]
    inter_out = jnp.exp(cumulative)[..., None] * jnp.einsum(
        "chpn,ctn->cthp", entering, queries, precision=PRECISE
    )
    mixed_out = (intra_out + inter_out + skip[None, None, :, None] * inputs).reshape(
        token_count, channels
    )
    mixer = (mixed_out * jax.nn.silu(z_gate.astype(jnp.float32))).astype(jnp.bfloat16)
    owners = lax.axis_size("exp")
    rows_here = residual.shape[0]
    arrived_mix = exchange(mixer.reshape(owners, rows_here, channels), 0)
    token_mix = arrived_mix.transpose(1, 0, 2).reshape(rows_here, owners * channels)
    stream = (residual.astype(jnp.float32) + token_mix.astype(jnp.float32)).astype(jnp.bfloat16)
    widened = stream.astype(jnp.float32)
    normed = (
        widened
        * lax.rsqrt(jnp.mean(widened * widened, axis=-1, keepdims=True) + 1e-06)
        * norm_gain[None, :]
    ).astype(jnp.bfloat16)
    local_experts = w_gate.shape[0]
    experts = owners * local_experts
    capacity = max(2, 2 * rows_here // experts + 1)
    width = residual.shape[1]
    chosen = expert_ids.reshape(-1)
    onehot = (chosen[:, None] == jnp.arange(experts)[None, :]).astype(jnp.int32)
    slot_index = jnp.sum((jnp.cumsum(onehot, axis=0) - onehot) * onehot, axis=1)
    target = chosen * capacity + slot_index
    placing = (target[None, :] == jnp.arange(experts * capacity)[:, None]).astype(jnp.bfloat16)
    pair_rows = jnp.repeat(normed, 2, axis=0)
    outgoing = jnp.dot(placing, pair_rows, preferred_element_type=jnp.float32).astype(jnp.bfloat16)
    block = capacity * width // 16
    arrived = exchange(outgoing.reshape(experts, 16, block), 1)
    arrived = arrived.reshape(capacity * experts, width)
    segment = lax.all_gather(arrived, "seq", axis=0, tiled=True)
    partial_value = expert_mlp(segment, w_gate[0], w_up[0], w_down[0])
    summed = lax.psum_scatter(partial_value, "seq", scatter_dimension=0, tiled=True)
    returned = exchange(summed.reshape(experts, 16, block), 2)
    results = returned.reshape(experts * capacity, width)
    picked = results[target].astype(jnp.float32).reshape(rows_here, 2, width)
    mixture = jnp.sum(picked * gate_weights[:, :, None], axis=1)
    return (widened + mixture).astype(jnp.bfloat16)


def solution(mesh):
    return jax.shard_map(
        on_device,
        mesh=mesh,
        in_specs=(
            P("seq", "exp"),
            P("seq", "exp"),
            P("seq", None),
            P("seq", None),
            P("seq", "exp"),
            P("exp"),
            P("exp"),
            P("exp", None, None),
            P(("seq", "exp"), None),
            P(),
            P(("seq", "exp"), None),
            P(("seq", "exp"), None),
            P("exp", None, "seq"),
            P("exp", None, "seq"),
            P("exp", "seq", None),
        ),
        out_specs=P(("seq", "exp"), None),
        check_vma=False,
    )
```

```python
import functools

import jax
import jax.numpy as jnp
from jax import lax
from jax.sharding import PartitionSpec as P
from jax.experimental import pallas as pl
from jax.experimental.pallas import tpu as pltpu

GROUP = 128


PRECISE = lax.Precision.HIGHEST


def exchange_body(x_ref, o_ref, send_sem, recv_sem, local_sem):
    devices = x_ref.shape[0]
    me = lax.axis_index("exp")
    row = lax.axis_index("seq")
    mesh_id = pl.DeviceIdType.MESH
    barrier = pltpu.get_barrier_semaphore()
    for step in range(1, devices):
        peer = lax.rem(me + step, devices)
        pl.semaphore_signal(barrier, 1, device_id=(row, peer), device_id_type=mesh_id)
    local = pltpu.make_async_copy(x_ref.at[me], o_ref.at[me], local_sem)
    local.start()
    pl.semaphore_wait(barrier, devices - 1)
    copies = []
    order = sorted(range(1, devices), key=lambda step: -min(step, devices - step))
    half = x_ref.shape[2] // 2
    for step in order:
        peer = lax.rem(me + step, devices)
        for part in range(2):
            columns = pl.ds(part * half, half)
            copy = pltpu.make_async_remote_copy(
                src_ref=x_ref.at[peer, :, columns],
                dst_ref=o_ref.at[me, :, columns],
                send_sem=send_sem.at[part, step],
                recv_sem=recv_sem.at[part, step],
                device_id=(row, peer),
                device_id_type=mesh_id,
            )
            copy.start()
            copies.append(copy)
    local.wait()
    for copy in copies:
        copy.wait()


def exchange(x, collective):
    devices = x.shape[0]
    return pl.pallas_call(
        exchange_body,
        out_shape=jax.ShapeDtypeStruct(x.shape, x.dtype),
        in_specs=[pl.BlockSpec(memory_space=pltpu.VMEM)],
        out_specs=pl.BlockSpec(memory_space=pltpu.VMEM),
        scratch_shapes=[
            pltpu.SemaphoreType.DMA((2, devices)),
            pltpu.SemaphoreType.DMA((2, devices)),
            pltpu.SemaphoreType.DMA,
        ],
        compiler_params=pltpu.CompilerParams(collective_id=collective, has_side_effects=True),
    )(x)


def expert_body(depth_steps, seg_ref, gate_ref, up_ref, down_ref, o_ref, gate_acc, up_acc, active):
    step = pl.program_id(0)

    @pl.when(step == 0)
    def _():
        gate_acc[...] = jnp.zeros_like(gate_acc)
        up_acc[...] = jnp.zeros_like(up_acc)

    @pl.when(step < depth_steps)
    def _():
        joined = jnp.concatenate([gate_ref[...], up_ref[...]], axis=1)
        both = jnp.dot(seg_ref[...], joined, preferred_element_type=jnp.float32)
        hidden = gate_acc.shape[1]
        gate_acc[...] += both[:, :hidden]
        up_acc[...] += both[:, hidden:]

    @pl.when(step == depth_steps - 1)
    def _():
        gate = gate_acc[...]
        active[...] = (gate / (1.0 + jnp.exp(-gate)) * up_acc[...]).astype(active.dtype)

    @pl.when(step >= depth_steps)
    def _():
        o_ref[...] = jnp.dot(
            active[...], down_ref[...], preferred_element_type=jnp.float32
        ).astype(o_ref.dtype)


def expert_mlp(segment, gate_w, up_w, down_w):
    rows, width = segment.shape
    hidden = gate_w.shape[1]
    block = 4096
    columns = 2048
    depth_steps = width // block
    column_steps = width // columns
    return pl.pallas_call(
        functools.partial(expert_body, depth_steps),
        grid=(depth_steps + column_steps,),
        in_specs=[
            pl.BlockSpec((rows, block), lambda i: (0, jnp.minimum(i, depth_steps - 1))),
            pl.BlockSpec((block, hidden), lambda i: (jnp.minimum(i, depth_steps - 1), 0)),
            pl.BlockSpec((block, hidden), lambda i: (jnp.minimum(i, depth_steps - 1), 0)),
            pl.BlockSpec((hidden, columns), lambda i: (0, jnp.maximum(i - depth_steps, 0))),
        ],
        out_specs=pl.BlockSpec((rows, columns), lambda i: (0, jnp.maximum(i - depth_steps, 0))),
        out_shape=jax.ShapeDtypeStruct((rows, width), jnp.bfloat16),
        scratch_shapes=[
            pltpu.VMEM((rows, hidden), jnp.float32),
            pltpu.VMEM((rows, hidden), jnp.float32),
            pltpu.VMEM((rows, hidden), jnp.bfloat16),
        ],
        cost_estimate=pl.CostEstimate(
            flops=6 * rows * width * hidden,
            transcendentals=rows * hidden,
            bytes_accessed=2 * (2 * rows * width + 3 * width * hidden),
        ),
    )(segment, gate_w, up_w, down_w)


def scan_rounds(devices):
    rounds, base = [], 1
    while base < devices:
        rounds.append([j * base for j in range(1, 4) if j * base < devices])
        base *= 4
    return rounds


def fold(earlier_state, earlier_log, later_state, later_log):
    decay = jnp.exp(later_log[:, 0:1, :])
    return decay * earlier_state + later_state, earlier_log + later_log


def scan_body(devices, x_state, x_log, o_state, o_log, inc_state, inc_log, wire, recv, send_sem, recv_sem):
    me = lax.axis_index("seq")
    col = lax.axis_index("exp")
    rows = x_state.shape[1]
    mesh_id = pl.DeviceIdType.MESH
    barrier = pltpu.get_barrier_semaphore()
    for step in range(1, devices):
        peer = lax.rem(me + step, devices)
        pl.semaphore_signal(barrier, 1, device_id=(peer, col), device_id_type=mesh_id)
    pl.semaphore_wait(barrier, devices - 1)
    o_state[...] = jnp.zeros_like(o_state)
    o_log[...] = jnp.zeros_like(o_log)
    levels = scan_rounds(devices)
    for level, shifts in enumerate(levels):
        last = level == len(levels) - 1
        state_now = x_state if level == 0 else inc_state.at[level]
        log_now = x_log[...] if level == 0 else inc_log[level]
        high = log_now.astype(jnp.bfloat16).astype(jnp.float32)
        wire[level, :, :rows, :] = state_now[...].astype(jnp.bfloat16)
        wire[level, :, rows:, :] = jnp.concatenate([high, log_now - high], axis=1).astype(jnp.bfloat16)

        def link(slot, peer):
            return pltpu.make_async_remote_copy(
                src_ref=wire.at[level],
                dst_ref=recv.at[level, slot],
                send_sem=send_sem.at[level, slot],
                recv_sem=recv_sem.at[level, slot],
                device_id=(peer, col),
                device_id_type=mesh_id,
            )
        for slot, shift in enumerate(shifts):
            @pl.when(me + shift < devices)
            def _():
                link(slot, me + shift).start()
        if not last:
            inc_state[level + 1] = state_now[...]
            inc_log[level + 1] = log_now
        for slot, shift in enumerate(shifts):
            @pl.when(me >= shift)
            def _():
                link(slot, me - shift).wait_recv()
                got_state = recv[level, slot, :, :rows, :].astype(jnp.float32)
                parts = recv[level, slot, :, rows:, :].astype(jnp.float32)
                got_log = parts[:, :8, :] + parts[:, 8:, :]
                if not last:
                    new_state, new_log = fold(got_state, got_log, inc_state[level + 1], inc_log[level + 1])
                    inc_state[level + 1] = new_state
                    inc_log[level + 1] = new_log
                new_state, new_log = fold(got_state, got_log, o_state[...], o_log[...])
                o_state[...] = new_state
                o_log[...] = new_log
        for slot, shift in enumerate(shifts):
            @pl.when(me + shift < devices)
            def _():
                link(slot, me + shift).wait_send()


def exclusive_scan(log, state, axis):
    devices = lax.axis_size(axis)
    heads, state_rows, lanes = state.shape
    log_rows = jnp.broadcast_to(log[:, None, None], (heads, 8, lanes))
    levels = len(scan_rounds(devices))
    wire_shape = (heads, state_rows + 16, lanes)
    prior_state, prior_log = pl.pallas_call(
        functools.partial(scan_body, devices),
        out_shape=(
            jax.ShapeDtypeStruct(state.shape, jnp.float32),
            jax.ShapeDtypeStruct(log_rows.shape, jnp.float32),
        ),
        in_specs=[pl.BlockSpec(memory_space=pltpu.VMEM)] * 2,
        out_specs=(pl.BlockSpec(memory_space=pltpu.VMEM),) * 2,
        scratch_shapes=[
            pltpu.VMEM((levels + 1,) + state.shape, jnp.float32),
            pltpu.VMEM((levels + 1,) + log_rows.shape, jnp.float32),
            pltpu.VMEM((levels,) + wire_shape, jnp.bfloat16),
            pltpu.VMEM((levels, 3) + wire_shape, jnp.bfloat16),
            pltpu.SemaphoreType.DMA((levels, 3)),
            pltpu.SemaphoreType.DMA((levels, 3)),
        ],
        compiler_params=pltpu.CompilerParams(collective_id=3, has_side_effects=True),
    )(state, log_rows)
    return prior_log[:, 0, 0], prior_state


def chain_combine(earlier, later):
    return (earlier[0] + later[0], jnp.exp(later[0])[:, None, None] * earlier[1] + later[1])


def on_device(
    x_in,
    z_gate,
    b_in,
    c_out,
    dt_step,
    rate,
    skip,
    init_state,
    residual,
    norm_gain,
    expert_ids,
    gate_weights,
    w_gate,
    w_up,
    w_down,
):
    token_count, channels = x_in.shape
    heads_here = rate.shape[0]
    head_width = channels // heads_here
    state_width = b_in.shape[1]
    blocks = token_count // GROUP
    inputs = x_in.astype(jnp.float32).reshape(blocks, GROUP, heads_here, head_width)
    keys_in = b_in.astype(jnp.float32).reshape(blocks, GROUP, state_width)
    queries = c_out.astype(jnp.float32).reshape(blocks, GROUP, state_width)
    log_steps = (-rate[None, :] * dt_step).reshape(blocks, GROUP, heads_here)
    cumulative = jnp.cumsum(log_steps, axis=1)
    scores = jnp.einsum("ctn,csn->cts", queries, keys_in, precision=PRECISE)
    causal = jnp.arange(GROUP)[:, None] >= jnp.arange(GROUP)[None, :]
    spread = cumulative[:, :, None, :] - cumulative[:, None, :, :]
    weights = jnp.exp(jnp.where(causal[None, :, :, None], spread, -jnp.inf)) * scores[..., None]
    intra_out = jnp.einsum("ctsh,cshp->cthp", weights, inputs, precision=PRECISE)
    tail_decay = jnp.exp(cumulative[:, -1:, :] - cumulative)
    block_state = jnp.einsum("csh,cshp,csn->chpn", tail_decay, inputs, keys_in, precision=PRECISE)
    block_log = cumulative[:, -1, :]

    def advance(carried, element):
        total_log, total_state = carried
        step_log, step_state = element
        updated = (
            total_log + step_log,
            jnp.exp(step_log)[:, None, None] * total_state + step_state,
        )
        return (updated, (total_log, total_state))

    zero_state = jnp.zeros((heads_here, head_width, state_width), jnp.float32)
    zero_log = jnp.zeros((heads_here,), jnp.float32)
    (device_log, device_state), (enter_log, enter_state) = lax.scan(
        advance, (zero_log, zero_state), (block_log, block_state)
    )
    prior_log, prior_state = exclusive_scan(device_log, device_state, "seq")
    incoming = prior_state + jnp.exp(prior_log)[:, None, None] * init_state
    entering = enter_state + jnp.exp(enter_log)[:, :, None, None] * incoming[None]
    inter_out = jnp.exp(cumulative)[..., None] * jnp.einsum(
        "chpn,ctn->cthp", entering, queries, precision=PRECISE
    )
    mixed_out = (intra_out + inter_out + skip[None, None, :, None] * inputs).reshape(
        token_count, channels
    )
    mixer = (mixed_out * jax.nn.silu(z_gate.astype(jnp.float32))).astype(jnp.bfloat16)
    owners = lax.axis_size("exp")
    rows_here = residual.shape[0]
    arrived_mix = exchange(mixer.reshape(owners, rows_here, channels), 0)
    token_mix = arrived_mix.transpose(1, 0, 2).reshape(rows_here, owners * channels)
    stream = (residual.astype(jnp.float32) + token_mix.astype(jnp.float32)).astype(jnp.bfloat16)
    widened = stream.astype(jnp.float32)
    normed = (
        widened
        * lax.rsqrt(jnp.mean(widened * widened, axis=-1, keepdims=True) + 1e-06)
        * norm_gain[None, :]
    ).astype(jnp.bfloat16)
    local_experts = w_gate.shape[0]
    experts = owners * local_experts
    capacity = max(2, 2 * rows_here // experts + 1)
    width = residual.shape[1]
    chosen = expert_ids.reshape(-1)
    onehot = (chosen[:, None] == jnp.arange(experts)[None, :]).astype(jnp.int32)
    slot_index = jnp.sum((jnp.cumsum(onehot, axis=0) - onehot) * onehot, axis=1)
    target = chosen * capacity + slot_index
    placing = (target[None, :] == jnp.arange(experts * capacity)[:, None]).astype(jnp.bfloat16)
    pair_rows = jnp.repeat(normed, 2, axis=0)
    outgoing = jnp.dot(placing, pair_rows, preferred_element_type=jnp.float32).astype(jnp.bfloat16)
    block = capacity * width // 16
    arrived = exchange(outgoing.reshape(experts, 16, block), 1)
    arrived = arrived.reshape(capacity * experts, width)
    segment = lax.all_gather(arrived, "seq", axis=0, tiled=True)
    partial_value = expert_mlp(segment, w_gate[0], w_up[0], w_down[0])
    summed = lax.psum_scatter(partial_value, "seq", scatter_dimension=0, tiled=True)
    returned = exchange(summed.reshape(experts, 16, block), 2)
    results = returned.reshape(experts * capacity, width)
    picked = results[target].astype(jnp.float32).reshape(rows_here, 2, width)
    mixture = jnp.sum(picked * gate_weights[:, :, None], axis=1)
    return (widened + mixture).astype(jnp.bfloat16)


def solution(mesh):
    return jax.shard_map(
        on_device,
        mesh=mesh,
        in_specs=(
            P("seq", "exp"),
            P("seq", "exp"),
            P("seq", None),
            P("seq", None),
            P("seq", "exp"),
            P("exp"),
            P("exp"),
            P("exp", None, None),
            P(("seq", "exp"), None),
            P(),
            P(("seq", "exp"), None),
            P(("seq", "exp"), None),
            P("exp", None, "seq"),
            P("exp", None, "seq"),
            P("exp", "seq", None),
        ),
        out_specs=P(("seq", "exp"), None),
        check_vma=False,
    )
```

```python
import functools

import jax
import jax.numpy as jnp
from jax import lax
from jax.sharding import PartitionSpec as P
from jax.experimental import pallas as pl
from jax.experimental.pallas import tpu as pltpu

GROUP = 128


PRECISE = lax.Precision.HIGHEST


def exchange_body(x_ref, o_ref, send_sem, recv_sem, local_sem):
    devices = x_ref.shape[0]
    me = lax.axis_index("exp")
    row = lax.axis_index("seq")
    mesh_id = pl.DeviceIdType.MESH
    barrier = pltpu.get_barrier_semaphore()
    for step in range(1, devices):
        peer = lax.rem(me + step, devices)
        pl.semaphore_signal(barrier, 1, device_id=(row, peer), device_id_type=mesh_id)
    local = pltpu.make_async_copy(x_ref.at[me], o_ref.at[me], local_sem)
    local.start()
    pl.semaphore_wait(barrier, devices - 1)
    copies = []
    order = sorted(range(1, devices), key=lambda step: -min(step, devices - step))
    for step in order:
        peer = lax.rem(me + step, devices)
        copy = pltpu.make_async_remote_copy(
            src_ref=x_ref.at[peer],
            dst_ref=o_ref.at[me],
            send_sem=send_sem.at[step],
            recv_sem=recv_sem.at[step],
            device_id=(row, peer),
            device_id_type=mesh_id,
        )
        copy.start()
        copies.append(copy)
    local.wait()
    for copy in copies:
        copy.wait()


def exchange(x, collective):
    devices = x.shape[0]
    return pl.pallas_call(
        exchange_body,
        out_shape=jax.ShapeDtypeStruct(x.shape, x.dtype),
        in_specs=[pl.BlockSpec(memory_space=pltpu.VMEM)],
        out_specs=pl.BlockSpec(memory_space=pltpu.VMEM),
        scratch_shapes=[
            pltpu.SemaphoreType.DMA((devices,)),
            pltpu.SemaphoreType.DMA((devices,)),
            pltpu.SemaphoreType.DMA,
        ],
        compiler_params=pltpu.CompilerParams(collective_id=collective, has_side_effects=True),
    )(x)


def expert_body(depth_steps, seg_ref, gate_ref, up_ref, down_ref, o_ref, gate_acc, up_acc, active):
    step = pl.program_id(0)

    @pl.when(step == 0)
    def _():
        gate_acc[...] = jnp.zeros_like(gate_acc)
        up_acc[...] = jnp.zeros_like(up_acc)

    @pl.when(step < depth_steps)
    def _():
        joined = jnp.concatenate([gate_ref[...], up_ref[...]], axis=1)
        both = jnp.dot(seg_ref[...], joined, preferred_element_type=jnp.float32)
        hidden = gate_acc.shape[1]
        gate_acc[...] += both[:, :hidden]
        up_acc[...] += both[:, hidden:]

    @pl.when(step == depth_steps - 1)
    def _():
        gate = gate_acc[...]
        active[...] = (gate / (1.0 + jnp.exp(-gate)) * up_acc[...]).astype(active.dtype)

    @pl.when(step >= depth_steps)
    def _():
        o_ref[...] = jnp.dot(
            active[...], down_ref[...], preferred_element_type=jnp.float32
        ).astype(o_ref.dtype)


def expert_mlp(segment, gate_w, up_w, down_w):
    rows, width = segment.shape
    hidden = gate_w.shape[1]
    block = 4096
    columns = 4096
    depth_steps = width // block
    column_steps = width // columns
    return pl.pallas_call(
        functools.partial(expert_body, depth_steps),
        grid=(depth_steps + column_steps,),
        in_specs=[
            pl.BlockSpec((rows, block), lambda i: (0, jnp.minimum(i, depth_steps - 1))),
            pl.BlockSpec((block, hidden), lambda i: (jnp.minimum(i, depth_steps - 1), 0)),
            pl.BlockSpec((block, hidden), lambda i: (jnp.minimum(i, depth_steps - 1), 0)),
            pl.BlockSpec((hidden, columns), lambda i: (0, jnp.maximum(i - depth_steps, 0))),
        ],
        out_specs=pl.BlockSpec((rows, columns), lambda i: (0, jnp.maximum(i - depth_steps, 0))),
        out_shape=jax.ShapeDtypeStruct((rows, width), jnp.bfloat16),
        scratch_shapes=[
            pltpu.VMEM((rows, hidden), jnp.float32),
            pltpu.VMEM((rows, hidden), jnp.float32),
            pltpu.VMEM((rows, hidden), jnp.bfloat16),
        ],
        cost_estimate=pl.CostEstimate(
            flops=6 * rows * width * hidden,
            transcendentals=rows * hidden,
            bytes_accessed=2 * (2 * rows * width + 3 * width * hidden),
        ),
    )(segment, gate_w, up_w, down_w)


def scan_rounds(devices):
    rounds, base = [], 1
    while base < devices:
        rounds.append([j * base for j in range(1, 4) if j * base < devices])
        base *= 4
    return rounds


def fold(earlier_state, earlier_log, later_state, later_log):
    decay = jnp.exp(later_log[:, 0:1, :])
    return decay * earlier_state + later_state, earlier_log + later_log


def scan_body(devices, x_state, x_log, o_state, o_log, inc_state, inc_log, wire, recv, send_sem, recv_sem):
    me = lax.axis_index("seq")
    col = lax.axis_index("exp")
    rows = x_state.shape[1]
    mesh_id = pl.DeviceIdType.MESH
    barrier = pltpu.get_barrier_semaphore()
    for step in range(1, devices):
        peer = lax.rem(me + step, devices)
        pl.semaphore_signal(barrier, 1, device_id=(peer, col), device_id_type=mesh_id)
    pl.semaphore_wait(barrier, devices - 1)
    o_state[...] = jnp.zeros_like(o_state)
    o_log[...] = jnp.zeros_like(o_log)
    levels = scan_rounds(devices)
    for level, shifts in enumerate(levels):
        last = level == len(levels) - 1
        state_now = x_state if level == 0 else inc_state.at[level]
        log_now = x_log[...] if level == 0 else inc_log[level]
        high = log_now.astype(jnp.bfloat16).astype(jnp.float32)
        wire[level, :, :rows, :] = state_now[...].astype(jnp.bfloat16)
        wire[level, :, rows:, :] = jnp.concatenate([high, log_now - high], axis=1).astype(jnp.bfloat16)

        def link(slot, peer):
            return pltpu.make_async_remote_copy(
                src_ref=wire.at[level],
                dst_ref=recv.at[level, slot],
                send_sem=send_sem.at[level, slot],
                recv_sem=recv_sem.at[level, slot],
                device_id=(peer, col),
                device_id_type=mesh_id,
            )
        for slot, shift in enumerate(shifts):
            @pl.when(me + shift < devices)
            def _():
                link(slot, me + shift).start()
        if not last:
            inc_state[level + 1] = state_now[...]
            inc_log[level + 1] = log_now
        for slot, shift in enumerate(shifts):
            @pl.when(me >= shift)
            def _():
                link(slot, me - shift).wait_recv()
                got_state = recv[level, slot, :, :rows, :].astype(jnp.float32)
                parts = recv[level, slot, :, rows:, :].astype(jnp.float32)
                got_log = parts[:, :8, :] + parts[:, 8:, :]
                if not last:
                    new_state, new_log = fold(got_state, got_log, inc_state[level + 1], inc_log[level + 1])
                    inc_state[level + 1] = new_state
                    inc_log[level + 1] = new_log
                new_state, new_log = fold(got_state, got_log, o_state[...], o_log[...])
                o_state[...] = new_state
                o_log[...] = new_log
        for slot, shift in enumerate(shifts):
            @pl.when(me + shift < devices)
            def _():
                link(slot, me + shift).wait_send()


def exclusive_scan(log, state, axis):
    devices = lax.axis_size(axis)
    heads, state_rows, lanes = state.shape
    log_rows = jnp.broadcast_to(log[:, None, None], (heads, 8, lanes))
    levels = len(scan_rounds(devices))
    wire_shape = (heads, state_rows + 16, lanes)
    prior_state, prior_log = pl.pallas_call(
        functools.partial(scan_body, devices),
        out_shape=(
            jax.ShapeDtypeStruct(state.shape, jnp.float32),
            jax.ShapeDtypeStruct(log_rows.shape, jnp.float32),
        ),
        in_specs=[pl.BlockSpec(memory_space=pltpu.VMEM)] * 2,
        out_specs=(pl.BlockSpec(memory_space=pltpu.VMEM),) * 2,
        scratch_shapes=[
            pltpu.VMEM((levels + 1,) + state.shape, jnp.float32),
            pltpu.VMEM((levels + 1,) + log_rows.shape, jnp.float32),
            pltpu.VMEM((levels,) + wire_shape, jnp.bfloat16),
            pltpu.VMEM((levels, 3) + wire_shape, jnp.bfloat16),
            pltpu.SemaphoreType.DMA((levels, 3)),
            pltpu.SemaphoreType.DMA((levels, 3)),
        ],
        compiler_params=pltpu.CompilerParams(collective_id=3, has_side_effects=True),
    )(state, log_rows)
    return prior_log[:, 0, 0], prior_state


def chain_combine(earlier, later):
    return (earlier[0] + later[0], jnp.exp(later[0])[:, None, None] * earlier[1] + later[1])


def on_device(
    x_in,
    z_gate,
    b_in,
    c_out,
    dt_step,
    rate,
    skip,
    init_state,
    residual,
    norm_gain,
    expert_ids,
    gate_weights,
    w_gate,
    w_up,
    w_down,
):
    token_count, channels = x_in.shape
    heads_here = rate.shape[0]
    head_width = channels // heads_here
    state_width = b_in.shape[1]
    blocks = token_count // GROUP
    inputs = x_in.astype(jnp.float32).reshape(blocks, GROUP, heads_here, head_width)
    keys_in = b_in.astype(jnp.float32).reshape(blocks, GROUP, state_width)
    queries = c_out.astype(jnp.float32).reshape(blocks, GROUP, state_width)
    log_steps = (-rate[None, :] * dt_step).reshape(blocks, GROUP, heads_here)
    cumulative = jnp.cumsum(log_steps, axis=1)
    scores = jnp.einsum("ctn,csn->cts", queries, keys_in, precision=PRECISE)
    causal = jnp.arange(GROUP)[:, None] >= jnp.arange(GROUP)[None, :]
    spread = cumulative[:, :, None, :] - cumulative[:, None, :, :]
    weights = jnp.exp(jnp.where(causal[None, :, :, None], spread, -jnp.inf)) * scores[..., None]
    intra_out = jnp.einsum("ctsh,cshp->cthp", weights, inputs, precision=PRECISE)
    tail_decay = jnp.exp(cumulative[:, -1:, :] - cumulative)
    block_state = jnp.einsum("csh,cshp,csn->chpn", tail_decay, inputs, keys_in, precision=PRECISE)
    block_log = cumulative[:, -1, :]

    def advance(carried, element):
        total_log, total_state = carried
        step_log, step_state = element
        updated = (
            total_log + step_log,
            jnp.exp(step_log)[:, None, None] * total_state + step_state,
        )
        return (updated, (total_log, total_state))

    zero_state = jnp.zeros((heads_here, head_width, state_width), jnp.float32)
    zero_log = jnp.zeros((heads_here,), jnp.float32)
    (device_log, device_state), (enter_log, enter_state) = lax.scan(
        advance, (zero_log, zero_state), (block_log, block_state)
    )
    prior_log, prior_state = exclusive_scan(device_log, device_state, "seq")
    incoming = prior_state + jnp.exp(prior_log)[:, None, None] * init_state
    entering = enter_state + jnp.exp(enter_log)[:, :, None, None] * incoming[None]
    inter_out = jnp.exp(cumulative)[..., None] * jnp.einsum(
        "chpn,ctn->cthp", entering, queries, precision=PRECISE
    )
    mixed_out = (intra_out + inter_out + skip[None, None, :, None] * inputs).reshape(
        token_count, channels
    )
    mixer = (mixed_out * jax.nn.silu(z_gate.astype(jnp.float32))).astype(jnp.bfloat16)
    owners = lax.axis_size("exp")
    rows_here = residual.shape[0]
    arrived_mix = exchange(mixer.reshape(owners, rows_here, channels), 0)
    token_mix = arrived_mix.transpose(1, 0, 2).reshape(rows_here, owners * channels)
    stream = (residual.astype(jnp.float32) + token_mix.astype(jnp.float32)).astype(jnp.bfloat16)
    widened = stream.astype(jnp.float32)
    normed = (
        widened
        * lax.rsqrt(jnp.mean(widened * widened, axis=-1, keepdims=True) + 1e-06)
        * norm_gain[None, :]
    ).astype(jnp.bfloat16)
    local_experts = w_gate.shape[0]
    experts = owners * local_experts
    capacity = max(2, 2 * rows_here // experts + 1)
    width = residual.shape[1]
    chosen = expert_ids.reshape(-1)
    onehot = (chosen[:, None] == jnp.arange(experts)[None, :]).astype(jnp.int32)
    slot_index = jnp.sum((jnp.cumsum(onehot, axis=0) - onehot) * onehot, axis=1)
    target = chosen * capacity + slot_index
    placing = (target[None, :] == jnp.arange(experts * capacity)[:, None]).astype(jnp.bfloat16)
    pair_rows = jnp.repeat(normed, 2, axis=0)
    outgoing = jnp.dot(placing, pair_rows, preferred_element_type=jnp.float32).astype(jnp.bfloat16)
    block = capacity * width // 16
    arrived = exchange(outgoing.reshape(experts, 16, block), 1)
    arrived = arrived.reshape(capacity * experts, width)
    segment = lax.all_gather(arrived, "seq", axis=0, tiled=True)
    partial_value = expert_mlp(segment, w_gate[0], w_up[0], w_down[0])
    summed = lax.psum_scatter(partial_value, "seq", scatter_dimension=0, tiled=True)
    returned = exchange(summed.reshape(experts, 16, block), 2)
    results = returned.reshape(experts * capacity, width)
    picked = results[target].astype(jnp.float32).reshape(rows_here, 2, width)
    mixture = jnp.sum(picked * gate_weights[:, :, None], axis=1)
    return (widened + mixture).astype(jnp.bfloat16)


def solution(mesh):
    return jax.shard_map(
        on_device,
        mesh=mesh,
        in_specs=(
            P("seq", "exp"),
            P("seq", "exp"),
            P("seq", None),
            P("seq", None),
            P("seq", "exp"),
            P("exp"),
            P("exp"),
            P("exp", None, None),
            P(("seq", "exp"), None),
            P(),
            P(("seq", "exp"), None),
            P(("seq", "exp"), None),
            P("exp", None, "seq"),
            P("exp", None, "seq"),
            P("exp", "seq", None),
        ),
        out_specs=P(("seq", "exp"), None),
        check_vma=False,
    )
```

```python
import functools

import jax
import jax.numpy as jnp
from jax import lax
from jax.sharding import PartitionSpec as P
from jax.experimental import pallas as pl
from jax.experimental.pallas import tpu as pltpu

GROUP = 128


PRECISE = lax.Precision.HIGHEST


def exchange_body(x_ref, o_ref, send_sem, recv_sem, local_sem):
    devices = x_ref.shape[0]
    me = lax.axis_index("exp")
    row = lax.axis_index("seq")
    mesh_id = pl.DeviceIdType.MESH
    barrier = pltpu.get_barrier_semaphore()
    for step in range(1, devices):
        peer = lax.rem(me + step, devices)
        pl.semaphore_signal(barrier, 1, device_id=(row, peer), device_id_type=mesh_id)
    local = pltpu.make_async_copy(x_ref.at[me], o_ref.at[me], local_sem)
    local.start()
    pl.semaphore_wait(barrier, devices - 1)
    copies = []
    order = sorted(range(1, devices), key=lambda step: -min(step, devices - step))
    for step in order:
        peer = lax.rem(me + step, devices)
        copy = pltpu.make_async_remote_copy(
            src_ref=x_ref.at[peer],
            dst_ref=o_ref.at[me],
            send_sem=send_sem.at[step],
            recv_sem=recv_sem.at[step],
            device_id=(row, peer),
            device_id_type=mesh_id,
        )
        copy.start()
        copies.append(copy)
    local.wait()
    for copy in copies:
        copy.wait()


def exchange(x, collective):
    devices = x.shape[0]
    return pl.pallas_call(
        exchange_body,
        out_shape=jax.ShapeDtypeStruct(x.shape, x.dtype),
        in_specs=[pl.BlockSpec(memory_space=pltpu.VMEM)],
        out_specs=pl.BlockSpec(memory_space=pltpu.VMEM),
        scratch_shapes=[
            pltpu.SemaphoreType.DMA((devices,)),
            pltpu.SemaphoreType.DMA((devices,)),
            pltpu.SemaphoreType.DMA,
        ],
        compiler_params=pltpu.CompilerParams(collective_id=collective, has_side_effects=True),
    )(x)


def expert_body(depth_steps, seg_ref, gate_ref, up_ref, down_ref, o_ref, gate_acc, up_acc, active):
    step = pl.program_id(0)

    @pl.when(step == 0)
    def _():
        gate_acc[...] = jnp.zeros_like(gate_acc)
        up_acc[...] = jnp.zeros_like(up_acc)

    @pl.when(step < depth_steps)
    def _():
        joined = jnp.concatenate([gate_ref[...], up_ref[...]], axis=1)
        both = jnp.dot(seg_ref[...], joined, preferred_element_type=jnp.float32)
        hidden = gate_acc.shape[1]
        gate_acc[...] += both[:, :hidden]
        up_acc[...] += both[:, hidden:]

    @pl.when(step == depth_steps - 1)
    def _():
        gate = gate_acc[...]
        active[...] = (gate / (1.0 + jnp.exp(-gate)) * up_acc[...]).astype(active.dtype)

    @pl.when(step >= depth_steps)
    def _():
        o_ref[...] = jnp.dot(
            active[...], down_ref[...], preferred_element_type=jnp.float32
        ).astype(o_ref.dtype)


def expert_mlp(segment, gate_w, up_w, down_w):
    rows, width = segment.shape
    hidden = gate_w.shape[1]
    block = 4096
    columns = 4096
    depth_steps = width // block
    column_steps = width // columns
    return pl.pallas_call(
        functools.partial(expert_body, depth_steps),
        grid=(depth_steps + column_steps,),
        in_specs=[
            pl.BlockSpec((rows, block), lambda i: (0, jnp.minimum(i, depth_steps - 1))),
            pl.BlockSpec((block, hidden), lambda i: (jnp.minimum(i, depth_steps - 1), 0)),
            pl.BlockSpec((block, hidden), lambda i: (jnp.minimum(i, depth_steps - 1), 0)),
            pl.BlockSpec((hidden, columns), lambda i: (0, jnp.maximum(i - depth_steps, 0))),
        ],
        out_specs=pl.BlockSpec((rows, columns), lambda i: (0, jnp.maximum(i - depth_steps, 0))),
        out_shape=jax.ShapeDtypeStruct((rows, width), jnp.bfloat16),
        scratch_shapes=[
            pltpu.VMEM((rows, hidden), jnp.float32),
            pltpu.VMEM((rows, hidden), jnp.float32),
            pltpu.VMEM((rows, hidden), jnp.bfloat16),
        ],
        cost_estimate=pl.CostEstimate(
            flops=6 * rows * width * hidden,
            transcendentals=rows * hidden,
            bytes_accessed=2 * (2 * rows * width + 3 * width * hidden),
        ),
    )(segment, gate_w, up_w, down_w)


def scan_rounds(devices):
    rounds, base = [], 1
    while base < devices:
        rounds.append([base])
        base *= 2
    return rounds


def fold(earlier_state, earlier_log, later_state, later_log):
    decay = jnp.exp(later_log[:, 0:1, :])
    return decay * earlier_state + later_state, earlier_log + later_log


def scan_body(devices, x_state, x_log, o_state, o_log, inc_state, inc_log, wire, recv, send_sem, recv_sem):
    me = lax.axis_index("seq")
    col = lax.axis_index("exp")
    rows = x_state.shape[1]
    mesh_id = pl.DeviceIdType.MESH
    barrier = pltpu.get_barrier_semaphore()
    for step in range(1, devices):
        peer = lax.rem(me + step, devices)
        pl.semaphore_signal(barrier, 1, device_id=(peer, col), device_id_type=mesh_id)
    pl.semaphore_wait(barrier, devices - 1)
    o_state[...] = jnp.zeros_like(o_state)
    o_log[...] = jnp.zeros_like(o_log)
    levels = scan_rounds(devices)
    for level, shifts in enumerate(levels):
        last = level == len(levels) - 1
        state_now = x_state if level == 0 else inc_state.at[level]
        log_now = x_log[...] if level == 0 else inc_log[level]
        high = log_now.astype(jnp.bfloat16).astype(jnp.float32)
        wire[level, :, :rows, :] = state_now[...].astype(jnp.bfloat16)
        wire[level, :, rows:, :] = jnp.concatenate([high, log_now - high], axis=1).astype(jnp.bfloat16)

        def link(slot, peer):
            return pltpu.make_async_remote_copy(
                src_ref=wire.at[level],
                dst_ref=recv.at[level, slot],
                send_sem=send_sem.at[level, slot],
                recv_sem=recv_sem.at[level, slot],
                device_id=(peer, col),
                device_id_type=mesh_id,
            )
        for slot, shift in enumerate(shifts):
            @pl.when(me + shift < devices)
            def _():
                link(slot, me + shift).start()
        if not last:
            inc_state[level + 1] = state_now[...]
            inc_log[level + 1] = log_now
        for slot, shift in enumerate(shifts):
            @pl.when(me >= shift)
            def _():
                link(slot, me - shift).wait_recv()
                got_state = recv[level, slot, :, :rows, :].astype(jnp.float32)
                parts = recv[level, slot, :, rows:, :].astype(jnp.float32)
                got_log = parts[:, :8, :] + parts[:, 8:, :]
                if not last:
                    new_state, new_log = fold(got_state, got_log, inc_state[level + 1], inc_log[level + 1])
                    inc_state[level + 1] = new_state
                    inc_log[level + 1] = new_log
                new_state, new_log = fold(got_state, got_log, o_state[...], o_log[...])
                o_state[...] = new_state
                o_log[...] = new_log
        for slot, shift in enumerate(shifts):
            @pl.when(me + shift < devices)
            def _():
                link(slot, me + shift).wait_send()


def exclusive_scan(log, state, axis):
    devices = lax.axis_size(axis)
    heads, state_rows, lanes = state.shape
    log_rows = jnp.broadcast_to(log[:, None, None], (heads, 8, lanes))
    levels = len(scan_rounds(devices))
    wire_shape = (heads, state_rows + 16, lanes)
    prior_state, prior_log = pl.pallas_call(
        functools.partial(scan_body, devices),
        out_shape=(
            jax.ShapeDtypeStruct(state.shape, jnp.float32),
            jax.ShapeDtypeStruct(log_rows.shape, jnp.float32),
        ),
        in_specs=[pl.BlockSpec(memory_space=pltpu.VMEM)] * 2,
        out_specs=(pl.BlockSpec(memory_space=pltpu.VMEM),) * 2,
        scratch_shapes=[
            pltpu.VMEM((levels + 1,) + state.shape, jnp.float32),
            pltpu.VMEM((levels + 1,) + log_rows.shape, jnp.float32),
            pltpu.VMEM((levels,) + wire_shape, jnp.bfloat16),
            pltpu.VMEM((levels, 1) + wire_shape, jnp.bfloat16),
            pltpu.SemaphoreType.DMA((levels, 1)),
            pltpu.SemaphoreType.DMA((levels, 1)),
        ],
        compiler_params=pltpu.CompilerParams(collective_id=3, has_side_effects=True),
    )(state, log_rows)
    return prior_log[:, 0, 0], prior_state


def chain_combine(earlier, later):
    return (earlier[0] + later[0], jnp.exp(later[0])[:, None, None] * earlier[1] + later[1])


def on_device(
    x_in,
    z_gate,
    b_in,
    c_out,
    dt_step,
    rate,
    skip,
    init_state,
    residual,
    norm_gain,
    expert_ids,
    gate_weights,
    w_gate,
    w_up,
    w_down,
):
    token_count, channels = x_in.shape
    heads_here = rate.shape[0]
    head_width = channels // heads_here
    state_width = b_in.shape[1]
    blocks = token_count // GROUP
    inputs = x_in.astype(jnp.float32).reshape(blocks, GROUP, heads_here, head_width)
    keys_in = b_in.astype(jnp.float32).reshape(blocks, GROUP, state_width)
    queries = c_out.astype(jnp.float32).reshape(blocks, GROUP, state_width)
    log_steps = (-rate[None, :] * dt_step).reshape(blocks, GROUP, heads_here)
    cumulative = jnp.cumsum(log_steps, axis=1)
    scores = jnp.einsum("ctn,csn->cts", queries, keys_in, precision=PRECISE)
    causal = jnp.arange(GROUP)[:, None] >= jnp.arange(GROUP)[None, :]
    spread = cumulative[:, :, None, :] - cumulative[:, None, :, :]
    weights = jnp.exp(jnp.where(causal[None, :, :, None], spread, -jnp.inf)) * scores[..., None]
    intra_out = jnp.einsum("ctsh,cshp->cthp", weights, inputs, precision=PRECISE)
    tail_decay = jnp.exp(cumulative[:, -1:, :] - cumulative)
    block_state = jnp.einsum("csh,cshp,csn->chpn", tail_decay, inputs, keys_in, precision=PRECISE)
    block_log = cumulative[:, -1, :]

    def advance(carried, element):
        total_log, total_state = carried
        step_log, step_state = element
        updated = (
            total_log + step_log,
            jnp.exp(step_log)[:, None, None] * total_state + step_state,
        )
        return (updated, (total_log, total_state))

    zero_state = jnp.zeros((heads_here, head_width, state_width), jnp.float32)
    zero_log = jnp.zeros((heads_here,), jnp.float32)
    (device_log, device_state), (enter_log, enter_state) = lax.scan(
        advance, (zero_log, zero_state), (block_log, block_state)
    )
    prior_log, prior_state = exclusive_scan(device_log, device_state, "seq")
    incoming = prior_state + jnp.exp(prior_log)[:, None, None] * init_state
    entering = enter_state + jnp.exp(enter_log)[:, :, None, None] * incoming[None]
    inter_out = jnp.exp(cumulative)[..., None] * jnp.einsum(
        "chpn,ctn->cthp", entering, queries, precision=PRECISE
    )
    mixed_out = (intra_out + inter_out + skip[None, None, :, None] * inputs).reshape(
        token_count, channels
    )
    mixer = (mixed_out * jax.nn.silu(z_gate.astype(jnp.float32))).astype(jnp.bfloat16)
    owners = lax.axis_size("exp")
    rows_here = residual.shape[0]
    arrived_mix = exchange(mixer.reshape(owners, rows_here, channels), 0)
    token_mix = arrived_mix.transpose(1, 0, 2).reshape(rows_here, owners * channels)
    stream = (residual.astype(jnp.float32) + token_mix.astype(jnp.float32)).astype(jnp.bfloat16)
    widened = stream.astype(jnp.float32)
    normed = (
        widened
        * lax.rsqrt(jnp.mean(widened * widened, axis=-1, keepdims=True) + 1e-06)
        * norm_gain[None, :]
    ).astype(jnp.bfloat16)
    local_experts = w_gate.shape[0]
    experts = owners * local_experts
    capacity = max(2, 2 * rows_here // experts + 1)
    width = residual.shape[1]
    chosen = expert_ids.reshape(-1)
    onehot = (chosen[:, None] == jnp.arange(experts)[None, :]).astype(jnp.int32)
    slot_index = jnp.sum((jnp.cumsum(onehot, axis=0) - onehot) * onehot, axis=1)
    target = chosen * capacity + slot_index
    placing = (target[None, :] == jnp.arange(experts * capacity)[:, None]).astype(jnp.bfloat16)
    pair_rows = jnp.repeat(normed, 2, axis=0)
    outgoing = jnp.dot(placing, pair_rows, preferred_element_type=jnp.float32).astype(jnp.bfloat16)
    block = capacity * width // 16
    arrived = exchange(outgoing.reshape(experts, 16, block), 1)
    arrived = arrived.reshape(capacity * experts, width)
    segment = lax.all_gather(arrived, "seq", axis=0, tiled=True)
    partial_value = expert_mlp(segment, w_gate[0], w_up[0], w_down[0])
    summed = lax.psum_scatter(partial_value, "seq", scatter_dimension=0, tiled=True)
    returned = exchange(summed.reshape(experts, 16, block), 2)
    results = returned.reshape(experts * capacity, width)
    picked = results[target].astype(jnp.float32).reshape(rows_here, 2, width)
    mixture = jnp.sum(picked * gate_weights[:, :, None], axis=1)
    return (widened + mixture).astype(jnp.bfloat16)


def solution(mesh):
    return jax.shard_map(
        on_device,
        mesh=mesh,
        in_specs=(
            P("seq", "exp"),
            P("seq", "exp"),
            P("seq", None),
            P("seq", None),
            P("seq", "exp"),
            P("exp"),
            P("exp"),
            P("exp", None, None),
            P(("seq", "exp"), None),
            P(),
            P(("seq", "exp"), None),
            P(("seq", "exp"), None),
            P("exp", None, "seq"),
            P("exp", None, "seq"),
            P("exp", "seq", None),
        ),
        out_specs=P(("seq", "exp"), None),
        check_vma=False,
    )
```
